32 devices in a mesh: groups: 2 (over y), dp: 2 (over core), seq: 8 (over z, x).
Axes of the slice: x: 2, y: 2, z: 4, core: 2. Of those that a mesh axis runs over, the one named last changes fastest.
Arguments:
- query_proj: bfloat16 [4, 1024, 2048], P(('groups', 'dp'), 'seq'), parts along dimension 0, may hold values from -6 to 6
- key_proj: bfloat16 [4, 1024, 2048], P(('groups', 'dp'), 'seq'), parts along dimension 0, may hold values from -6 to 6
- value_proj: bfloat16 [4, 1024, 2048], P(('groups', 'dp'), 'seq'), parts along dimension 0, may hold values from -6 to 6
- cotangent: bfloat16 [4, 1024, 2048], P(('groups', 'dp'), 'seq'), parts along dimension 0, may hold values from -6 to 6
- boundary: int32 [4], P(('groups', 'dp')), parts along dimension 0, may hold values from 128 to 511
- short_taps: float32 [3, 3, 2048], replicated, may hold values from -3 to 3
- skip_gain: float32 [2048], replicated, may hold values from -4 to 4
- long_filter: bfloat16 [1024, 2048], P('seq'), may hold values from -1.1 to 1.1
Outputs:
- query_grad: bfloat16 [4, 1024, 2048], P(('groups', 'dp'), 'seq'), parts along dimension 0
- key_grad: bfloat16 [4, 1024, 2048], P(('groups', 'dp'), 'seq'), parts along dimension 0
- value_grad: bfloat16 [4, 1024, 2048], P(('groups', 'dp'), 'seq'), parts along dimension 0
- filter_grad: bfloat16 [2048, 2048], P(('groups', 'seq')), parts along dimension 0
- taps_grad: float32 [6, 3, 2048], P('groups', None, 'seq'), parts along dimension 0
- skip_grad: float32 [4096], P(('groups', 'seq')), parts along dimension 0
The draws below stay inside these ranges and needn't reach their ends.
There are 2 independent parts, one for each index of `groups`. The reference program is written for one: setup_inputs(seed, part) draws one part's arguments, and reference() takes and returns one part's arrays. A program takes and returns all parts, laid end to end along the dimension named above; an argument that names none is the same for every part. Nothing has to cross between parts.
All inputs are finite; a program needn't handle non-finite values.
Results may differ from the reference program's by a relative error of at most 0.001.
Values may be sent and summed in bfloat16 or wider, within the bound.
A program may use at most 128 MiB of HBM per device.

```python
import math
import jax
import jax.numpy as jnp
from jax import lax

CH = 2048
PAIRS = 2
SEQ_LEN = 1024


def draw_long_filter(key, part):
    key_noise = jax.random.fold_in(key, 11)
    key_rate = jax.random.fold_in(key, 12)
    key_kind = jax.random.fold_in(key, 13)
    steps = jnp.arange(SEQ_LEN, dtype=jnp.float32)[:, None]
    spread = jax.random.uniform(key_rate, (1, CH), dtype=jnp.float32)
    noise = jnp.clip(jax.random.normal(key_noise, (SEQ_LEN, CH), dtype=jnp.float32), -4.0, 4.0)
    slow = (jax.random.uniform(key_kind, (1, CH), dtype=jnp.float32) < 0.5).astype(jnp.float32)
    slow_rate = (0.2 + 1.8 * spread) / SEQ_LEN
    fast_rate = 1.0 / (30.0 + 20.0 * spread)
    rate = jnp.minimum(slow * slow_rate + (1.0 - slow) * fast_rate, 1.0 / 30.0)
    return (noise * jnp.sqrt(2.0 * rate) * jnp.exp(-rate * steps)).astype(jnp.bfloat16)


def shard_levels(key, shape, pieces, smallest, high):
    def one(position, blocks):
        heights = jax.random.uniform(jax.random.fold_in(jax.random.fold_in(key, 6), position), (blocks,), jnp.float32, smallest / len(pieces), high / len(pieces))
        return jnp.repeat(jnp.exp(heights), shape[position] // blocks).reshape((-1,) + (1,) * (len(shape) - position - 1))

    gain = one(*pieces[0])
    for cut in pieces[1:]:
        gain = gain * one(*cut)
    return gain


def gaussian(rng, dims, scale, bound, cuts=(), held_as=jnp.bfloat16):
    drawn = scale * jax.random.normal(rng, dims, jnp.float32)
    if cuts:
        drawn = drawn * shard_levels(rng, dims, cuts, -0.22, 0.18)
    return jnp.clip(drawn, -bound, bound).astype(held_as)


def setup_inputs(seed: int = 0, part: int = 0) -> dict:
    arg_keys = jax.random.split(jax.random.key(seed), 9)
    part_splits = jax.random.split(jax.random.fold_in(arg_keys[8], part), 9)
    return {
        "query_proj": gaussian(part_splits[0], (PAIRS, SEQ_LEN, CH), 1.0, 6.0, ((0, 2), (1, 8))),
        "key_proj": gaussian(part_splits[1], (PAIRS, SEQ_LEN, CH), 1.0, 6.0, ((0, 2), (1, 8))),
        "value_proj": gaussian(part_splits[2], (PAIRS, SEQ_LEN, CH), 1.0, 6.0, ((0, 2), (1, 8))),
        "cotangent": gaussian(part_splits[3], (PAIRS, SEQ_LEN, CH), 1.0, 6.0, ((0, 2), (1, 8))),
        "boundary": jax.random.randint(part_splits[4], (PAIRS,), SEQ_LEN // 8, SEQ_LEN // 2).astype(jnp.int32),
        "short_taps": gaussian(arg_keys[5], (3, 3, CH), 0.6, 3.0, (), jnp.float32),
        "skip_gain": gaussian(arg_keys[6], (CH,), 1.0, 4.0, (), jnp.float32),
        "long_filter": draw_long_filter(jax.random.fold_in(arg_keys[8], 71), part),
    }


def shifted(x, lag):
    return jnp.pad(x, ((lag, 0), (0, 0)))[:x.shape[0]]

def advanced(x, lag):
    return jnp.pad(x, ((0, lag), (0, 0)))[lag:]

def short_conv(x, taps):
    return taps[0] * x + taps[1] * shifted(x, 1) + taps[2] * shifted(x, 2)

def short_conv_back(grad, taps):
    return taps[0] * grad + taps[1] * advanced(grad, 1) + taps[2] * advanced(grad, 2)

def spectrum(x):
    return jnp.fft.rfft(x, n=2 * x.shape[0], axis=0)

def restore(spec, length):
    return jnp.fft.irfft(spec, n=2 * length, axis=0)[:length]

def reference(query_proj, key_proj, value_proj, cotangent, boundary, short_taps, skip_gain, long_filter):
    scale = 1.0 / math.sqrt(PAIRS * SEQ_LEN)
    filt_spec = spectrum(long_filter.astype(jnp.float32))
    positions = jnp.arange(SEQ_LEN, dtype=jnp.int32)[:, None]
    filter_sum = jnp.zeros((SEQ_LEN, CH), jnp.float32)
    skip_sum = jnp.zeros((CH,), jnp.float32)
    taps_sum = jnp.zeros((3, 3, CH), jnp.float32)
    outs_q = []
    outs_k = []
    outs_v = []
    for pair in range(PAIRS):
        query = query_proj[pair].astype(jnp.float32)
        keys = key_proj[pair].astype(jnp.float32)
        values = value_proj[pair].astype(jnp.float32)
        conv_q = short_conv(query, short_taps[0])
        conv_k = short_conv(keys, short_taps[1])
        conv_v = short_conv(values, short_taps[2])
        gated = conv_k * conv_v
        gated_spec = spectrum(gated)
        mixed = restore(gated_spec * filt_spec, SEQ_LEN) + skip_gain * gated
        mask = (positions >= boundary[pair]).astype(jnp.float32)
        dout = cotangent[pair].astype(jnp.float32) * mask
        grad_q = dout * mixed
        dmix = dout * conv_q
        dmix_spec = spectrum(dmix)
        dgated = restore(jnp.conj(filt_spec) * dmix_spec, SEQ_LEN) + skip_gain * dmix
        filter_sum = filter_sum + restore(dmix_spec * jnp.conj(gated_spec), SEQ_LEN) * scale
        skip_sum = skip_sum + lax.optimization_barrier(jnp.sum(dmix * gated, axis=0)) * scale
        grad_k = dgated * conv_v
        grad_v = dgated * conv_k
        rows = []
        for branch, (grad, raw) in enumerate(((grad_q, query), (grad_k, keys), (grad_v, values))):
            rows.append(jnp.stack([lax.optimization_barrier(jnp.sum(grad * shifted(raw, lag), axis=0)) for lag in range(3)]))
        taps_sum = taps_sum + jnp.stack(rows) * scale
        outs_q.append(short_conv_back(grad_q, short_taps[0]).astype(jnp.bfloat16))
        outs_k.append(short_conv_back(grad_k, short_taps[1]).astype(jnp.bfloat16))
        outs_v.append(short_conv_back(grad_v, short_taps[2]).astype(jnp.bfloat16))
    return (jnp.stack(outs_q), jnp.stack(outs_k), jnp.stack(outs_v), filter_sum.astype(jnp.bfloat16), taps_sum, skip_sum)
```

```python
import functools
import math

import jax
import jax.numpy as jnp
import numpy as np
from jax import lax
from jax.experimental import pallas as pl
from jax.experimental.pallas import tpu as pltpu
from jax.sharding import PartitionSpec as P

DENSE_LIMIT = 1024
LANES = 128
CODES = 32767.0
MESH = pl.DeviceIdType.MESH


def passed_along(value, axis, by):
    count = lax.axis_size(axis)
    pairs = [(i, i + by) for i in range(count) if 0 <= i + by < count]
    return lax.ppermute(value, axis, pairs)


def matmul_high(form, left, right):
    return jnp.einsum(
        form, left, right, precision=lax.Precision.HIGHEST, preferred_element_type=jnp.float32
    )


def dot_high(left, right):
    return jnp.dot(left, right, precision=lax.Precision.HIGHEST, preferred_element_type=jnp.float32)


def angle_table(left, right, period):
    phase = (left[:, None] * right[None, :] % period).astype(jnp.float32) * (2.0 * math.pi / period)
    return (jnp.cos(phase), jnp.sin(phase))


def build_tables(seq_len):
    cols = min(128, seq_len)
    rows = 2 * seq_len // cols
    half = rows // 2
    keep = half + 1
    col_index = jnp.arange(cols, dtype=jnp.int32)
    keep_index = jnp.arange(keep, dtype=jnp.int32)
    half_index = jnp.arange(half, dtype=jnp.int32)
    col_cos, col_sin = angle_table(col_index, col_index, cols)
    first_cos, first_sin = angle_table(keep_index, half_index, rows)
    first = jnp.stack((first_cos, -first_sin))
    twist_cos, twist_sin = angle_table(keep_index, col_index, 2 * seq_len)
    twist_cos = twist_cos[:, None, :]
    twist_sin = twist_sin[:, None, :]
    fwd_real = jnp.concatenate((col_cos, -col_sin), axis=1)
    fwd_imag = jnp.concatenate((col_sin, col_cos), axis=1)
    inv_real = jnp.concatenate((col_cos, col_sin), axis=1)
    inv_imag = jnp.concatenate((-col_sin, col_cos), axis=1)
    edge = (keep_index == 0) | (keep_index == half)
    weights = jnp.where(edge, 1.0, 2.0).astype(jnp.float32) / (2.0 * seq_len)
    last_cos, last_sin = angle_table(half_index, keep_index, rows)
    last_cos = last_cos * weights[None, :]
    last_sin = last_sin * weights[None, :]
    return (first, twist_cos, twist_sin, fwd_real, fwd_imag, inv_real, inv_imag, last_cos, last_sin)


def forward_half(signal, tables):
    first, twist_cos, twist_sin, fwd_real, fwd_imag = tables[:5]
    width_c, length = signal.shape
    cols = fwd_real.shape[0]
    grid = jnp.transpose(signal.reshape(width_c, length // cols, cols), (1, 0, 2))
    partial_dft = matmul_high("pkn,nca->pkca", first, grid)
    turned_re = partial_dft[0] * twist_cos + partial_dft[1] * twist_sin
    turned_im = partial_dft[1] * twist_cos - partial_dft[0] * twist_sin
    keep = partial_dft.shape[1]
    spec = dot_high(turned_re.reshape(-1, cols), fwd_real) + dot_high(
        turned_im.reshape(-1, cols), fwd_imag
    )
    spec = spec.reshape(keep, width_c, 2, cols)
    return (spec[:, :, 0], spec[:, :, 1])


def inverse_half(spec_re, spec_im, tables):
    twist_cos, twist_sin = (tables[1], tables[2])
    inv_real, inv_imag, last_cos, last_sin = tables[5:]
    keep, width_c, cols = spec_re.shape
    wide = dot_high(spec_re.reshape(-1, cols), inv_real) + dot_high(
        spec_im.reshape(-1, cols), inv_imag
    )
    wide = wide.reshape(keep, width_c, 2, cols)
    wide_re = wide[:, :, 0]
    wide_im = wide[:, :, 1]
    turned_re = wide_re * twist_cos - wide_im * twist_sin
    turned_im = wide_im * twist_cos + wide_re * twist_sin
    grid = matmul_high("nk,kca->nca", last_cos, turned_re) - matmul_high(
        "nk,kca->nca", last_sin, turned_im
    )
    return jnp.transpose(grid, (1, 0, 2)).reshape(width_c, -1)


def convolve_cols(gated_spec, filt_spec, tables):
    gated_re, gated_im = gated_spec
    filt_re, filt_im = filt_spec
    return inverse_half(
        gated_re * filt_re - gated_im * filt_im, gated_re * filt_im + gated_im * filt_re, tables
    )


def correlate_cols(gated_spec, filt_spec, dmix_cols, tables):
    gated_re, gated_im = gated_spec
    filt_re, filt_im = filt_spec
    grad_re, grad_im = forward_half(dmix_cols, tables)
    back = inverse_half(
        filt_re * grad_re + filt_im * grad_im, filt_re * grad_im - filt_im * grad_re, tables
    )
    filt_part = inverse_half(
        grad_re * gated_re + grad_im * gated_im, grad_im * gated_re - grad_re * gated_im, tables
    )
    return (back, filt_part)


def phase_tables(n):
    index = 4 * np.arange(n, dtype=np.int64) + 1
    unit = 2.0 * np.pi / (16 * n)
    fine = (index[:, None] * index[None, :LANES] % (16 * n)) * unit
    coarse = (index[:, None] * (4 * LANES * np.arange(n // LANES))[None, :] % (16 * n)) * unit
    turn = index[:, None] * unit
    pack = lambda x: np.stack((np.cos(x), np.sin(x))).astype(np.float32)
    return pack(fine), pack(np.concatenate((coarse, turn), axis=1))


def split_to(ref, lead, rows, value, cols=slice(None)):
    high = value.astype(jnp.bfloat16)
    ref[(*lead, 0, rows, cols)] = high
    ref[(*lead, 1, rows, cols)] = (value - high.astype(jnp.float32)).astype(jnp.bfloat16)


def dot(left, right):
    return jnp.dot(left, right, preferred_element_type=jnp.float32)


def dot3(high, low, ref, lead):
    top = ref[(*lead, 0)]
    return dot(high, top) + (dot(high, ref[(*lead, 1)]) + dot(low, top))


def coded(value, top):
    return jnp.round(value * (CODES / jnp.maximum(top, 1e-30))).astype(jnp.int32).astype(jnp.int16)


def decoded(code, step):
    return code.astype(jnp.int32).astype(jnp.float32) * step


def operator_kernel(
    n, parts, scale, bound, q_in, k_in, v_in, c_in, h_in, taps_in, skip_in, fine, coarse,
    gq_out, gk_out, gv_out, f_out, taps_out, skip_out,
    loc, tails, heads, tails_in, heads_in, short_out, dout, codes, tops, codes_in, tops_in,
    hb, cosines, sines, gd, spec, hspec, gspec, back, edges, back_in, edges_in,
    filt, fother, fown, stage, sums, sums_in, total, other,
    send_sem, recv_sem, local_sem, dp_send, dp_recv, halo_send, halo_recv,
):
    tok = n // parts
    channels = loc.shape[2]
    width = channels // parts
    half = width // 2
    rows = 64
    block = min(256, n)
    span = block // tok
    me = lax.axis_index("seq")
    core = lax.axis_index("dp")
    group = lax.axis_index("groups")
    partner = {"dp": 1 - core}
    twin = {"groups": 1 - group}
    group_rows = pl.ds(pl.multiple_of(group * (tok // 2), tok // 2), tok // 2)
    f32, bf16 = jnp.float32, jnp.bfloat16
    mine = pl.ds(pl.multiple_of(me * tok, tok), tok)
    my_half = pl.ds(pl.multiple_of(core * half, half), half)
    other_half = pl.ds(pl.multiple_of((1 - core) * half, half), half)

    def cols_of(owner):
        return pl.ds(pl.multiple_of(owner * width, width), width)

    def half_cols_of(owner):
        return pl.ds(pl.multiple_of(owner * width + core * half, half), half)

    def rows_of(owner):
        return pl.ds(pl.multiple_of(owner * tok, tok), tok)

    first = me == 0
    last = me == parts - 1
    own_cols = cols_of(me)
    peers = [lax.rem(me + s, parts) for s in range(parts)]
    sources = [lax.rem(me + parts - s, parts) for s in range(parts)]

    loads = [
        pltpu.make_async_copy(x.at[0], loc.at[i], local_sem.at[i])
        for i, x in enumerate((q_in, k_in, v_in, c_in))
    ]
    for load in loads:
        load.start()

    barrier = pltpu.get_barrier_semaphore()
    for s in range(1, parts):
        pl.semaphore_signal(barrier, inc=1, device_id={"seq": peers[s]}, device_id_type=MESH)
    for device in (partner, twin):
        pl.semaphore_signal(barrier, inc=1, device_id=device, device_id_type=MESH)

    for load in loads:
        load.wait()
    for i in range(4):
        tails[2 * i : 2 * i + 2, :] = loc[i, tok - 16 :, :].astype(f32)[14:]
        heads[2 * i : 2 * i + 2, :] = loc[i, :16, :].astype(f32)[:2]

    pl.semaphore_wait(barrier, parts + 1)

    def remote(source, target, sems, device):
        return pltpu.make_async_remote_copy(
            src_ref=source,
            dst_ref=target,
            send_sem=sems[0],
            recv_sem=sems[1],
            device_id=device,
            device_id_type=MESH,
        )

    def to_peer(a, s, source, target):
        return remote(
            source, target, (send_sem.at[a, s], recv_sem.at[a, s]), {"seq": lax.rem(me + s, parts)}
        )

    def to_partner(i, source, target, device=partner):
        return remote(source, target, (dp_send.at[i], dp_recv.at[i]), device)

    @pl.when(first)
    def _():
        back_in[0, :, :] = jnp.zeros((tok, channels), jnp.int16)

    halos = [
        remote(x, y, (halo_send.at[i], halo_recv.at[i]), {"seq": peer})
        for i, (x, y, peer) in enumerate(
            ((tails, tails_in, peers[1]), (heads, heads_in, peers[parts - 1]))
        )
    ]
    for halo in halos:
        halo.start()

    def exchange(a, source, target):
        own = pltpu.make_async_copy(source(me), target, local_sem.at[4 + a])
        own.start()
        copies = []
        for s in range(1, parts):
            copy = to_peer(a, s, source(peers[s]), target)
            copy.start()
            copies.append(copy)
        return own, copies

    def arrived(moved):
        moved[0].wait()
        for copy in moved[1]:
            copy.wait_recv()

    h_moved = exchange(
        0, lambda o: h_in.at[group_rows, half_cols_of(o)], hb.at[me, group, :, my_half]
    )

    chunk = 128

    def at_cols(i):
        return pl.ds(pl.multiple_of(i * chunk, chunk), chunk)

    def extended(b, cols):
        before = jnp.where(first, 0.0, pltpu.roll(tails_in[:, cols], 6 - 2 * b, 0))
        after = heads_in[:, cols]
        if b:
            after = pltpu.roll(after, 8 - 2 * b, 0)
        return before, loc[b, :, cols].astype(f32), after

    def lagged(b, cols, ahead):
        before, here, after = extended(b, cols)
        ext = jnp.concatenate((before, here, after) if ahead else (before, here), axis=0)
        return ext[8:], pltpu.roll(ext, 1, 0)[8:], pltpu.roll(ext, 2, 0)[8:]

    def short(b, lags, cols):
        tap = [taps_in[b, j : j + 1, cols] for j in range(3)]
        return tap[0] * lags[0] + tap[1] * lags[1] + tap[2] * lags[2]

    def encode(i, value, cols):
        top = jnp.max(jnp.abs(value), axis=0, keepdims=True)
        codes[i, :, cols] = coded(value, top)
        tops[i, 0:1, cols] = top * (1.0 / CODES)

    for halo in halos:
        halo.wait_recv()

    @pl.loop(0, channels // chunk)
    def _(i):
        cols = at_cols(i)
        s1 = short(1, lagged(1, cols, True), cols)
        s2 = short(2, lagged(2, cols, True), cols)
        short_out[1, :, cols] = s1
        short_out[2, :, cols] = s2
        encode(0, s1[:tok] * s2[:tok], cols)

    def send_codes(i):
        return (
            exchange(1 + 2 * i, lambda o: codes.at[i, :, cols_of(o)], codes_in.at[i, mine, :]),
            exchange(2 + 2 * i, lambda o: tops.at[i, 0:1, cols_of(o)], tops_in.at[i, me, 0:1, :]),
        )

    g_moved = send_codes(0)

    arrived(h_moved)
    h_quarter = hb.at[:, group, :, my_half]
    h_twin = to_partner(3 + parts, h_quarter, h_quarter, twin)
    h_twin.start()

    @pl.loop(0, n // rows)
    def _(i):
        at = pl.ds(pl.multiple_of(i * rows, rows), rows)
        fr, fi = fine[0, at, :], fine[1, at, :]
        cr, ci = coarse[0, at, :], coarse[1, at, :]
        for a in range(n // LANES):
            ar, ai = cr[:, a : a + 1], ci[:, a : a + 1]
            cols = slice(a * LANES, (a + 1) * LANES)
            split_to(cosines, (), at, fr * ar - fi * ai, cols)
            split_to(sines, (), at, fr * ai + fi * ar, cols)

    h_twin.wait_recv()
    h_relay = to_partner(0, hb.at[:, :, :, my_half], hb.at[:, :, :, my_half])
    h_relay.start()

    @pl.loop(0, channels // chunk)
    def _(i):
        cols = at_cols(i)
        before, here, after = extended(3, cols)
        ext = jnp.concatenate((here, after), axis=0)
        pos = me * tok + lax.broadcasted_iota(jnp.int32, (tok + 8, chunk), 0)
        masked = jnp.where((pos >= bound[0]) & (pos < n), ext, 0.0)
        dout[:, cols] = masked
        s0 = short(0, lagged(0, cols, True), cols)
        short_out[0, :, cols] = s0
        encode(1, masked[:tok] * s0[:tok], cols)

    m_moved = [
        [
            to_peer(3, s, codes.at[1, :, cols_of(peers[s])], codes_in.at[1, mine, :]),
            to_peer(4, s, tops.at[1, 0:1, cols_of(peers[s])], tops_in.at[1, me, 0:1, :]),
        ]
        for s in range(1, parts)
    ]
    m_own = [
        pltpu.make_async_copy(codes.at[1, :, own_cols], codes_in.at[1, mine, :], local_sem.at[7]),
        pltpu.make_async_copy(tops.at[1, 0:1, own_cols], tops_in.at[1, me, 0:1, :], local_sem.at[8]),
    ]

    @pl.when(me > 0)
    def _():
        for copy in m_own:
            copy.start()
        for copies in m_moved:
            for copy in copies:
                copy.start()

    def at_rows(i):
        return pl.ds(pl.multiple_of(i * rows, rows), rows)

    def blocks(table, at):
        return table[0, at, :], table[1, at, :]

    def inverse(b, at):
        ch, cl = blocks(cosines, at)
        sh, sl = blocks(sines, at)
        return dot3(ch, cl, spec, (b, 0)) - dot3(sh, sl, spec, (b, 1))

    def turned(at, re, im):
        end = coarse.shape[2] - 1
        tr, ti = coarse[0, at, end:], coarse[1, at, end:]
        return re * tr - im * ti, re * ti + im * tr

    def at_block(j):
        return pl.ds(pl.multiple_of(j * block, block), block)

    def decode(i, start):
        @pl.loop(start // rows, n // rows)
        def _(r):
            at = at_rows(r)
            step = tops_in[i, r // (tok // rows), 0:1, :]
            split_to(gd, (i,), at, decoded(codes_in[i, at, :], step))

    h_relay.wait_recv()

    @pl.loop(0, n // block)
    def _(j):
        at = at_block(j)
        ch, cl = blocks(cosines, at)
        sh, sl = blocks(sines, at)
        h = hb[...].reshape(n, width)
        hr, hi = turned(at, dot(ch, h) + dot(cl, h), -(dot(sh, h) + dot(sl, h)))
        hspec[0, at, :], hspec[1, at, :] = hr, hi

    for moved in g_moved:
        arrived(moved)
    decode(0, 0)

    @pl.loop(0, n // block)
    def _(j):
        at = at_block(j)
        ch, cl = blocks(cosines, at)
        sh, sl = blocks(sines, at)
        hr, hi = hspec[0, at, :], hspec[1, at, :]
        gr, gi = dot3(ch, cl, gd, (0,)), -dot3(sh, sl, gd, (0,))
        split_to(spec, (0, 0), at, gr * hr - gi * hi)
        split_to(spec, (0, 1), at, gr * hi + gi * hr)
        gspec[0, at, :], gspec[1, at, :] = turned(at, gr, gi)

    def back_copy(i, s, dest):
        return to_peer(5 + 2 * i, s, back.at[i, rows_of(dest), :], back_in.at[i, :, own_cols])

    def edge_copy(i, s, dest):
        return to_peer(6 + 2 * i, s, edges.at[i, dest, 0:3, :], edges_in.at[i, 0:3, own_cols])

    def needed(i, dest):
        return (dest != me) if i else ((dest != me) & (dest != 0))

    def send_back(i):
        steps = n // block

        @pl.loop(0, steps)
        def _(r):
            j = lax.rem(me // span + steps // 2 + r, steps)
            value = inverse(i, at_block(j)) * (1.0 / n)
            for e in range(span):
                dest = j * span + e
                piece = value[e * tok : (e + 1) * tok]
                top = jnp.max(jnp.abs(piece), axis=0, keepdims=True)
                back[i, rows_of(dest), :] = coded(piece, top)
                edges[i, dest, 0:1, :] = top * (1.0 / CODES)
                edges[i, lax.rem(dest + parts - 1, parts), 1:3, :] = piece[:2]
            for e in range(span):
                dest = j * span + e

                @pl.when(needed(i, dest))
                def _():
                    back_copy(i, lax.rem(dest + parts - me, parts), dest).start()

        for s in range(1, parts):
            edge_copy(i, s, peers[s]).start()
        own = (
            pltpu.make_async_copy(
                back.at[i, mine, :], back_in.at[i, :, own_cols], local_sem.at[9 + 2 * i]
            ),
            pltpu.make_async_copy(
                edges.at[i, me, 0:3, :], edges_in.at[i, 0:3, own_cols], local_sem.at[10 + 2 * i]
            ),
        )
        for copy in own:
            copy.start()
        return own

    def back_arrived(i, own):
        for copy in own:
            copy.wait()
        for s in range(1, parts):
            data = back_copy(i, s, peers[s])
            edge_copy(i, s, peers[s]).wait_recv()
            if i:
                data.wait_recv()
            else:
                pl.when(me > 0)(data.wait_recv)

    def back_sent(i):
        for s in range(1, parts):
            data = back_copy(i, s, peers[s])
            edge_copy(i, s, peers[s]).wait_send()
            if i:
                data.wait_send()
            else:
                pl.when(peers[s] != 0)(data.wait_send)

    y_own = send_back(0)

    gd[1, :, :tok, :] = jnp.zeros((2, tok, width), bf16)

    @pl.when(me > 0)
    def _():
        for copy in m_own:
            copy.wait()
    for s in range(1, parts):

        @pl.when(sources[s] != 0)
        def _(s=s):
            for copy in m_moved[s - 1]:
                copy.wait_recv()

    decode(1, tok)

    @pl.loop(0, n // block)
    def _(j):
        at = at_block(j)
        ch, cl = blocks(cosines, at)
        sh, sl = blocks(sines, at)
        dr, di = dot3(ch, cl, gd, (1,)), -dot3(sh, sl, gd, (1,))
        hr, hi = hspec[0, at, :], hspec[1, at, :]
        split_to(spec, (1, 0), at, hr * dr + hi * di)
        split_to(spec, (1, 1), at, hr * di - hi * dr)
        gr, gi = gspec[0, at, :], gspec[1, at, :]
        split_to(spec, (2, 0), at, gr * dr + gi * di)
        split_to(spec, (2, 1), at, gr * di - gi * dr)

    d_own = send_back(1)

    @pl.loop(0, n // block)
    def _(j):
        at = at_block(j)
        filt[at, :] = inverse(2, at) * (scale / n)

    f_add = to_partner(1, filt.at[:, other_half], fother)
    f_add.start()
    f_add.wait_recv()

    @pl.loop(0, n // rows)
    def _(i):
        at = at_rows(i)
        fown[at, :] = (filt[at, my_half] + fother[at, :]).astype(bf16)

    f_moved = exchange(9, lambda o: fown.at[rows_of(o), :], f_out.at[:, half_cols_of(me)])
    own_relay = to_partner(3, fown.at[mine, :], f_out.at[:, half_cols_of(me)])
    own_relay.start()

    def ahead(x, by):
        return pltpu.roll(x, x.shape[0] - by, 0)[:tok]

    def finish(b, d, cols):
        tap = [taps_in[b, j : j + 1, cols] for j in range(3)]
        grad = tap[0] * d[:tok] + tap[1] * ahead(d, 1) + tap[2] * ahead(d, 2)
        stage[b, :, cols] = grad.astype(bf16)

    def total_of(value):
        return jnp.sum(jnp.sum(value.reshape(tok // 8, 8, chunk), axis=0), axis=0, keepdims=True)

    def add_taps(r, b, d, cols):
        lags = lagged(b, cols, False)
        for j in range(3):
            row = r + j
            sums[row // 8, row % 8 : row % 8 + 1, cols] = total_of(d[:tok] * lags[j])

    def returned(i, cols):
        here = decoded(back_in[i, :, cols], edges_in[i, 0:1, cols])
        edge = jnp.where(last, 0.0, pltpu.roll(edges_in[i, :, cols], 7, 0))
        return jnp.concatenate((here, edge), axis=0)

    back_arrived(0, y_own)

    @pl.loop(0, channels // chunk)
    def _(i):
        cols = at_cols(i)
        gated = short_out[1, :, cols] * short_out[2, :, cols]
        dmask = dout[:, cols]
        d = dmask * (returned(0, cols) + skip_in[:, cols] * gated)
        finish(0, d, cols)
        add_taps(0, 0, d, cols)
        dmix = dmask * short_out[0, :, cols]
        sums[0, 3:4, cols] = total_of((dmix * gated)[:tok])

    outs = [
        pltpu.make_async_copy(stage.at[b], out.at[0], local_sem.at[16 + b])
        for b, out in enumerate((gq_out, gk_out, gv_out))
    ]
    outs[0].start()
    sum_moved = [exchange(10, lambda o: sums.at[0, 0:4, cols_of(o)], sums_in.at[me, 0, 0:4, :])]

    back_arrived(1, d_own)

    @pl.loop(0, channels // chunk)
    def _(i):
        cols = at_cols(i)
        dmix = dout[:, cols] * short_out[0, :, cols]
        dg = returned(1, cols) + skip_in[:, cols] * dmix
        d1 = dg * short_out[2, :, cols]
        finish(1, d1, cols)
        add_taps(8, 1, d1, cols)
        d2 = dg * short_out[1, :, cols]
        finish(2, d2, cols)
        add_taps(11, 2, d2, cols)

    outs[1].start()
    outs[2].start()
    sum_moved.append(
        exchange(11, lambda o: sums.at[1, 0:6, cols_of(o)], sums_in.at[me, 1, 0:6, :])
    )

    relays = [own_relay]
    for s in range(1, parts):
        f_moved[1][s - 1].wait_recv()
        block_cols = half_cols_of(sources[s])
        relay = to_partner(3 + s, f_out.at[:, block_cols], f_out.at[:, block_cols])
        relay.start()
        relays.append(relay)

    for moved in sum_moved:
        arrived(moved)
    for r, count in ((0, 4), (1, 6)):
        value = sums_in[0, r, 0:count, :]
        for p in range(1, parts):
            value = value + sums_in[p, r, 0:count, :]
        total[r, 0:count, :] = value * scale
    s_add = to_partner(2, total, other)
    s_add.start()
    s_add.wait_recv()
    taps_out[0] = total[0, 0:3, :] + other[0, 0:3, :]
    skip_out[...] = total[0, 3:4, :] + other[0, 3:4, :]
    taps_out[1] = total[1, 0:3, :] + other[1, 0:3, :]
    taps_out[2] = total[1, 3:6, :] + other[1, 3:6, :]

    f_moved[0].wait()
    for out in outs:
        out.wait()
    for relay in relays:
        relay.wait_recv()
    for halo in halos:
        halo.wait_send()
    for moved in (h_moved, *g_moved, f_moved, *sum_moved):
        for copy in moved[1]:
            copy.wait_send()

    @pl.when(me > 0)
    def _():
        for copies in m_moved:
            for copy in copies:
                copy.wait_send()

    back_sent(0)
    back_sent(1)
    for copy in (h_twin, h_relay, f_add, s_add, *relays):
        copy.wait_send()


def copy_kernel(*refs):
    count = len(refs) // 2
    for i in range(count):
        refs[count + i][...] = refs[i][...]


def dense_body(query_proj, key_proj, value_proj, cotangent, boundary, short_taps, skip_gain, long_filter):
    tok, width = query_proj.shape[1:]
    parts = lax.axis_size("seq")
    n = tok * parts
    own = width // parts
    scale = 1.0 / math.sqrt(lax.axis_size("dp") * n)
    fine, coarse = phase_tables(n)
    vmem = pl.BlockSpec(memory_space=pltpu.VMEM)
    anywhere = pl.BlockSpec(memory_space=pl.ANY)
    f32, bf16, i16 = jnp.float32, jnp.bfloat16, jnp.int16
    shape = jax.ShapeDtypeStruct
    dma = pltpu.SemaphoreType.DMA
    blocks = [pl.BlockSpec((1, tok // 4, width), lambda i: (0, i, 0))] * 3 + [
        pl.BlockSpec((tok // 4, width), lambda i: (i, 0)),
        pl.BlockSpec((3, 3, own), lambda i: (0, 0, 0)),
        pl.BlockSpec((1, own), lambda i: (0, 0)),
    ]
    results = pl.pallas_call(
        functools.partial(operator_kernel, n, parts, scale),
        out_shape=[shape((1, tok, width), bf16)] * 3
        + [shape((tok, width), bf16), shape((3, 3, own), f32), shape((1, own), f32)],
        in_specs=[pl.BlockSpec(memory_space=pltpu.SMEM)] + [anywhere] * 5 + [vmem] * 4,
        out_specs=[anywhere] * 4 + [vmem] * 2,
        scratch_shapes=[
            pltpu.VMEM((4, tok, width), bf16),
            pltpu.VMEM((8, width), f32),
            pltpu.VMEM((8, width), f32),
            pltpu.VMEM((8, width), f32),
            pltpu.VMEM((8, width), f32),
            pltpu.VMEM((3, tok + 8, width), f32),
            pltpu.VMEM((tok + 8, width), f32),
            pltpu.VMEM((2, tok, width), i16),
            pltpu.VMEM((2, 8, width), f32),
            pltpu.VMEM((2, n, own), i16),
            pltpu.VMEM((2, parts, 8, own), f32),
            pltpu.VMEM((parts, 2, tok // 2, own), bf16),
            pltpu.VMEM((2, n, n), bf16),
            pltpu.VMEM((2, n, n), bf16),
            pltpu.VMEM((2, 2, n, own), bf16),
            pltpu.VMEM((3, 2, 2, n, own), bf16),
            pltpu.VMEM((2, n, own), f32),
            pltpu.VMEM((2, n, own), f32),
            pltpu.VMEM((2, n, own), i16),
            pltpu.VMEM((2, parts, 8, own), f32),
            pltpu.VMEM((2, tok, width), i16),
            pltpu.VMEM((2, 8, width), f32),
            pltpu.VMEM((n, own), f32),
            pltpu.VMEM((n, own // 2), f32),
            pltpu.VMEM((n, own // 2), bf16),
            pltpu.VMEM((3, tok, width), bf16),
            pltpu.VMEM((2, 8, width), f32),
            pltpu.VMEM((parts, 2, 8, own), f32),
            pltpu.VMEM((2, 8, own), f32),
            pltpu.VMEM((2, 8, own), f32),
            dma((12, parts)),
            dma((12, parts)),
            dma((19,)),
            dma((4 + parts,)),
            dma((4 + parts,)),
            dma((2,)),
            dma((2,)),
        ],
        compiler_params=pltpu.CompilerParams(
            collective_id=0, has_side_effects=True, vmem_limit_bytes=56 * 2**20
        ),
    )(
        boundary, query_proj, key_proj, value_proj, cotangent, long_filter,
        short_taps, skip_gain[None], jnp.asarray(fine), jnp.asarray(coarse),
    )
    gq, gk, gv, filter_grad, taps_grad, skip_grad = pl.pallas_call(
        copy_kernel,
        out_shape=[shape(x.shape, x.dtype) for x in results],
        grid=(4,),
        in_specs=blocks,
        out_specs=blocks,
    )(*results)
    return gq, gk, gv, filter_grad, taps_grad, skip_grad.reshape(own)


def body(query_proj, key_proj, value_proj, cotangent, boundary, short_taps, skip_gain, long_filter):
    pairs, tok, width = query_proj.shape
    parts = lax.axis_size("seq")
    seq_len = tok * parts
    scale = 1.0 / math.sqrt(pairs * lax.axis_size("dp") * seq_len)
    tables = build_tables(seq_len)
    filter_cols = lax.all_to_all(
        jnp.transpose(long_filter), "seq", split_axis=0, concat_axis=1, tiled=True
    ).astype(jnp.float32)
    filt_spec = forward_half(filter_cols, tables)
    taps = short_taps[:, :, None, None, :]
    raw = jnp.stack((query_proj, key_proj, value_proj))
    tails = passed_along(raw[:, :, tok - 2 :], "seq", 1)
    extended = jnp.concatenate((tails, raw), axis=2).astype(jnp.float32)
    conv = (
        taps[:, 0] * extended[:, :, 2:]
        + taps[:, 1] * extended[:, :, 1:-1]
        + taps[:, 2] * extended[:, :, :-2]
    )
    gated = conv[1] * conv[2]
    position = lax.axis_index("seq") * tok + jnp.arange(tok, dtype=jnp.int32)
    mask = (position[None, :] >= boundary[:, None]).astype(jnp.float32)
    dout = cotangent.astype(jnp.float32) * mask[:, :, None]
    dmix = dout * conv[0]
    gated_cols = lax.all_to_all(
        jnp.transpose(gated, (0, 2, 1)), "seq", split_axis=1, concat_axis=2, tiled=True
    )
    spectra = forward_half(gated_cols[0], tables)
    conv_cols = jnp.stack([convolve_cols(spectra, filt_spec, tables)])
    conv_rows = lax.all_to_all(conv_cols, "seq", split_axis=2, concat_axis=1, tiled=True)
    dmix_cols = lax.all_to_all(
        jnp.transpose(dmix, (0, 2, 1)), "seq", split_axis=1, concat_axis=2, tiled=True
    )
    back_cols, filt_part = correlate_cols(spectra, filt_spec, dmix_cols[0], tables)
    back_list = [back_cols]
    filt_list = [filt_part]
    back_rows = lax.all_to_all(jnp.stack(back_list), "seq", split_axis=2, concat_axis=1, tiled=True)
    mixed = jnp.transpose(conv_rows, (0, 2, 1)) + skip_gain * gated
    filter_part = jnp.sum(jnp.stack(filt_list), axis=0) * scale
    filter_total = lax.psum(filter_part, "dp")
    filter_rows = lax.all_to_all(
        filter_total.astype(jnp.bfloat16), "seq", split_axis=1, concat_axis=0, tiled=True
    )
    filter_grad = jnp.transpose(filter_rows)
    dgated = jnp.transpose(back_rows, (0, 2, 1)) + skip_gain * dmix
    upstream = jnp.stack((dout * mixed, dgated * conv[2], dgated * conv[1]))
    heads = passed_along(upstream[:, :, :2], "seq", -1)
    grad_ext = jnp.concatenate((upstream, heads), axis=2)
    grads = (
        taps[:, 0] * grad_ext[:, :, :tok]
        + taps[:, 1] * grad_ext[:, :, 1 : tok + 1]
        + taps[:, 2] * grad_ext[:, :, 2:]
    )
    grads = grads.astype(jnp.bfloat16)
    taps_part = (
        jnp.stack(
            [
                jnp.sum(upstream * extended[:, :, 2 - lag : 2 - lag + tok], axis=(1, 2))
                for lag in range(3)
            ],
            axis=1,
        )
        * scale
    )
    skip_part = jnp.sum(dmix * gated, axis=(0, 1)) * scale
    taps_local, skip_local = (
        lax.psum_scatter(taps_part, "seq", scatter_dimension=2, tiled=True),
        lax.psum_scatter(skip_part, "seq", scatter_dimension=0, tiled=True),
    )
    taps_grad, skip_grad = lax.psum((taps_local, skip_local), "dp")
    return (grads[0], grads[1], grads[2], filter_grad, taps_grad, skip_grad)


def solution(mesh):
    in_specs = (
        P(("groups", "dp"), "seq", None),
        P(("groups", "dp"), "seq", None),
        P(("groups", "dp"), "seq", None),
        P(("groups", "dp"), "seq", None),
        P(("groups", "dp")),
        P(),
        P(),
        P("seq", None),
    )
    out_specs = (
        P(("groups", "dp"), "seq", None),
        P(("groups", "dp"), "seq", None),
        P(("groups", "dp"), "seq", None),
        P(("groups", "seq"), None),
        P("groups", None, "seq"),
        P(("groups", "seq")),
    )
    def chosen(query_proj, *rest):
        pairs, tok, _ = query_proj.shape
        dense = pairs == 1 and mesh.shape["dp"] == mesh.shape["groups"] == 2 and tok * mesh.shape["seq"] <= DENSE_LIMIT
        return (dense_body if dense else body)(query_proj, *rest)

    return jax.shard_map(chosen, mesh=mesh, in_specs=in_specs, out_specs=out_specs, check_vma=False)
```

```python
import functools
import math

import jax
import jax.numpy as jnp
import numpy as np
from jax import lax
from jax.experimental import pallas as pl
from jax.experimental.pallas import tpu as pltpu
from jax.sharding import PartitionSpec as P

DENSE_LIMIT = 1024
LANES = 128
CODES = 32767.0
MESH = pl.DeviceIdType.MESH


def passed_along(value, axis, by):
    count = lax.axis_size(axis)
    pairs = [(i, i + by) for i in range(count) if 0 <= i + by < count]
    return lax.ppermute(value, axis, pairs)


def matmul_high(form, left, right):
    return jnp.einsum(
        form, left, right, precision=lax.Precision.HIGHEST, preferred_element_type=jnp.float32
    )


def dot_high(left, right):
    return jnp.dot(left, right, precision=lax.Precision.HIGHEST, preferred_element_type=jnp.float32)


def angle_table(left, right, period):
    phase = (left[:, None] * right[None, :] % period).astype(jnp.float32) * (2.0 * math.pi / period)
    return (jnp.cos(phase), jnp.sin(phase))


def build_tables(seq_len):
    cols = min(128, seq_len)
    rows = 2 * seq_len // cols
    half = rows // 2
    keep = half + 1
    col_index = jnp.arange(cols, dtype=jnp.int32)
    keep_index = jnp.arange(keep, dtype=jnp.int32)
    half_index = jnp.arange(half, dtype=jnp.int32)
    col_cos, col_sin = angle_table(col_index, col_index, cols)
    first_cos, first_sin = angle_table(keep_index, half_index, rows)
    first = jnp.stack((first_cos, -first_sin))
    twist_cos, twist_sin = angle_table(keep_index, col_index, 2 * seq_len)
    twist_cos = twist_cos[:, None, :]
    twist_sin = twist_sin[:, None, :]
    fwd_real = jnp.concatenate((col_cos, -col_sin), axis=1)
    fwd_imag = jnp.concatenate((col_sin, col_cos), axis=1)
    inv_real = jnp.concatenate((col_cos, col_sin), axis=1)
    inv_imag = jnp.concatenate((-col_sin, col_cos), axis=1)
    edge = (keep_index == 0) | (keep_index == half)
    weights = jnp.where(edge, 1.0, 2.0).astype(jnp.float32) / (2.0 * seq_len)
    last_cos, last_sin = angle_table(half_index, keep_index, rows)
    last_cos = last_cos * weights[None, :]
    last_sin = last_sin * weights[None, :]
    return (first, twist_cos, twist_sin, fwd_real, fwd_imag, inv_real, inv_imag, last_cos, last_sin)


def forward_half(signal, tables):
    first, twist_cos, twist_sin, fwd_real, fwd_imag = tables[:5]
    width_c, length = signal.shape
    cols = fwd_real.shape[0]
    grid = jnp.transpose(signal.reshape(width_c, length // cols, cols), (1, 0, 2))
    partial_dft = matmul_high("pkn,nca->pkca", first, grid)
    turned_re = partial_dft[0] * twist_cos + partial_dft[1] * twist_sin
    turned_im = partial_dft[1] * twist_cos - partial_dft[0] * twist_sin
    keep = partial_dft.shape[1]
    spec = dot_high(turned_re.reshape(-1, cols), fwd_real) + dot_high(
        turned_im.reshape(-1, cols), fwd_imag
    )
    spec = spec.reshape(keep, width_c, 2, cols)
    return (spec[:, :, 0], spec[:, :, 1])


def inverse_half(spec_re, spec_im, tables):
    twist_cos, twist_sin = (tables[1], tables[2])
    inv_real, inv_imag, last_cos, last_sin = tables[5:]
    keep, width_c, cols = spec_re.shape
    wide = dot_high(spec_re.reshape(-1, cols), inv_real) + dot_high(
        spec_im.reshape(-1, cols), inv_imag
    )
    wide = wide.reshape(keep, width_c, 2, cols)
    wide_re = wide[:, :, 0]
    wide_im = wide[:, :, 1]
    turned_re = wide_re * twist_cos - wide_im * twist_sin
    turned_im = wide_im * twist_cos + wide_re * twist_sin
    grid = matmul_high("nk,kca->nca", last_cos, turned_re) - matmul_high(
        "nk,kca->nca", last_sin, turned_im
    )
    return jnp.transpose(grid, (1, 0, 2)).reshape(width_c, -1)


def convolve_cols(gated_spec, filt_spec, tables):
    gated_re, gated_im = gated_spec
    filt_re, filt_im = filt_spec
    return inverse_half(
        gated_re * filt_re - gated_im * filt_im, gated_re * filt_im + gated_im * filt_re, tables
    )


def correlate_cols(gated_spec, filt_spec, dmix_cols, tables):
    gated_re, gated_im = gated_spec
    filt_re, filt_im = filt_spec
    grad_re, grad_im = forward_half(dmix_cols, tables)
    back = inverse_half(
        filt_re * grad_re + filt_im * grad_im, filt_re * grad_im - filt_im * grad_re, tables
    )
    filt_part = inverse_half(
        grad_re * gated_re + grad_im * gated_im, grad_im * gated_re - grad_re * gated_im, tables
    )
    return (back, filt_part)


def phase_tables(n):
    index = 4 * np.arange(n, dtype=np.int64) + 1
    unit = 2.0 * np.pi / (16 * n)
    fine = (index[:, None] * index[None, :LANES] % (16 * n)) * unit
    coarse = (index[:, None] * (4 * LANES * np.arange(n // LANES))[None, :] % (16 * n)) * unit
    turn = index[:, None] * unit
    pack = lambda x: np.stack((np.cos(x), np.sin(x))).astype(np.float32)
    return pack(fine), pack(np.concatenate((coarse, turn), axis=1))


def split_to(ref, lead, rows, value, cols=slice(None)):
    high = value.astype(jnp.bfloat16)
    ref[(*lead, 0, rows, cols)] = high
    ref[(*lead, 1, rows, cols)] = (value - high.astype(jnp.float32)).astype(jnp.bfloat16)


def dot(left, right):
    return jnp.dot(left, right, preferred_element_type=jnp.float32)


def dot3(high, low, ref, lead):
    top = ref[(*lead, 0)]
    return dot(high, top) + (dot(high, ref[(*lead, 1)]) + dot(low, top))


def coded(value, top):
    return jnp.round(value * (CODES / jnp.maximum(top, 1e-30))).astype(jnp.int32).astype(jnp.int16)


def decoded(code, step):
    return code.astype(jnp.int32).astype(jnp.float32) * step


def operator_kernel(
    parts, scale, bound, q_in, k_in, v_in, c_in, h_in, taps_in, skip_in, fine, coarse,
    gq_out, gk_out, gv_out, f_out, taps_out, skip_out,
    loc, tails, heads, tails_in, heads_in, short_out, dout, codes, tops, codes_in, tops_in,
    hb, cosines, sines, gd, raw, spec, hspec, kspec, back, edges, back_in, edges_in, cross_in,
    filt, fother, fown, fcode, fcode_in, ftop, ftop_in, stage, sums, sums_in, total, other,
    send_sem, recv_sem, local_sem, dp_send, dp_recv, halo_send, halo_recv,
):
    tok, channels = loc.shape[1:]
    team = parts // 2
    n = tok * team
    width = channels // team
    half = width // 2
    share = channels // parts
    rows = 32
    block = min(256, n)
    span = block // tok
    me = lax.axis_index("seq")
    core = lax.axis_index("dp")
    group = lax.axis_index("groups")
    side = me // team
    rank = lax.rem(me, team)
    low = side == 0
    high = side == 1
    sign = jnp.where(low, 1.0, -1.0).astype(jnp.float32)
    last = me == parts - 1
    seam = me == team - 1
    partner = {"dp": 1 - core}
    twin = {"groups": 1 - group}
    group_rows = pl.ds(pl.multiple_of(group * (tok // 2), tok // 2), tok // 2)
    f32, bf16 = jnp.float32, jnp.bfloat16
    my_half = pl.ds(pl.multiple_of(core * half, half), half)
    other_half = pl.ds(pl.multiple_of((1 - core) * half, half), half)
    teams, peers = range(1, team), range(1, parts)

    def cols_of(owner):
        return pl.ds(pl.multiple_of(owner * width, width), width)

    def half_cols_of(owner):
        return pl.ds(pl.multiple_of(owner * width + core * half, half), half)

    def share_of(owner):
        return pl.ds(pl.multiple_of(owner * share, share), share)

    def rows_of(owner):
        return pl.ds(pl.multiple_of(owner * tok, tok), tok)

    mine, own_cols = rows_of(rank), cols_of(rank)

    def mate(s):
        return lax.rem(rank + s, team)

    loads = [
        pltpu.make_async_copy(x.at[0], loc.at[i], local_sem.at[i])
        for i, x in enumerate((q_in, k_in, v_in, c_in))
    ]
    for load in loads:
        load.start()

    barrier = pltpu.get_barrier_semaphore()
    for s in peers:
        device = {"seq": lax.rem(me + s, parts)}
        pl.semaphore_signal(barrier, inc=1, device_id=device, device_id_type=MESH)
    for device in (partner, twin):
        pl.semaphore_signal(barrier, inc=1, device_id=device, device_id_type=MESH)

    for load in loads:
        load.wait()
    for i in range(4):
        tails[2 * i : 2 * i + 2, :] = loc[i, tok - 16 :, :].astype(f32)[14:]
        heads[2 * i : 2 * i + 2, :] = loc[i, :16, :].astype(f32)[:2]

    pl.semaphore_wait(barrier, parts + 1)

    def remote(source, target, sems, device):
        return pltpu.make_async_remote_copy(
            src_ref=source,
            dst_ref=target,
            send_sem=sems[0],
            recv_sem=sems[1],
            device_id=device,
            device_id_type=MESH,
        )

    def to_seq(a, slot, device, source, target):
        return remote(source, target, (send_sem.at[a, slot], recv_sem.at[a, slot]), {"seq": device})

    def to_mate(a, s, source, target):
        return to_seq(a, s, side * team + mate(s), source, target)

    def across(a, s, source, target):
        return to_seq(a, team + s, (1 - side) * team + mate(s), source, target)

    def to_partner(i, source, target, device=partner):
        return remote(source, target, (dp_send.at[i], dp_recv.at[i]), device)

    def local(a, source, target):
        return pltpu.make_async_copy(source, target, local_sem.at[a])

    @pl.when(me == 0)
    def _():
        back_in[0, :, :] = jnp.zeros((tok, channels), jnp.int16)

    halos = [
        remote(x, y, (halo_send.at[i], halo_recv.at[i]), {"seq": lax.rem(me + by, parts)})
        for i, (x, y, by) in enumerate(((tails, tails_in, 1), (heads, heads_in, parts - 1)))
    ]
    for halo in halos:
        halo.start()

    h_target = hb.at[side, rank, group, :, my_half]
    h_own = local(4, h_in.at[group_rows, half_cols_of(rank)], h_target)
    h_moved = [
        to_mate(0, s, h_in.at[group_rows, half_cols_of(mate(s))], h_target) for s in teams
    ] + [
        across(0, s, h_in.at[group_rows, half_cols_of(mate(s))], h_target) for s in range(team)
    ]
    h_own.start()
    for copy in h_moved:
        copy.start()

    chunk = 128

    def at_cols(i):
        return pl.ds(pl.multiple_of(i * chunk, chunk), chunk)

    def extended(b, cols):
        before = jnp.where(me == 0, 0.0, pltpu.roll(tails_in[:, cols], 6 - 2 * b, 0))
        after = heads_in[:, cols]
        if b:
            after = pltpu.roll(after, 8 - 2 * b, 0)
        return before, loc[b, :, cols].astype(f32), after

    def lagged(b, cols, ahead):
        before, here, after = extended(b, cols)
        ext = jnp.concatenate((before, here, after) if ahead else (before, here), axis=0)
        return ext[8:], pltpu.roll(ext, 1, 0)[8:], pltpu.roll(ext, 2, 0)[8:]

    def short(b, lags, cols):
        tap = [taps_in[b, j : j + 1, cols] for j in range(3)]
        return tap[0] * lags[0] + tap[1] * lags[1] + tap[2] * lags[2]

    def encode(i, value, cols):
        top = jnp.max(jnp.abs(value), axis=0, keepdims=True)
        codes[i, :, cols] = coded(value, top)
        tops[i, 0:1, cols] = top * (1.0 / CODES)

    def make_gated(slot):
        @pl.loop(0, channels // chunk)
        def _(i):
            cols = at_cols(i)
            s1 = short(1, lagged(1, cols, True), cols)
            s2 = short(2, lagged(2, cols, True), cols)
            short_out[1, :, cols] = s1
            short_out[2, :, cols] = s2
            encode(slot, s1[:tok] * s2[:tok], cols)

    def make_dmix(slot):
        @pl.loop(0, channels // chunk)
        def _(i):
            cols = at_cols(i)
            _, here, after = extended(3, cols)
            ext = jnp.concatenate((here, after), axis=0)
            pos = me * tok + lax.broadcasted_iota(jnp.int32, (tok + 8, chunk), 0)
            masked = jnp.where((pos >= bound[0]) & (pos < parts * tok), ext, 0.0)
            dout[:, cols] = masked
            s0 = short(0, lagged(0, cols, True), cols)
            short_out[0, :, cols] = s0
            encode(slot, masked[:tok] * s0[:tok], cols)

    def code_copies(slot):
        owns, sent = [], []
        for k, (source, target) in enumerate(
            (
                (lambda o: tops.at[slot, 0:1, cols_of(o)], lambda to: tops_in.at[to, rank, 0:1, :]),
                (lambda o: codes.at[slot, :, cols_of(o)], lambda to: codes_in.at[to, mine, :]),
            )
        ):
            a = 1 + 2 * slot + k
            owns.append(local(4 + a, source(rank), target(slot)))
            sent.append([to_mate(a, s, source(mate(s)), target(slot)) for s in teams])
            if slot == 0:
                sent[-1] += [across(a, s, source(mate(s)), target(2)) for s in range(team)]
        return owns, sent

    for halo in halos:
        halo.wait_recv()
    pl.when(low)(lambda: make_gated(0))
    pl.when(high)(lambda: make_dmix(0))
    first_own, first_sent = code_copies(0)
    for copy in (*first_sent[0], *first_sent[1], *first_own):
        copy.start()

    h_own.wait()
    for copy in h_moved:
        copy.wait_recv()
    h_quarter = hb.at[:, :, group, :, my_half]
    h_twin = to_partner(1, h_quarter, h_quarter, twin)
    h_twin.start()

    @pl.loop(0, n // rows)
    def _(i):
        at = pl.ds(pl.multiple_of(i * rows, rows), rows)
        fr, fi = fine[0, at, :], fine[1, at, :]
        cr, ci = coarse[0, at, :], coarse[1, at, :]
        for a in range(n // LANES):
            ar, ai = cr[:, a : a + 1], ci[:, a : a + 1]
            cols = slice(a * LANES, (a + 1) * LANES)
            split_to(cosines, (), at, fr * ar - fi * ai, cols)
            split_to(sines, (), at, fr * ai + fi * ar, cols)

    h_twin.wait_recv()
    h_relay = to_partner(0, hb.at[:, :, :, :, my_half], hb.at[:, :, :, :, my_half])
    h_relay.start()

    pl.when(low)(lambda: make_dmix(1))
    pl.when(high)(lambda: make_gated(1))
    second_own, second_sent = code_copies(1)
    second = (*second_sent[0], *second_sent[1])

    @pl.when(me > 0)
    def _():
        for copy in (*second, *second_own):
            copy.start()

    def at_rows(i):
        return pl.ds(pl.multiple_of(i * rows, rows), rows)

    def at_block(j):
        return pl.ds(pl.multiple_of(j * block, block), block)

    def blocks(table, at):
        return table[0, at, :], table[1, at, :]

    def inverse(b, at):
        ch, cl = blocks(cosines, at)
        sh, sl = blocks(sines, at)
        return dot3(ch, cl, spec, (b, 0)) - dot3(sh, sl, spec, (b, 1))

    def turned(at, re, im):
        end = coarse.shape[2] - 1
        tr, ti = coarse[0, at, end:], coarse[1, at, end:]
        return re * tr - im * ti, re * ti + im * tr

    def forward(i, at):
        ch, cl = blocks(cosines, at)
        sh, sl = blocks(sines, at)
        return dot3(ch, cl, gd, (i,)), -dot3(sh, sl, gd, (i,))

    def decode(i):
        @pl.loop(0, n // rows)
        def _(r):
            at = at_rows(r)
            step = tops_in[i, r // (tok // rows), 0:1, :]
            split_to(gd, (i,), at, decoded(codes_in[i, at, :], step))

    def product_to(i, at, re, im):
        split_to(spec, (i, 0), at, re)
        split_to(spec, (i, 1), at, im)

    h_relay.wait_recv()

    @pl.loop(0, n // block)
    def _(j):
        at = at_block(j)
        ch, cl = blocks(cosines, at)
        sh, sl = blocks(sines, at)
        near, far = hb[0].reshape(n, width), hb[1].reshape(n, width)
        nr, ni = turned(at, dot(ch, near) + dot(cl, near), -(dot(sh, near) + dot(sl, near)))
        fr, fi = turned(at, dot(ch, far) + dot(cl, far), -(dot(sh, far) + dot(sl, far)))
        hspec[0, at, :], hspec[1, at, :] = nr, ni * sign
        kspec[0, at, :], kspec[1, at, :] = fr - ni, (fi + nr) * sign

    for copy in first_own:
        copy.wait()
    for k in range(2):
        for s in teams:
            first_sent[k][s - 1].wait_recv()
    decode(0)

    @pl.loop(0, n // block)
    def _(j):
        at = at_block(j)
        hr, hi = hspec[0, at, :], hspec[1, at, :]
        re, im = forward(0, at)
        raw[0, 0, at, :], raw[0, 1, at, :] = re, im
        product_to(0, at, re * hr - im * hi, re * hi + im * hr)

    def back_copy(i, s):
        return to_mate(5 + 2 * i, s, back.at[i, rows_of(mate(s)), :], back_in.at[i, :, own_cols])

    def edge_copy(i, s):
        return to_mate(6 + 2 * i, s, edges.at[i, mate(s), 0:3, :], edges_in.at[i, 0:3, own_cols])

    def cross_copy(i):
        slot = team + lax.rem(2 * team - 1 - rank, team)
        target = cross_in.at[i, 0:2, own_cols]
        return to_seq(6 + 2 * i, slot, team - 1, edges.at[i, team - 1, 1:3, :], target)

    def back_own(i):
        return (
            local(9 + 2 * i, back.at[i, mine, :], back_in.at[i, :, own_cols]),
            local(10 + 2 * i, edges.at[i, rank, 0:3, :], edges_in.at[i, 0:3, own_cols]),
        )

    def send_back(i):
        steps = n // block

        @pl.loop(0, steps)
        def _(r):
            j = lax.rem(rank // span + 1 + r, steps)
            value = inverse(i, at_block(j)) * (1.0 / n)
            for e in range(span):
                dest = j * span + e
                piece = value[e * tok : (e + 1) * tok]
                top = jnp.max(jnp.abs(piece), axis=0, keepdims=True)
                back[i, rows_of(dest), :] = coded(piece, top)
                edges[i, dest, 0:1, :] = top * (1.0 / CODES)
                edges[i, lax.rem(dest + team - 1, team), 1:3, :] = piece[:2]
            for e in range(span):
                dest = j * span + e
                wanted = dest != rank
                if i == 0:
                    wanted = wanted & (side * team + dest != 0)

                @pl.when(wanted)
                def _():
                    to_seq(
                        5 + 2 * i, lax.rem(dest + team - rank, team), side * team + dest,
                        back.at[i, rows_of(dest), :], back_in.at[i, :, own_cols],
                    ).start()

        for s in teams:
            edge_copy(i, s).start()
        for copy in back_own(i):
            copy.start()

        @pl.when(high)
        def _():
            cross_copy(i).start()

    def back_arrived(i):
        for copy in back_own(i):
            copy.wait()
        for s in teams:
            edge_copy(i, s).wait_recv()
            if i:
                back_copy(i, s).wait_recv()
            else:
                pl.when(me > 0)(back_copy(i, s).wait_recv)

    def cross_arrived(i):
        @pl.when(seam)
        def _():
            for s in range(team):
                source, target = edges.at[i, team - 1, 1:3, :], cross_in.at[i, 0:2, own_cols]
                to_seq(6 + 2 * i, team + s, lax.rem(me + team, parts), source, target).wait_recv()

    def back_sent(i):
        for s in teams:
            edge_copy(i, s).wait_send()
            if i:
                back_copy(i, s).wait_send()
            else:
                pl.when(side * team + mate(s) != 0)(back_copy(i, s).wait_send)

        @pl.when(high)
        def _():
            cross_copy(i).wait_send()

    send_back(0)

    @pl.when(me > 0)
    def _():
        for copy in second_own:
            copy.wait()

    for s in teams:
        source = side * team + lax.rem(rank + team - s, team)

        @pl.when(source != 0)
        def _(s=s):
            for k in range(2):
                second_sent[k][s - 1].wait_recv()

    @pl.when(low)
    def _():
        codes_in[1, 0:tok, :] = jnp.zeros((tok, width), jnp.int16)
        tops_in[1, 0, 0:1, :] = jnp.zeros((1, width), f32)

    decode(1)

    @pl.when(low)
    def _():
        @pl.loop(0, n // block)
        def _(j):
            at = at_block(j)
            raw[1, 0, at, :], raw[1, 1, at, :] = forward(1, at)

    f_part = to_partner(2, filt.at[0, :, other_half], fother.at[0])
    f_ends = [
        to_seq(9, team + 1, rank + team * (1 - side), ftop.at[0:1, :], ftop_in.at[0:1, :]),
        to_seq(9, team, rank + team * (1 - side), fcode, fcode_in),
    ]

    @pl.when(high)
    def _():
        @pl.loop(0, n // block)
        def _(j):
            at = at_block(j)
            re, im = forward(1, at)
            raw[1, 0, at, :], raw[1, 1, at, :] = re, im
            gr, gi = turned(at, re, im)
            dr, di = raw[0, 0, at, :], raw[0, 1, at, :]
            product_to(2, at, gr * dr + gi * di, gr * di - gi * dr)

        @pl.loop(0, n // block)
        def _(j):
            at = at_block(j)
            filt[0, at, :] = inverse(2, at) * (scale / n)

        f_part.start()
        f_part.wait_recv()
        part = filt[0, :, my_half] + fother[0]
        top = jnp.max(jnp.abs(part), axis=0, keepdims=True)
        fcode[...] = coded(part, top)
        ftop[0:1, :] = top * (1.0 / CODES)
        for copy in f_ends:
            copy.start()

    for k in range(2):
        for s in range(team):
            first_sent[k][team - 1 + s].wait_recv()
    decode(2)

    def second_stage(at):
        cr, ci = forward(2, at)
        hr, hi = hspec[0, at, :], hspec[1, at, :]
        kr, ki = kspec[0, at, :], kspec[1, at, :]
        sr, si = raw[1, 0, at, :], raw[1, 1, at, :]
        product_to(
            1, at, hr * sr + hi * si + (kr * cr + ki * ci), hr * si - hi * sr + (kr * ci - ki * cr)
        )
        return cr, ci, sr, si

    @pl.when(low)
    def _():
        @pl.loop(0, n // block)
        def _(j):
            at = at_block(j)
            cr, ci, sr, si = second_stage(at)
            gr, gi = turned(at, raw[0, 0, at, :], raw[0, 1, at, :])
            dr, di = sr + ci, si - cr
            product_to(2, at, gr * dr + gi * di, gr * di - gi * dr)

    @pl.when(high)
    def _():
        @pl.loop(0, n // block)
        def _(j):
            at = at_block(j)
            cr, ci, _, _ = second_stage(at)
            gr, gi = turned(at, cr, ci)
            dr, di = raw[0, 0, at, :], raw[0, 1, at, :]
            product_to(2, at, gr * dr + gi * di, gr * di - gi * dr)

    send_back(1)

    @pl.loop(0, n // block)
    def _(j):
        at = at_block(j)
        filt[1, at, :] = inverse(2, at) * (scale / n)

    f_add = to_partner(3, filt.at[1, :, other_half], fother.at[1])
    f_add.start()
    f_add.wait_recv()

    @pl.when(low)
    def _():
        for copy in f_ends:
            copy.wait_recv()
        part = filt[1, :, my_half] + fother[1]
        fown[...] = (part + decoded(fcode_in[...], ftop_in[0:1, :])).astype(bf16)

    @pl.when(high)
    def _():
        fown[...] = (filt[1, :, my_half] + fother[1]).astype(bf16)

    f_target = f_out.at[:, half_cols_of(rank)]
    f_own = local(13, fown.at[mine, :], f_target)
    f_moved = [to_mate(9, s, fown.at[rows_of(mate(s)), :], f_target) for s in teams]
    own_relay = to_partner(4, fown.at[mine, :], f_target)
    for copy in (*f_moved, f_own, own_relay):
        copy.start()

    def ahead(x, by):
        return pltpu.roll(x, x.shape[0] - by, 0)[:tok]

    def finish(b, d, cols):
        tap = [taps_in[b, j : j + 1, cols] for j in range(3)]
        grad = tap[0] * d[:tok] + tap[1] * ahead(d, 1) + tap[2] * ahead(d, 2)
        stage[b, :, cols] = grad.astype(bf16)

    def total_of(value):
        return jnp.sum(jnp.sum(value.reshape(tok // 8, 8, chunk), axis=0), axis=0, keepdims=True)

    def add_taps(r, b, d, cols):
        lags = lagged(b, cols, False)
        for j in range(3):
            row = r + j
            sums[row // 8, row % 8 : row % 8 + 1, cols] = total_of(d[:tok] * lags[j])

    def returned(i, cols):
        here = decoded(back_in[i, :, cols], edges_in[i, 0:1, cols])
        edge = pltpu.roll(edges_in[i, :, cols], 7, 0)
        edge = jnp.where(seam, cross_in[1 - i, :, cols], edge)
        return jnp.concatenate((here, jnp.where(last, 0.0, edge)), axis=0)

    counts = (4, 6)

    def sum_own(r):
        return local(
            14 + r, sums.at[r, 0 : counts[r], share_of(me)], sums_in.at[me, r, 0 : counts[r], :]
        )

    def sum_copy(r, s):
        peer = lax.rem(me + s, parts)
        source = sums.at[r, 0 : counts[r], share_of(peer)]
        return to_seq(10 + r, s, peer, source, sums_in.at[me, r, 0 : counts[r], :])

    outs = [
        local(16 + b, stage.at[b], out.at[0]) for b, out in enumerate((gq_out, gk_out, gv_out))
    ]

    def finish_query():
        @pl.loop(0, channels // chunk)
        def _(i):
            cols = at_cols(i)
            gated = short_out[1, :, cols] * short_out[2, :, cols]
            dmask = dout[:, cols]
            d = dmask * (returned(side, cols) + skip_in[:, cols] * gated)
            finish(0, d, cols)
            add_taps(0, 0, d, cols)
            dmix = dmask * short_out[0, :, cols]
            sums[0, 3:4, cols] = total_of((dmix * gated)[:tok])

        outs[0].start()
        sum_own(0).start()
        for s in peers:
            sum_copy(0, s).start()

    def finish_rest():
        @pl.loop(0, channels // chunk)
        def _(i):
            cols = at_cols(i)
            dmix = dout[:, cols] * short_out[0, :, cols]
            dg = returned(1 - side, cols) + skip_in[:, cols] * dmix
            d1 = dg * short_out[2, :, cols]
            finish(1, d1, cols)
            add_taps(8, 1, d1, cols)
            d2 = dg * short_out[1, :, cols]
            finish(2, d2, cols)
            add_taps(11, 2, d2, cols)

        outs[1].start()
        outs[2].start()
        sum_own(1).start()
        for s in peers:
            sum_copy(1, s).start()

    back_arrived(0)
    cross_arrived(1)
    pl.when(low)(finish_query)
    pl.when(high)(finish_rest)
    back_arrived(1)
    cross_arrived(0)
    pl.when(low)(finish_rest)
    pl.when(high)(finish_query)

    relays = [own_relay]
    for s in teams:
        f_moved[s - 1].wait_recv()
        block_cols = half_cols_of(lax.rem(rank + team - s, team))
        relay = to_partner(4 + s, f_out.at[:, block_cols], f_out.at[:, block_cols])
        relay.start()
        relays.append(relay)

    for r in range(2):
        sum_own(r).wait()
        for s in peers:
            sum_copy(r, s).wait_recv()
        value = sums_in[0, r, 0 : counts[r], :]
        for p in range(1, parts):
            value = value + sums_in[p, r, 0 : counts[r], :]
        total[r, 0 : counts[r], :] = value * scale
    s_add = to_partner(4 + team, total, other)
    s_add.start()
    s_add.wait_recv()
    taps_out[0] = total[0, 0:3, :] + other[0, 0:3, :]
    skip_out[...] = total[0, 3:4, :] + other[0, 3:4, :]
    taps_out[1] = total[1, 0:3, :] + other[1, 0:3, :]
    taps_out[2] = total[1, 3:6, :] + other[1, 3:6, :]

    f_own.wait()
    for out in outs:
        out.wait()
    for relay in relays:
        relay.wait_recv()

    for copy in (*halos, *h_moved, *first_sent[0], *first_sent[1], *f_moved):
        copy.wait_send()

    @pl.when(me > 0)
    def _():
        for copy in second:
            copy.wait_send()

    @pl.when(high)
    def _():
        f_part.wait_send()
        for copy in f_ends:
            copy.wait_send()

    back_sent(0)
    back_sent(1)
    for r in range(2):
        for s in peers:
            sum_copy(r, s).wait_send()
    for copy in (h_twin, h_relay, f_add, s_add, *relays):
        copy.wait_send()


def copy_kernel(*refs):
    count = len(refs) // 2
    for i in range(count):
        refs[count + i][...] = refs[i][...]


def dense_body(query_proj, key_proj, value_proj, cotangent, boundary, short_taps, skip_gain, long_filter):
    tok, width = query_proj.shape[1:]
    parts = lax.axis_size("seq")
    team = parts // 2
    n = tok * team
    own, wide = width // parts, width // team
    scale = 1.0 / math.sqrt(lax.axis_size("dp") * tok * parts)
    fine, coarse = phase_tables(n)
    vmem = pl.BlockSpec(memory_space=pltpu.VMEM)
    anywhere = pl.BlockSpec(memory_space=pl.ANY)
    f32, bf16, i16 = jnp.float32, jnp.bfloat16, jnp.int16
    shape = jax.ShapeDtypeStruct
    dma = pltpu.SemaphoreType.DMA
    blocks = [pl.BlockSpec((1, tok // 4, width), lambda i: (0, i, 0))] * 3 + [
        pl.BlockSpec((tok // 4, width), lambda i: (i, 0)),
        pl.BlockSpec((3, 3, own), lambda i: (0, 0, 0)),
        pl.BlockSpec((1, own), lambda i: (0, 0)),
    ]
    results = pl.pallas_call(
        functools.partial(operator_kernel, parts, scale),
        out_shape=[shape((1, tok, width), bf16)] * 3
        + [shape((tok, width), bf16), shape((3, 3, own), f32), shape((1, own), f32)],
        in_specs=[pl.BlockSpec(memory_space=pltpu.SMEM)] + [anywhere] * 5 + [vmem] * 4,
        out_specs=[anywhere] * 4 + [vmem] * 2,
        scratch_shapes=[
            pltpu.VMEM((4, tok, width), bf16),
            pltpu.VMEM((8, width), f32),
            pltpu.VMEM((8, width), f32),
            pltpu.VMEM((8, width), f32),
            pltpu.VMEM((8, width), f32),
            pltpu.VMEM((3, tok + 8, width), f32),
            pltpu.VMEM((tok + 8, width), f32),
            pltpu.VMEM((2, tok, width), i16),
            pltpu.VMEM((2, 8, width), f32),
            pltpu.VMEM((3, n, wide), i16),
            pltpu.VMEM((3, team, 8, wide), f32),
            pltpu.VMEM((2, team, 2, tok // 2, wide), bf16),
            pltpu.VMEM((2, n, n), bf16),
            pltpu.VMEM((2, n, n), bf16),
            pltpu.VMEM((3, 2, n, wide), bf16),
            pltpu.VMEM((2, 2, n, wide), f32),
            pltpu.VMEM((3, 2, 2, n, wide), bf16),
            pltpu.VMEM((2, n, wide), f32),
            pltpu.VMEM((2, n, wide), f32),
            pltpu.VMEM((2, n, wide), i16),
            pltpu.VMEM((2, team, 8, wide), f32),
            pltpu.VMEM((2, tok, width), i16),
            pltpu.VMEM((2, 8, width), f32),
            pltpu.VMEM((2, 8, width), f32),
            pltpu.VMEM((2, n, wide), f32),
            pltpu.VMEM((2, n, wide // 2), f32),
            pltpu.VMEM((n, wide // 2), bf16),
            pltpu.VMEM((n, wide // 2), i16),
            pltpu.VMEM((n, wide // 2), i16),
            pltpu.VMEM((8, wide // 2), f32),
            pltpu.VMEM((8, wide // 2), f32),
            pltpu.VMEM((3, tok, width), bf16),
            pltpu.VMEM((2, 8, width), f32),
            pltpu.VMEM((parts, 2, 8, own), f32),
            pltpu.VMEM((2, 8, own), f32),
            pltpu.VMEM((2, 8, own), f32),
            dma((12, parts)),
            dma((12, parts)),
            dma((19,)),
            dma((5 + team,)),
            dma((5 + team,)),
            dma((2,)),
            dma((2,)),
        ],
        compiler_params=pltpu.CompilerParams(
            collective_id=0, has_side_effects=True, vmem_limit_bytes=56 * 2**20
        ),
    )(
        boundary, query_proj, key_proj, value_proj, cotangent, long_filter,
        short_taps, skip_gain[None], jnp.asarray(fine), jnp.asarray(coarse),
    )
    gq, gk, gv, filter_grad, taps_grad, skip_grad = pl.pallas_call(
        copy_kernel,
        out_shape=[shape(x.shape, x.dtype) for x in results],
        grid=(4,),
        in_specs=blocks,
        out_specs=blocks,
    )(*results)
    return gq, gk, gv, filter_grad, taps_grad, skip_grad.reshape(own)


def body(query_proj, key_proj, value_proj, cotangent, boundary, short_taps, skip_gain, long_filter):
    pairs, tok, width = query_proj.shape
    parts = lax.axis_size("seq")
    seq_len = tok * parts
    scale = 1.0 / math.sqrt(pairs * lax.axis_size("dp") * seq_len)
    tables = build_tables(seq_len)
    filter_cols = lax.all_to_all(
        jnp.transpose(long_filter), "seq", split_axis=0, concat_axis=1, tiled=True
    ).astype(jnp.float32)
    filt_spec = forward_half(filter_cols, tables)
    taps = short_taps[:, :, None, None, :]
    raw = jnp.stack((query_proj, key_proj, value_proj))
    tails = passed_along(raw[:, :, tok - 2 :], "seq", 1)
    extended = jnp.concatenate((tails, raw), axis=2).astype(jnp.float32)
    conv = (
        taps[:, 0] * extended[:, :, 2:]
        + taps[:, 1] * extended[:, :, 1:-1]
        + taps[:, 2] * extended[:, :, :-2]
    )
    gated = conv[1] * conv[2]
    position = lax.axis_index("seq") * tok + jnp.arange(tok, dtype=jnp.int32)
    mask = (position[None, :] >= boundary[:, None]).astype(jnp.float32)
    dout = cotangent.astype(jnp.float32) * mask[:, :, None]
    dmix = dout * conv[0]
    gated_cols = lax.all_to_all(
        jnp.transpose(gated, (0, 2, 1)), "seq", split_axis=1, concat_axis=2, tiled=True
    )
    spectra = forward_half(gated_cols[0], tables)
    conv_cols = jnp.stack([convolve_cols(spectra, filt_spec, tables)])
    conv_rows = lax.all_to_all(conv_cols, "seq", split_axis=2, concat_axis=1, tiled=True)
    dmix_cols = lax.all_to_all(
        jnp.transpose(dmix, (0, 2, 1)), "seq", split_axis=1, concat_axis=2, tiled=True
    )
    back_cols, filt_part = correlate_cols(spectra, filt_spec, dmix_cols[0], tables)
    back_list = [back_cols]
    filt_list = [filt_part]
    back_rows = lax.all_to_all(jnp.stack(back_list), "seq", split_axis=2, concat_axis=1, tiled=True)
    mixed = jnp.transpose(conv_rows, (0, 2, 1)) + skip_gain * gated
    filter_part = jnp.sum(jnp.stack(filt_list), axis=0) * scale
    filter_total = lax.psum(filter_part, "dp")
    filter_rows = lax.all_to_all(
        filter_total.astype(jnp.bfloat16), "seq", split_axis=1, concat_axis=0, tiled=True
    )
    filter_grad = jnp.transpose(filter_rows)
    dgated = jnp.transpose(back_rows, (0, 2, 1)) + skip_gain * dmix
    upstream = jnp.stack((dout * mixed, dgated * conv[2], dgated * conv[1]))
    heads = passed_along(upstream[:, :, :2], "seq", -1)
    grad_ext = jnp.concatenate((upstream, heads), axis=2)
    grads = (
        taps[:, 0] * grad_ext[:, :, :tok]
        + taps[:, 1] * grad_ext[:, :, 1 : tok + 1]
        + taps[:, 2] * grad_ext[:, :, 2:]
    )
    grads = grads.astype(jnp.bfloat16)
    taps_part = (
        jnp.stack(
            [
                jnp.sum(upstream * extended[:, :, 2 - lag : 2 - lag + tok], axis=(1, 2))
                for lag in range(3)
            ],
            axis=1,
        )
        * scale
    )
    skip_part = jnp.sum(dmix * gated, axis=(0, 1)) * scale
    taps_local, skip_local = (
        lax.psum_scatter(taps_part, "seq", scatter_dimension=2, tiled=True),
        lax.psum_scatter(skip_part, "seq", scatter_dimension=0, tiled=True),
    )
    taps_grad, skip_grad = lax.psum((taps_local, skip_local), "dp")
    return (grads[0], grads[1], grads[2], filter_grad, taps_grad, skip_grad)


def solution(mesh):
    in_specs = (
        P(("groups", "dp"), "seq", None),
        P(("groups", "dp"), "seq", None),
        P(("groups", "dp"), "seq", None),
        P(("groups", "dp"), "seq", None),
        P(("groups", "dp")),
        P(),
        P(),
        P("seq", None),
    )
    out_specs = (
        P(("groups", "dp"), "seq", None),
        P(("groups", "dp"), "seq", None),
        P(("groups", "dp"), "seq", None),
        P(("groups", "seq"), None),
        P("groups", None, "seq"),
        P(("groups", "seq")),
    )
    def chosen(query_proj, *rest):
        pairs, tok, _ = query_proj.shape
        dense = pairs == 1 and mesh.shape["seq"] == 8 and mesh.shape["dp"] == mesh.shape["groups"] == 2 and tok * mesh.shape["seq"] <= DENSE_LIMIT
        return (dense_body if dense else body)(query_proj, *rest)

    return jax.shard_map(chosen, mesh=mesh, in_specs=in_specs, out_specs=out_specs, check_vma=False)
```

```python
import functools
import math

import jax
import jax.numpy as jnp
import numpy as np
from jax import lax
from jax.experimental import pallas as pl
from jax.experimental.pallas import tpu as pltpu
from jax.sharding import PartitionSpec as P

DENSE_LIMIT = 1024
LANES = 128
CODES = 32767.0
MESH = pl.DeviceIdType.MESH


def passed_along(value, axis, by):
    count = lax.axis_size(axis)
    pairs = [(i, i + by) for i in range(count) if 0 <= i + by < count]
    return lax.ppermute(value, axis, pairs)


def matmul_high(form, left, right):
    return jnp.einsum(
        form, left, right, precision=lax.Precision.HIGHEST, preferred_element_type=jnp.float32
    )


def dot_high(left, right):
    return jnp.dot(left, right, precision=lax.Precision.HIGHEST, preferred_element_type=jnp.float32)


def angle_table(left, right, period):
    phase = (left[:, None] * right[None, :] % period).astype(jnp.float32) * (2.0 * math.pi / period)
    return (jnp.cos(phase), jnp.sin(phase))


def build_tables(seq_len):
    cols = min(128, seq_len)
    rows = 2 * seq_len // cols
    half = rows // 2
    keep = half + 1
    col_index = jnp.arange(cols, dtype=jnp.int32)
    keep_index = jnp.arange(keep, dtype=jnp.int32)
    half_index = jnp.arange(half, dtype=jnp.int32)
    col_cos, col_sin = angle_table(col_index, col_index, cols)
    first_cos, first_sin = angle_table(keep_index, half_index, rows)
    first = jnp.stack((first_cos, -first_sin))
    twist_cos, twist_sin = angle_table(keep_index, col_index, 2 * seq_len)
    twist_cos = twist_cos[:, None, :]
    twist_sin = twist_sin[:, None, :]
    fwd_real = jnp.concatenate((col_cos, -col_sin), axis=1)
    fwd_imag = jnp.concatenate((col_sin, col_cos), axis=1)
    inv_real = jnp.concatenate((col_cos, col_sin), axis=1)
    inv_imag = jnp.concatenate((-col_sin, col_cos), axis=1)
    edge = (keep_index == 0) | (keep_index == half)
    weights = jnp.where(edge, 1.0, 2.0).astype(jnp.float32) / (2.0 * seq_len)
    last_cos, last_sin = angle_table(half_index, keep_index, rows)
    last_cos = last_cos * weights[None, :]
    last_sin = last_sin * weights[None, :]
    return (first, twist_cos, twist_sin, fwd_real, fwd_imag, inv_real, inv_imag, last_cos, last_sin)


def forward_half(signal, tables):
    first, twist_cos, twist_sin, fwd_real, fwd_imag = tables[:5]
    width_c, length = signal.shape
    cols = fwd_real.shape[0]
    grid = jnp.transpose(signal.reshape(width_c, length // cols, cols), (1, 0, 2))
    partial_dft = matmul_high("pkn,nca->pkca", first, grid)
    turned_re = partial_dft[0] * twist_cos + partial_dft[1] * twist_sin
    turned_im = partial_dft[1] * twist_cos - partial_dft[0] * twist_sin
    keep = partial_dft.shape[1]
    spec = dot_high(turned_re.reshape(-1, cols), fwd_real) + dot_high(
        turned_im.reshape(-1, cols), fwd_imag
    )
    spec = spec.reshape(keep, width_c, 2, cols)
    return (spec[:, :, 0], spec[:, :, 1])


def inverse_half(spec_re, spec_im, tables):
    twist_cos, twist_sin = (tables[1], tables[2])
    inv_real, inv_imag, last_cos, last_sin = tables[5:]
    keep, width_c, cols = spec_re.shape
    wide = dot_high(spec_re.reshape(-1, cols), inv_real) + dot_high(
        spec_im.reshape(-1, cols), inv_imag
    )
    wide = wide.reshape(keep, width_c, 2, cols)
    wide_re = wide[:, :, 0]
    wide_im = wide[:, :, 1]
    turned_re = wide_re * twist_cos - wide_im * twist_sin
    turned_im = wide_im * twist_cos + wide_re * twist_sin
    grid = matmul_high("nk,kca->nca", last_cos, turned_re) - matmul_high(
        "nk,kca->nca", last_sin, turned_im
    )
    return jnp.transpose(grid, (1, 0, 2)).reshape(width_c, -1)


def convolve_cols(gated_spec, filt_spec, tables):
    gated_re, gated_im = gated_spec
    filt_re, filt_im = filt_spec
    return inverse_half(
        gated_re * filt_re - gated_im * filt_im, gated_re * filt_im + gated_im * filt_re, tables
    )


def correlate_cols(gated_spec, filt_spec, dmix_cols, tables):
    gated_re, gated_im = gated_spec
    filt_re, filt_im = filt_spec
    grad_re, grad_im = forward_half(dmix_cols, tables)
    back = inverse_half(
        filt_re * grad_re + filt_im * grad_im, filt_re * grad_im - filt_im * grad_re, tables
    )
    filt_part = inverse_half(
        grad_re * gated_re + grad_im * gated_im, grad_im * gated_re - grad_re * gated_im, tables
    )
    return (back, filt_part)


def phase_tables(n):
    index = 4 * np.arange(n, dtype=np.int64) + 1
    unit = 2.0 * np.pi / (16 * n)
    fine = (index[:, None] * index[None, :LANES] % (16 * n)) * unit
    coarse = (index[:, None] * (4 * LANES * np.arange(n // LANES))[None, :] % (16 * n)) * unit
    turn = index[:, None] * unit
    pack = lambda x: np.stack((np.cos(x), np.sin(x))).astype(np.float32)
    return pack(fine), pack(np.concatenate((coarse, turn), axis=1))


def split_to(ref, lead, rows, value, cols=slice(None)):
    high = value.astype(jnp.bfloat16)
    ref[(*lead, 0, rows, cols)] = high
    ref[(*lead, 1, rows, cols)] = (value - high.astype(jnp.float32)).astype(jnp.bfloat16)


def dot(left, right):
    return jnp.dot(left, right, preferred_element_type=jnp.float32)


def dot3(high, low, ref, lead, cols=slice(None)):
    top = ref[(*lead, 0, slice(None), cols)]
    return dot(high, top) + (dot(high, ref[(*lead, 1, slice(None), cols)]) + dot(low, top))


def coded(value, top):
    return jnp.round(value * (CODES / jnp.maximum(top, 1e-30))).astype(jnp.int32).astype(jnp.int16)


def decoded(code, step):
    return code.astype(jnp.int32).astype(jnp.float32) * step


def operator_kernel(
    parts, scale, bound, q_in, k_in, v_in, c_in, h_in, taps_in, skip_in, fine, coarse,
    gq_out, gk_out, gv_out, f_out, taps_out, skip_out,
    loc, tails, heads, tails_in, heads_in, short_out, dout, codes, tops, codes_in, tops_in,
    hb, cosines, sines, gd, raw, spec, hspec, kspec, back, edges, back_in, edges_in, cross_in,
    filt, fother, fown, fcode, fcode_in, ftop, ftop_in, stage, sums, sums_in, total, other,
    send_sem, recv_sem, local_sem, dp_send, dp_recv, halo_send, halo_recv,
):
    tok, channels = loc.shape[1:]
    team = parts // 2
    n = tok * team
    width = channels // team
    half = width // 2
    share = channels // parts
    rows = 32
    block = min(256, n)
    span = block // tok
    me = lax.axis_index("seq")
    core = lax.axis_index("dp")
    group = lax.axis_index("groups")
    side = me // team
    rank = lax.rem(me, team)
    low = side == 0
    high = side == 1
    sign = jnp.where(low, 1.0, -1.0).astype(jnp.float32)
    last = me == parts - 1
    seam = me == team - 1
    partner = {"dp": 1 - core}
    twin = {"groups": 1 - group}
    group_rows = pl.ds(pl.multiple_of(group * (tok // 2), tok // 2), tok // 2)
    f32, bf16 = jnp.float32, jnp.bfloat16
    my_half = pl.ds(pl.multiple_of(core * half, half), half)
    other_half = pl.ds(pl.multiple_of((1 - core) * half, half), half)
    teams, peers = range(1, team), range(1, parts)

    def cols_of(owner):
        return pl.ds(pl.multiple_of(owner * width, width), width)

    def half_cols_of(owner):
        return pl.ds(pl.multiple_of(owner * width + core * half, half), half)

    def share_of(owner):
        return pl.ds(pl.multiple_of(owner * share, share), share)

    def rows_of(owner):
        return pl.ds(pl.multiple_of(owner * tok, tok), tok)

    mine, own_cols = rows_of(rank), cols_of(rank)

    def mate(s):
        return lax.rem(rank + s, team)

    loads = [
        pltpu.make_async_copy(x.at[0], loc.at[i], local_sem.at[i])
        for i, x in enumerate((q_in, k_in, v_in, c_in))
    ]
    for load in loads:
        load.start()

    barrier = pltpu.get_barrier_semaphore()
    for s in peers:
        device = {"seq": lax.rem(me + s, parts)}
        pl.semaphore_signal(barrier, inc=1, device_id=device, device_id_type=MESH)
    for device in (partner, twin):
        pl.semaphore_signal(barrier, inc=1, device_id=device, device_id_type=MESH)

    for load in loads:
        load.wait()
    for i in range(4):
        tails[2 * i : 2 * i + 2, :] = loc[i, tok - 16 :, :].astype(f32)[14:]
        heads[2 * i : 2 * i + 2, :] = loc[i, :16, :].astype(f32)[:2]

    pl.semaphore_wait(barrier, parts + 1)

    def remote(source, target, sems, device):
        return pltpu.make_async_remote_copy(
            src_ref=source,
            dst_ref=target,
            send_sem=sems[0],
            recv_sem=sems[1],
            device_id=device,
            device_id_type=MESH,
        )

    def to_seq(a, slot, device, source, target):
        return remote(source, target, (send_sem.at[a, slot], recv_sem.at[a, slot]), {"seq": device})

    def to_mate(a, s, source, target):
        return to_seq(a, s, side * team + mate(s), source, target)

    def across(a, s, source, target):
        return to_seq(a, team + s, (1 - side) * team + mate(s), source, target)

    def to_partner(i, source, target, device=partner):
        return remote(source, target, (dp_send.at[i], dp_recv.at[i]), device)

    def local(a, source, target):
        return pltpu.make_async_copy(source, target, local_sem.at[a])

    @pl.when(me == 0)
    def _():
        back_in[0, :, :] = jnp.zeros((tok, channels), jnp.int16)

    halos = [
        remote(x, y, (halo_send.at[i], halo_recv.at[i]), {"seq": lax.rem(me + by, parts)})
        for i, (x, y, by) in enumerate(((tails, tails_in, 1), (heads, heads_in, parts - 1)))
    ]
    for halo in halos:
        halo.start()

    h_target = hb.at[side, rank, group, :, my_half]
    h_own = local(4, h_in.at[group_rows, half_cols_of(rank)], h_target)
    h_moved = [
        to_mate(0, s, h_in.at[group_rows, half_cols_of(mate(s))], h_target) for s in teams
    ] + [
        across(0, s, h_in.at[group_rows, half_cols_of(mate(s))], h_target) for s in range(team)
    ]
    h_own.start()
    for copy in h_moved:
        copy.start()

    chunk = 128

    def at_cols(i):
        return pl.ds(pl.multiple_of(i * chunk, chunk), chunk)

    def extended(b, cols):
        before = jnp.where(me == 0, 0.0, pltpu.roll(tails_in[:, cols], 6 - 2 * b, 0))
        after = heads_in[:, cols]
        if b:
            after = pltpu.roll(after, 8 - 2 * b, 0)
        return before, loc[b, :, cols].astype(f32), after

    def lagged(b, cols, ahead):
        before, here, after = extended(b, cols)
        ext = jnp.concatenate((before, here, after) if ahead else (before, here), axis=0)
        return ext[8:], pltpu.roll(ext, 1, 0)[8:], pltpu.roll(ext, 2, 0)[8:]

    def short(b, lags, cols):
        tap = [taps_in[b, j : j + 1, cols] for j in range(3)]
        return tap[0] * lags[0] + tap[1] * lags[1] + tap[2] * lags[2]

    def encode(i, value, cols):
        top = jnp.max(jnp.abs(value), axis=0, keepdims=True)
        codes[i, :, cols] = coded(value, top)
        tops[i, 0:1, cols] = top * (1.0 / CODES)

    def make_gated(slot):
        @pl.loop(0, channels // chunk)
        def _(i):
            cols = at_cols(i)
            s1 = short(1, lagged(1, cols, True), cols)
            s2 = short(2, lagged(2, cols, True), cols)
            short_out[1, :, cols] = s1
            short_out[2, :, cols] = s2
            encode(slot, s1[:tok] * s2[:tok], cols)

    def make_dmix(slot):
        @pl.loop(0, channels // chunk)
        def _(i):
            cols = at_cols(i)
            _, here, after = extended(3, cols)
            ext = jnp.concatenate((here, after), axis=0)
            pos = me * tok + lax.broadcasted_iota(jnp.int32, (tok + 8, chunk), 0)
            masked = jnp.where((pos >= bound[0]) & (pos < parts * tok), ext, 0.0)
            dout[:, cols] = masked
            s0 = short(0, lagged(0, cols, True), cols)
            short_out[0, :, cols] = s0
            encode(slot, masked[:tok] * s0[:tok], cols)

    def tops_of(slot, to):
        def source(o):
            return tops.at[slot, 0:1, cols_of(o)]

        return local(5 + 2 * slot, source(rank), tops_in.at[to, rank, 0:1, :]), [
            to_mate(1 + 2 * slot, s, source(mate(s)), tops_in.at[to, rank, 0:1, :]) for s in teams
        ]

    def codes_of(slot, to):
        def source(o):
            return codes.at[slot, :, cols_of(o)]

        return local(6 + 2 * slot, source(rank), codes_in.at[to, mine, :]), [
            to_mate(2 + 2 * slot, s, source(mate(s)), codes_in.at[to, mine, :]) for s in teams
        ]

    def part_cols(k, owner):
        start = owner * width + (core if k else 1 - core) * half
        return pl.ds(pl.multiple_of(start, half), half)

    cross_tops = [
        across(1, s, tops.at[0, 0:1, cols_of(mate(s))], tops_in.at[2, rank, 0:1, :])
        for s in range(team)
    ]
    cross_codes = [
        [
            across(
                12 if k else 2, s,
                codes.at[0, :, part_cols(k, mate(s))], codes_in.at[2, mine, part_cols(k, 0)],
            )
            for s in range(team)
        ]
        for k in range(2)
    ]

    for halo in halos:
        halo.wait_recv()
    pl.when(low)(lambda: make_gated(0))
    pl.when(high)(lambda: make_dmix(0))
    first_tops, first_codes = tops_of(0, 0), codes_of(0, 0)
    for copy in (*first_tops[1], *cross_tops):
        copy.start()
    for s in range(team):
        cross_codes[0][s].start()
        if s:
            first_codes[1][s - 1].start()
    first_tops[0].start()
    first_codes[0].start()

    h_own.wait()
    for copy in h_moved:
        copy.wait_recv()
    h_quarter = hb.at[:, :, group, :, my_half]
    h_twin = to_partner(1, h_quarter, h_quarter, twin)
    h_twin.start()

    pl.when(low)(lambda: make_dmix(1))
    pl.when(high)(lambda: make_gated(1))
    second_tops, second_codes = tops_of(1, 1), codes_of(1, 1)
    second = (*second_tops[1], *second_codes[1])

    @pl.when(me > 0)
    def _():
        for copy in (*second, second_tops[0], second_codes[0]):
            copy.start()

    for copy in cross_codes[1]:
        copy.start()
    h_twin.wait_recv()
    h_relay = to_partner(0, hb.at[:, :, :, :, my_half], hb.at[:, :, :, :, my_half])
    h_relay.start()

    @pl.loop(0, n // rows)
    def _(i):
        at = pl.ds(pl.multiple_of(i * rows, rows), rows)
        fr, fi = fine[0, at, :], fine[1, at, :]
        cr, ci = coarse[0, at, :], coarse[1, at, :]
        for a in range(n // LANES):
            ar, ai = cr[:, a : a + 1], ci[:, a : a + 1]
            cols = slice(a * LANES, (a + 1) * LANES)
            split_to(cosines, (), at, fr * ar - fi * ai, cols)
            split_to(sines, (), at, fr * ai + fi * ar, cols)

    def at_rows(i):
        return pl.ds(pl.multiple_of(i * rows, rows), rows)

    def at_block(j):
        return pl.ds(pl.multiple_of(j * block, block), block)

    def blocks(table, at):
        return table[0, at, :], table[1, at, :]

    every = pl.ds(0, width)

    def inverse(b, at, cols=every):
        ch, cl = blocks(cosines, at)
        sh, sl = blocks(sines, at)
        return dot3(ch, cl, spec, (b, 0), cols) - dot3(sh, sl, spec, (b, 1), cols)

    def turned(at, re, im):
        end = coarse.shape[2] - 1
        tr, ti = coarse[0, at, end:], coarse[1, at, end:]
        return re * tr - im * ti, re * ti + im * tr

    def forward(i, at, cols=every):
        ch, cl = blocks(cosines, at)
        sh, sl = blocks(sines, at)
        return dot3(ch, cl, gd, (i,), cols), -dot3(sh, sl, gd, (i,), cols)

    def decode(i, cols=every):
        @pl.loop(0, n // rows)
        def _(r):
            at = at_rows(r)
            step = tops_in[i, r // (tok // rows), 0:1, cols]
            split_to(gd, (i,), at, decoded(codes_in[i, at, cols], step), cols)

    def product_to(i, at, re, im, cols=every):
        split_to(spec, (i, 0), at, re, cols)
        split_to(spec, (i, 1), at, im, cols)

    h_relay.wait_recv()

    @pl.loop(0, n // block)
    def _(j):
        at = at_block(j)
        ch, cl = blocks(cosines, at)
        sh, sl = blocks(sines, at)
        near, far = hb[0].reshape(n, width), hb[1].reshape(n, width)
        nr, ni = turned(at, dot(ch, near) + dot(cl, near), -(dot(sh, near) + dot(sl, near)))
        fr, fi = turned(at, dot(ch, far) + dot(cl, far), -(dot(sh, far) + dot(sl, far)))
        hspec[0, at, :], hspec[1, at, :] = nr, ni * sign
        kspec[0, at, :], kspec[1, at, :] = fr - ni, (fi + nr) * sign

    for own, moved in (first_tops, first_codes):
        own.wait()
        for copy in moved:
            copy.wait_recv()
    decode(0)

    @pl.loop(0, n // block)
    def _(j):
        at = at_block(j)
        hr, hi = hspec[0, at, :], hspec[1, at, :]
        re, im = forward(0, at)
        raw[0, 0, at, :], raw[0, 1, at, :] = re, im
        product_to(0, at, re * hr - im * hi, re * hi + im * hr)

    def src_cols(p):
        return part_cols(p - 1, 0) if p else every

    def dst_cols(p):
        return part_cols(p - 1, rank) if p else own_cols

    data_row, edge_row, own_sem = (5, 7, 13), (6, 8, 14), (9, 11, 19)

    def back_to(p, s, dest):
        i = min(p, 1)
        return to_seq(
            data_row[p], s, side * team + dest,
            back.at[i, rows_of(dest), src_cols(p)], back_in.at[i, :, dst_cols(p)],
        )

    def back_copy(p, s):
        return back_to(p, s, mate(s))

    def edge_copy(p, s):
        i = min(p, 1)
        source = edges.at[i, mate(s), 0:3, src_cols(p)]
        return to_mate(edge_row[p], s, source, edges_in.at[i, 0:3, dst_cols(p)])

    def cross_edge(p, slot, device):
        i = min(p, 1)
        source = edges.at[i, team - 1, 1:3, src_cols(p)]
        return to_seq(edge_row[p], team + slot, device, source, cross_in.at[i, 0:2, dst_cols(p)])

    def cross_copy(p):
        return cross_edge(p, lax.rem(2 * team - 1 - rank, team), team - 1)

    def back_own(p):
        i = min(p, 1)
        return (
            local(own_sem[p], back.at[i, mine, src_cols(p)], back_in.at[i, :, dst_cols(p)]),
            local(
                own_sem[p] + 1,
                edges.at[i, rank, 0:3, src_cols(p)], edges_in.at[i, 0:3, dst_cols(p)],
            ),
        )

    def send_back(p):
        i = min(p, 1)
        cols = src_cols(p)
        steps = n // block

        @pl.loop(0, steps)
        def _(r):
            j = lax.rem(rank // span + 1 + r, steps)
            value = inverse(i, at_block(j), cols) * (1.0 / n)
            for e in range(span):
                dest = j * span + e
                piece = value[e * tok : (e + 1) * tok]
                top = jnp.max(jnp.abs(piece), axis=0, keepdims=True)
                back[i, rows_of(dest), cols] = coded(piece, top)
                edges[i, dest, 0:1, cols] = top * (1.0 / CODES)
                edges[i, lax.rem(dest + team - 1, team), 1:3, cols] = piece[:2]
            for e in range(span):
                dest = j * span + e
                wanted = dest != rank
                if p == 0:
                    wanted = wanted & (side * team + dest != 0)

                @pl.when(wanted)
                def _():
                    back_to(p, lax.rem(dest + team - rank, team), dest).start()

        for s in teams:
            edge_copy(p, s).start()
        for copy in back_own(p):
            copy.start()

        @pl.when(high)
        def _():
            cross_copy(p).start()

    def back_arrived(p):
        for copy in back_own(p):
            copy.wait()
        for s in teams:
            edge_copy(p, s).wait_recv()
            if p:
                back_copy(p, s).wait_recv()
            else:
                pl.when(me > 0)(back_copy(p, s).wait_recv)

    def cross_arrived(p):
        @pl.when(seam)
        def _():
            for s in range(team):
                cross_edge(p, s, lax.rem(me + team, parts)).wait_recv()

    def back_sent(p):
        for s in teams:
            edge_copy(p, s).wait_send()
            if p:
                back_copy(p, s).wait_send()
            else:
                pl.when(side * team + mate(s) != 0)(back_copy(p, s).wait_send)

        @pl.when(high)
        def _():
            cross_copy(p).wait_send()

    send_back(0)

    @pl.when(me > 0)
    def _():
        second_tops[0].wait()
        second_codes[0].wait()

    for s in teams:
        source = side * team + lax.rem(rank + team - s, team)

        @pl.when(source != 0)
        def _(s=s):
            second_tops[1][s - 1].wait_recv()
            second_codes[1][s - 1].wait_recv()

    @pl.when(low)
    def _():
        codes_in[1, 0:tok, :] = jnp.zeros((tok, width), jnp.int16)
        tops_in[1, 0, 0:1, :] = jnp.zeros((1, width), f32)

    decode(1)

    @pl.when(low)
    def _():
        @pl.loop(0, n // block)
        def _(j):
            at = at_block(j)
            raw[1, 0, at, :], raw[1, 1, at, :] = forward(1, at)

    f_part = to_partner(2, filt.at[0, :, other_half], fother.at[0])
    f_ends = [
        to_seq(9, team + 1, rank + team * (1 - side), ftop.at[0:1, :], ftop_in.at[0:1, :]),
        to_seq(9, team, rank + team * (1 - side), fcode, fcode_in),
    ]

    @pl.when(high)
    def _():
        @pl.loop(0, n // block)
        def _(j):
            at = at_block(j)
            re, im = forward(1, at)
            raw[1, 0, at, :], raw[1, 1, at, :] = re, im
            gr, gi = turned(at, re, im)
            dr, di = raw[0, 0, at, :], raw[0, 1, at, :]
            product_to(2, at, gr * dr + gi * di, gr * di - gi * dr)

        @pl.loop(0, n // block)
        def _(j):
            at = at_block(j)
            filt[0, at, :] = inverse(2, at) * (scale / n)

        f_part.start()
        f_part.wait_recv()
        part = filt[0, :, my_half] + fother[0]
        top = jnp.max(jnp.abs(part), axis=0, keepdims=True)
        fcode[...] = coded(part, top)
        ftop[0:1, :] = top * (1.0 / CODES)
        for copy in f_ends:
            copy.start()

    def second_stage(at, cols):
        cr, ci = forward(2, at, cols)
        hr, hi = hspec[0, at, cols], hspec[1, at, cols]
        kr, ki = kspec[0, at, cols], kspec[1, at, cols]
        sr, si = raw[1, 0, at, cols], raw[1, 1, at, cols]
        re = hr * sr + hi * si + (kr * cr + ki * ci)
        im = hr * si - hi * sr + (kr * ci - ki * cr)
        product_to(1, at, re, im, cols)
        return cr, ci, sr, si

    f_add = to_partner(3, filt.at[1, :, other_half], fother.at[1])
    for copy in cross_tops:
        copy.wait_recv()
    for k in range(2):
        cols = part_cols(k, 0)
        for copy in cross_codes[k]:
            copy.wait_recv()
        decode(2, cols)

        @pl.when(low)
        def _():
            @pl.loop(0, n // block)
            def _(j):
                at = at_block(j)
                cr, ci, sr, si = second_stage(at, cols)
                gr, gi = turned(at, raw[0, 0, at, cols], raw[0, 1, at, cols])
                dr, di = sr + ci, si - cr
                product_to(2, at, gr * dr + gi * di, gr * di - gi * dr, cols)

        @pl.when(high)
        def _():
            @pl.loop(0, n // block)
            def _(j):
                at = at_block(j)
                cr, ci, _, _ = second_stage(at, cols)
                gr, gi = turned(at, cr, ci)
                dr, di = raw[0, 0, at, cols], raw[0, 1, at, cols]
                product_to(2, at, gr * dr + gi * di, gr * di - gi * dr, cols)

        send_back(1 + k)

        @pl.loop(0, n // block)
        def _(j):
            at = at_block(j)
            filt[1, at, cols] = inverse(2, at, cols) * (scale / n)

        if k == 0:
            f_add.start()
    f_add.wait_recv()

    @pl.when(low)
    def _():
        for copy in f_ends:
            copy.wait_recv()
        part = filt[1, :, my_half] + fother[1]
        fown[...] = (part + decoded(fcode_in[...], ftop_in[0:1, :])).astype(bf16)

    @pl.when(high)
    def _():
        fown[...] = (filt[1, :, my_half] + fother[1]).astype(bf16)

    f_target = f_out.at[:, half_cols_of(rank)]
    f_own = local(13, fown.at[mine, :], f_target)
    f_moved = [to_mate(9, s, fown.at[rows_of(mate(s)), :], f_target) for s in teams]
    own_relay = to_partner(4, fown.at[mine, :], f_target)
    for copy in (*f_moved, f_own, own_relay):
        copy.start()

    def finish(b, d, cols, row=0):
        tap = [taps_in[b, j : j + 1, cols] for j in range(3)]
        count = tok - row
        ahead = [pltpu.roll(d, d.shape[0] - by, 0)[:count] for by in (1, 2)]
        grad = tap[0] * d[:count] + tap[1] * ahead[0] + tap[2] * ahead[1]
        stage[b, row:, cols] = grad.astype(bf16)

    def total_of(value):
        return jnp.sum(jnp.sum(value.reshape(tok // 8, 8, chunk), axis=0), axis=0, keepdims=True)

    def add_taps(r, b, d, cols):
        lags = lagged(b, cols, False)
        for j in range(3):
            row = r + j
            sums[row // 8, row % 8 : row % 8 + 1, cols] = total_of(d[:tok] * lags[j])

    def returned(i, cols, row, crossed):
        here = decoded(back_in[i, row:, cols], edges_in[i, 0:1, cols])
        edge = pltpu.roll(edges_in[i, :, cols], 7, 0)
        if crossed:
            edge = jnp.where(seam, cross_in[1 - i, :, cols], edge)
        return jnp.concatenate((here, jnp.where(last, 0.0, edge)), axis=0)

    counts = (4, 6)

    def sum_own(r):
        return local(
            14 + r, sums.at[r, 0 : counts[r], share_of(me)], sums_in.at[me, r, 0 : counts[r], :]
        )

    def sum_copy(r, s):
        peer = lax.rem(me + s, parts)
        source = sums.at[r, 0 : counts[r], share_of(peer)]
        return to_seq(10 + r, s, peer, source, sums_in.at[me, r, 0 : counts[r], :])

    outs = [
        local(16 + b, stage.at[b], out.at[0]) for b, out in enumerate((gq_out, gk_out, gv_out))
    ]

    def over_cols(p, work):
        if p == 0:
            pl.loop(0, channels // chunk)(lambda i: work(at_cols(i)))
        else:
            per = half // chunk

            @pl.loop(0, team * per)
            def _(i):
                owner, c = i // per, lax.rem(i, per)
                start = owner * width + (core if p == 2 else 1 - core) * half + c * chunk
                work(pl.ds(pl.multiple_of(start, chunk), chunk))

    def query_signal(cols, row, crossed):
        gated = short_out[1, row:, cols] * short_out[2, row:, cols]
        dmask = dout[row:, cols]
        return gated, dmask, dmask * (returned(side, cols, row, crossed) + skip_in[:, cols] * gated)

    def finish_query(cols):
        gated, dmask, d = query_signal(cols, 0, False)
        finish(0, d, cols)
        add_taps(0, 0, d, cols)
        dmix = dmask * short_out[0, :, cols]
        sums[0, 3:4, cols] = total_of((dmix * gated)[:tok])

    def finish_rest(cols):
        dmix = dout[:, cols] * short_out[0, :, cols]
        dg = returned(1 - side, cols, 0, True) + skip_in[:, cols] * dmix
        d1 = dg * short_out[2, :, cols]
        finish(1, d1, cols)
        add_taps(8, 1, d1, cols)
        d2 = dg * short_out[1, :, cols]
        finish(2, d2, cols)
        add_taps(11, 2, d2, cols)

    def send_sums(r):
        sum_own(r).start()
        for s in peers:
            sum_copy(r, s).start()

    back_arrived(0)
    cross_arrived(0)

    @pl.when(low)
    def _():
        over_cols(0, finish_query)
        send_sums(0)

    @pl.when(high)
    def _():
        over_cols(0, finish_rest)
        send_sums(1)

    for p in (1, 2):
        back_arrived(p)
        pl.when(low)(lambda: over_cols(p, finish_rest))
        pl.when(high)(lambda: over_cols(p, finish_query))

    pl.when(low)(lambda: send_sums(1))
    pl.when(high)(lambda: send_sums(0))
    cross_arrived(1)
    cross_arrived(2)

    @pl.when(seam)
    def _():
        def mend(cols):
            finish(0, query_signal(cols, tok - 16, True)[2], cols, tok - 16)

        over_cols(0, mend)

    for out in outs:
        out.start()

    relays = [own_relay]
    for s in teams:
        f_moved[s - 1].wait_recv()
        block_cols = half_cols_of(lax.rem(rank + team - s, team))
        relay = to_partner(4 + s, f_out.at[:, block_cols], f_out.at[:, block_cols])
        relay.start()
        relays.append(relay)

    for r in range(2):
        sum_own(r).wait()
        for s in peers:
            sum_copy(r, s).wait_recv()
        value = sums_in[0, r, 0 : counts[r], :]
        for p in range(1, parts):
            value = value + sums_in[p, r, 0 : counts[r], :]
        total[r, 0 : counts[r], :] = value * scale
    s_add = to_partner(4 + team, total, other)
    s_add.start()
    s_add.wait_recv()
    taps_out[0] = total[0, 0:3, :] + other[0, 0:3, :]
    skip_out[...] = total[0, 3:4, :] + other[0, 3:4, :]
    taps_out[1] = total[1, 0:3, :] + other[1, 0:3, :]
    taps_out[2] = total[1, 3:6, :] + other[1, 3:6, :]

    f_own.wait()
    for out in outs:
        out.wait()
    for relay in relays:
        relay.wait_recv()

    for copy in (*halos, *h_moved, *first_tops[1], *first_codes[1], *f_moved):
        copy.wait_send()
    for copy in (*cross_tops, *cross_codes[0], *cross_codes[1]):
        copy.wait_send()

    @pl.when(me > 0)
    def _():
        for copy in second:
            copy.wait_send()

    @pl.when(high)
    def _():
        f_part.wait_send()
        for copy in f_ends:
            copy.wait_send()

    for p in range(3):
        back_sent(p)
    for r in range(2):
        for s in peers:
            sum_copy(r, s).wait_send()
    for copy in (h_twin, h_relay, f_add, s_add, *relays):
        copy.wait_send()


def copy_kernel(*refs):
    count = len(refs) // 2
    for i in range(count):
        refs[count + i][...] = refs[i][...]


def dense_body(query_proj, key_proj, value_proj, cotangent, boundary, short_taps, skip_gain, long_filter):
    tok, width = query_proj.shape[1:]
    parts = lax.axis_size("seq")
    team = parts // 2
    n = tok * team
    own, wide = width // parts, width // team
    scale = 1.0 / math.sqrt(lax.axis_size("dp") * tok * parts)
    fine, coarse = phase_tables(n)
    vmem = pl.BlockSpec(memory_space=pltpu.VMEM)
    anywhere = pl.BlockSpec(memory_space=pl.ANY)
    f32, bf16, i16 = jnp.float32, jnp.bfloat16, jnp.int16
    shape = jax.ShapeDtypeStruct
    dma = pltpu.SemaphoreType.DMA
    blocks = [pl.BlockSpec((1, tok // 4, width), lambda i: (0, i, 0))] * 3 + [
        pl.BlockSpec((tok // 4, width), lambda i: (i, 0)),
        pl.BlockSpec((3, 3, own), lambda i: (0, 0, 0)),
        pl.BlockSpec((1, own), lambda i: (0, 0)),
    ]
    results = pl.pallas_call(
        functools.partial(operator_kernel, parts, scale),
        out_shape=[shape((1, tok, width), bf16)] * 3
        + [shape((tok, width), bf16), shape((3, 3, own), f32), shape((1, own), f32)],
        in_specs=[pl.BlockSpec(memory_space=pltpu.SMEM)] + [anywhere] * 5 + [vmem] * 4,
        out_specs=[anywhere] * 4 + [vmem] * 2,
        scratch_shapes=[
            pltpu.VMEM((4, tok, width), bf16),
            pltpu.VMEM((8, width), f32),
            pltpu.VMEM((8, width), f32),
            pltpu.VMEM((8, width), f32),
            pltpu.VMEM((8, width), f32),
            pltpu.VMEM((3, tok + 8, width), f32),
            pltpu.VMEM((tok + 8, width), f32),
            pltpu.VMEM((2, tok, width), i16),
            pltpu.VMEM((2, 8, width), f32),
            pltpu.VMEM((3, n, wide), i16),
            pltpu.VMEM((3, team, 8, wide), f32),
            pltpu.VMEM((2, team, 2, tok // 2, wide), bf16),
            pltpu.VMEM((2, n, n), bf16),
            pltpu.VMEM((2, n, n), bf16),
            pltpu.VMEM((3, 2, n, wide), bf16),
            pltpu.VMEM((2, 2, n, wide), f32),
            pltpu.VMEM((3, 2, 2, n, wide), bf16),
            pltpu.VMEM((2, n, wide), f32),
            pltpu.VMEM((2, n, wide), f32),
            pltpu.VMEM((2, n, wide), i16),
            pltpu.VMEM((2, team, 8, wide), f32),
            pltpu.VMEM((2, tok, width), i16),
            pltpu.VMEM((2, 8, width), f32),
            pltpu.VMEM((2, 8, width), f32),
            pltpu.VMEM((2, n, wide), f32),
            pltpu.VMEM((2, n, wide // 2), f32),
            pltpu.VMEM((n, wide // 2), bf16),
            pltpu.VMEM((n, wide // 2), i16),
            pltpu.VMEM((n, wide // 2), i16),
            pltpu.VMEM((8, wide // 2), f32),
            pltpu.VMEM((8, wide // 2), f32),
            pltpu.VMEM((3, tok, width), bf16),
            pltpu.VMEM((2, 8, width), f32),
            pltpu.VMEM((parts, 2, 8, own), f32),
            pltpu.VMEM((2, 8, own), f32),
            pltpu.VMEM((2, 8, own), f32),
            dma((15, parts)),
            dma((15, parts)),
            dma((21,)),
            dma((5 + team,)),
            dma((5 + team,)),
            dma((2,)),
            dma((2,)),
        ],
        compiler_params=pltpu.CompilerParams(
            collective_id=0, has_side_effects=True, vmem_limit_bytes=56 * 2**20
        ),
    )(
        boundary, query_proj, key_proj, value_proj, cotangent, long_filter,
        short_taps, skip_gain[None], jnp.asarray(fine), jnp.asarray(coarse),
    )
    gq, gk, gv, filter_grad, taps_grad, skip_grad = pl.pallas_call(
        copy_kernel,
        out_shape=[shape(x.shape, x.dtype) for x in results],
        grid=(4,),
        in_specs=blocks,
        out_specs=blocks,
    )(*results)
    return gq, gk, gv, filter_grad, taps_grad, skip_grad.reshape(own)


def body(query_proj, key_proj, value_proj, cotangent, boundary, short_taps, skip_gain, long_filter):
    pairs, tok, width = query_proj.shape
    parts = lax.axis_size("seq")
    seq_len = tok * parts
    scale = 1.0 / math.sqrt(pairs * lax.axis_size("dp") * seq_len)
    tables = build_tables(seq_len)
    filter_cols = lax.all_to_all(
        jnp.transpose(long_filter), "seq", split_axis=0, concat_axis=1, tiled=True
    ).astype(jnp.float32)
    filt_spec = forward_half(filter_cols, tables)
    taps = short_taps[:, :, None, None, :]
    raw = jnp.stack((query_proj, key_proj, value_proj))
    tails = passed_along(raw[:, :, tok - 2 :], "seq", 1)
    extended = jnp.concatenate((tails, raw), axis=2).astype(jnp.float32)
    conv = (
        taps[:, 0] * extended[:, :, 2:]
        + taps[:, 1] * extended[:, :, 1:-1]
        + taps[:, 2] * extended[:, :, :-2]
    )
    gated = conv[1] * conv[2]
    position = lax.axis_index("seq") * tok + jnp.arange(tok, dtype=jnp.int32)
    mask = (position[None, :] >= boundary[:, None]).astype(jnp.float32)
    dout = cotangent.astype(jnp.float32) * mask[:, :, None]
    dmix = dout * conv[0]
    gated_cols = lax.all_to_all(
        jnp.transpose(gated, (0, 2, 1)), "seq", split_axis=1, concat_axis=2, tiled=True
    )
    spectra = forward_half(gated_cols[0], tables)
    conv_cols = jnp.stack([convolve_cols(spectra, filt_spec, tables)])
    conv_rows = lax.all_to_all(conv_cols, "seq", split_axis=2, concat_axis=1, tiled=True)
    dmix_cols = lax.all_to_all(
        jnp.transpose(dmix, (0, 2, 1)), "seq", split_axis=1, concat_axis=2, tiled=True
    )
    back_cols, filt_part = correlate_cols(spectra, filt_spec, dmix_cols[0], tables)
    back_list = [back_cols]
    filt_list = [filt_part]
    back_rows = lax.all_to_all(jnp.stack(back_list), "seq", split_axis=2, concat_axis=1, tiled=True)
    mixed = jnp.transpose(conv_rows, (0, 2, 1)) + skip_gain * gated
    filter_part = jnp.sum(jnp.stack(filt_list), axis=0) * scale
    filter_total = lax.psum(filter_part, "dp")
    filter_rows = lax.all_to_all(
        filter_total.astype(jnp.bfloat16), "seq", split_axis=1, concat_axis=0, tiled=True
    )
    filter_grad = jnp.transpose(filter_rows)
    dgated = jnp.transpose(back_rows, (0, 2, 1)) + skip_gain * dmix
    upstream = jnp.stack((dout * mixed, dgated * conv[2], dgated * conv[1]))
    heads = passed_along(upstream[:, :, :2], "seq", -1)
    grad_ext = jnp.concatenate((upstream, heads), axis=2)
    grads = (
        taps[:, 0] * grad_ext[:, :, :tok]
        + taps[:, 1] * grad_ext[:, :, 1 : tok + 1]
        + taps[:, 2] * grad_ext[:, :, 2:]
    )
    grads = grads.astype(jnp.bfloat16)
    taps_part = (
        jnp.stack(
            [
                jnp.sum(upstream * extended[:, :, 2 - lag : 2 - lag + tok], axis=(1, 2))
                for lag in range(3)
            ],
            axis=1,
        )
        * scale
    )
    skip_part = jnp.sum(dmix * gated, axis=(0, 1)) * scale
    taps_local, skip_local = (
        lax.psum_scatter(taps_part, "seq", scatter_dimension=2, tiled=True),
        lax.psum_scatter(skip_part, "seq", scatter_dimension=0, tiled=True),
    )
    taps_grad, skip_grad = lax.psum((taps_local, skip_local), "dp")
    return (grads[0], grads[1], grads[2], filter_grad, taps_grad, skip_grad)


def solution(mesh):
    in_specs = (
        P(("groups", "dp"), "seq", None),
        P(("groups", "dp"), "seq", None),
        P(("groups", "dp"), "seq", None),
        P(("groups", "dp"), "seq", None),
        P(("groups", "dp")),
        P(),
        P(),
        P("seq", None),
    )
    out_specs = (
        P(("groups", "dp"), "seq", None),
        P(("groups", "dp"), "seq", None),
        P(("groups", "dp"), "seq", None),
        P(("groups", "seq"), None),
        P("groups", None, "seq"),
        P(("groups", "seq")),
    )
    def chosen(query_proj, *rest):
        pairs, tok, _ = query_proj.shape
        dense = pairs == 1 and mesh.shape["seq"] == 8 and mesh.shape["dp"] == mesh.shape["groups"] == 2 and tok * mesh.shape["seq"] <= DENSE_LIMIT
        return (dense_body if dense else body)(query_proj, *rest)

    return jax.shard_map(chosen, mesh=mesh, in_specs=in_specs, out_specs=out_specs, check_vma=False)
```

```python
import functools
import math

import jax
import jax.numpy as jnp
import numpy as np
from jax import lax
from jax.experimental import pallas as pl
from jax.experimental.pallas import tpu as pltpu
from jax.sharding import PartitionSpec as P

DENSE_LIMIT = 1024
LANES = 128
CODES = 32767.0
MESH = pl.DeviceIdType.MESH


def passed_along(value, axis, by):
    count = lax.axis_size(axis)
    pairs = [(i, i + by) for i in range(count) if 0 <= i + by < count]
    return lax.ppermute(value, axis, pairs)


def matmul_high(form, left, right):
    return jnp.einsum(
        form, left, right, precision=lax.Precision.HIGHEST, preferred_element_type=jnp.float32
    )


def dot_high(left, right):
    return jnp.dot(left, right, precision=lax.Precision.HIGHEST, preferred_element_type=jnp.float32)


def angle_table(left, right, period):
    phase = (left[:, None] * right[None, :] % period).astype(jnp.float32) * (2.0 * math.pi / period)
    return (jnp.cos(phase), jnp.sin(phase))


def build_tables(seq_len):
    cols = min(128, seq_len)
    rows = 2 * seq_len // cols
    half = rows // 2
    keep = half + 1
    col_index = jnp.arange(cols, dtype=jnp.int32)
    keep_index = jnp.arange(keep, dtype=jnp.int32)
    half_index = jnp.arange(half, dtype=jnp.int32)
    col_cos, col_sin = angle_table(col_index, col_index, cols)
    first_cos, first_sin = angle_table(keep_index, half_index, rows)
    first = jnp.stack((first_cos, -first_sin))
    twist_cos, twist_sin = angle_table(keep_index, col_index, 2 * seq_len)
    twist_cos = twist_cos[:, None, :]
    twist_sin = twist_sin[:, None, :]
    fwd_real = jnp.concatenate((col_cos, -col_sin), axis=1)
    fwd_imag = jnp.concatenate((col_sin, col_cos), axis=1)
    inv_real = jnp.concatenate((col_cos, col_sin), axis=1)
    inv_imag = jnp.concatenate((-col_sin, col_cos), axis=1)
    edge = (keep_index == 0) | (keep_index == half)
    weights = jnp.where(edge, 1.0, 2.0).astype(jnp.float32) / (2.0 * seq_len)
    last_cos, last_sin = angle_table(half_index, keep_index, rows)
    last_cos = last_cos * weights[None, :]
    last_sin = last_sin * weights[None, :]
    return (first, twist_cos, twist_sin, fwd_real, fwd_imag, inv_real, inv_imag, last_cos, last_sin)


def forward_half(signal, tables):
    first, twist_cos, twist_sin, fwd_real, fwd_imag = tables[:5]
    width_c, length = signal.shape
    cols = fwd_real.shape[0]
    grid = jnp.transpose(signal.reshape(width_c, length // cols, cols), (1, 0, 2))
    partial_dft = matmul_high("pkn,nca->pkca", first, grid)
    turned_re = partial_dft[0] * twist_cos + partial_dft[1] * twist_sin
    turned_im = partial_dft[1] * twist_cos - partial_dft[0] * twist_sin
    keep = partial_dft.shape[1]
    spec = dot_high(turned_re.reshape(-1, cols), fwd_real) + dot_high(
        turned_im.reshape(-1, cols), fwd_imag
    )
    spec = spec.reshape(keep, width_c, 2, cols)
    return (spec[:, :, 0], spec[:, :, 1])


def inverse_half(spec_re, spec_im, tables):
    twist_cos, twist_sin = (tables[1], tables[2])
    inv_real, inv_imag, last_cos, last_sin = tables[5:]
    keep, width_c, cols = spec_re.shape
    wide = dot_high(spec_re.reshape(-1, cols), inv_real) + dot_high(
        spec_im.reshape(-1, cols), inv_imag
    )
    wide = wide.reshape(keep, width_c, 2, cols)
    wide_re = wide[:, :, 0]
    wide_im = wide[:, :, 1]
    turned_re = wide_re * twist_cos - wide_im * twist_sin
    turned_im = wide_im * twist_cos + wide_re * twist_sin
    grid = matmul_high("nk,kca->nca", last_cos, turned_re) - matmul_high(
        "nk,kca->nca", last_sin, turned_im
    )
    return jnp.transpose(grid, (1, 0, 2)).reshape(width_c, -1)


def convolve_cols(gated_spec, filt_spec, tables):
    gated_re, gated_im = gated_spec
    filt_re, filt_im = filt_spec
    return inverse_half(
        gated_re * filt_re - gated_im * filt_im, gated_re * filt_im + gated_im * filt_re, tables
    )


def correlate_cols(gated_spec, filt_spec, dmix_cols, tables):
    gated_re, gated_im = gated_spec
    filt_re, filt_im = filt_spec
    grad_re, grad_im = forward_half(dmix_cols, tables)
    back = inverse_half(
        filt_re * grad_re + filt_im * grad_im, filt_re * grad_im - filt_im * grad_re, tables
    )
    filt_part = inverse_half(
        grad_re * gated_re + grad_im * gated_im, grad_im * gated_re - grad_re * gated_im, tables
    )
    return (back, filt_part)


def phase_tables(n):
    index = 4 * np.arange(n, dtype=np.int64) + 1
    unit = 2.0 * np.pi / (16 * n)
    fine = (index[:, None] * index[None, :LANES] % (16 * n)) * unit
    coarse = (index[:, None] * (4 * LANES * np.arange(n // LANES))[None, :] % (16 * n)) * unit
    turn = index[:, None] * unit
    pack = lambda x: np.stack((np.cos(x), np.sin(x))).astype(np.float32)
    return pack(fine), pack(np.concatenate((coarse, turn), axis=1))


def split_to(ref, lead, rows, value, cols=slice(None)):
    high = value.astype(jnp.bfloat16)
    ref[(*lead, 0, rows, cols)] = high
    ref[(*lead, 1, rows, cols)] = (value - high.astype(jnp.float32)).astype(jnp.bfloat16)


def dot(left, right):
    return jnp.dot(left, right, preferred_element_type=jnp.float32)


def dot3(high, low, ref, lead, cols=slice(None)):
    top = ref[(*lead, 0, slice(None), cols)]
    return dot(high, top) + (dot(high, ref[(*lead, 1, slice(None), cols)]) + dot(low, top))


def coded(value, top):
    return jnp.round(value * (CODES / jnp.maximum(top, 1e-30))).astype(jnp.int32).astype(jnp.int16)


def decoded(code, step):
    return code.astype(jnp.int32).astype(jnp.float32) * step


def operator_kernel(
    parts, scale, bound, q_in, k_in, v_in, c_in, h_in, taps_in, skip_in, fine, coarse,
    gq_out, gk_out, gv_out, f_out, taps_out, skip_out,
    loc, tails, heads, tails_in, heads_in, short_out, dout, codes, tops, codes_in, tops_in,
    hb, cosines, sines, gd, raw, spec, hspec, kspec, back, edges, back_in, edges_in, cross_in,
    filt, fsend, fother, ftotal, fown, fcode, fcode_in, ftop, ftop_in, stage, sums, sums_in, total, other,
    send_sem, recv_sem, local_sem, dp_send, dp_recv, halo_send, halo_recv,
):
    tok, channels = loc.shape[1:]
    team = parts // 2
    n = tok * team
    width = channels // team
    half = width // 2
    share = channels // parts
    rows = 32
    block = min(256, n)
    span = block // tok
    me = lax.axis_index("seq")
    core = lax.axis_index("dp")
    group = lax.axis_index("groups")
    side = me // team
    rank = lax.rem(me, team)
    low = side == 0
    high = side == 1
    sign = jnp.where(low, 1.0, -1.0).astype(jnp.float32)
    last = me == parts - 1
    seam = me == team - 1
    partner = {"dp": 1 - core}
    twin = {"groups": 1 - group}
    group_rows = pl.ds(pl.multiple_of(group * (tok // 2), tok // 2), tok // 2)
    f32, bf16 = jnp.float32, jnp.bfloat16
    my_half = pl.ds(pl.multiple_of(core * half, half), half)
    other_half = pl.ds(pl.multiple_of((1 - core) * half, half), half)
    teams, peers = range(1, team), range(1, parts)

    def cols_of(owner):
        return pl.ds(pl.multiple_of(owner * width, width), width)

    def half_cols_of(owner):
        return pl.ds(pl.multiple_of(owner * width + core * half, half), half)

    def share_of(owner):
        return pl.ds(pl.multiple_of(owner * share, share), share)

    def rows_of(owner):
        return pl.ds(pl.multiple_of(owner * tok, tok), tok)

    mine, own_cols = rows_of(rank), cols_of(rank)

    def mate(s):
        return lax.rem(rank + s, team)

    loads = [
        pltpu.make_async_copy(x.at[0], loc.at[i], local_sem.at[i])
        for i, x in enumerate((q_in, k_in, v_in, c_in))
    ]
    for load in loads:
        load.start()

    barrier = pltpu.get_barrier_semaphore()
    for s in peers:
        device = {"seq": lax.rem(me + s, parts)}
        pl.semaphore_signal(barrier, inc=1, device_id=device, device_id_type=MESH)
    for device in (partner, twin):
        pl.semaphore_signal(barrier, inc=1, device_id=device, device_id_type=MESH)

    for load in loads:
        load.wait()
    for i in range(4):
        tails[2 * i : 2 * i + 2, :] = loc[i, tok - 16 :, :].astype(f32)[14:]
        heads[2 * i : 2 * i + 2, :] = loc[i, :16, :].astype(f32)[:2]

    pl.semaphore_wait(barrier, parts + 1)

    def remote(source, target, sems, device):
        return pltpu.make_async_remote_copy(
            src_ref=source,
            dst_ref=target,
            send_sem=sems[0],
            recv_sem=sems[1],
            device_id=device,
            device_id_type=MESH,
        )

    def to_seq(a, slot, device, source, target):
        return remote(source, target, (send_sem.at[a, slot], recv_sem.at[a, slot]), {"seq": device})

    def to_mate(a, s, source, target):
        return to_seq(a, s, side * team + mate(s), source, target)

    def across(a, s, source, target):
        return to_seq(a, team + s, (1 - side) * team + mate(s), source, target)

    def to_partner(i, source, target, device=partner):
        return remote(source, target, (dp_send.at[i], dp_recv.at[i]), device)

    def local(a, source, target):
        return pltpu.make_async_copy(source, target, local_sem.at[a])

    @pl.when(me == 0)
    def _():
        back_in[0, :, :] = jnp.zeros((tok, channels), jnp.int16)

    halos = [
        remote(x, y, (halo_send.at[i], halo_recv.at[i]), {"seq": lax.rem(me + by, parts)})
        for i, (x, y, by) in enumerate(((tails, tails_in, 1), (heads, heads_in, parts - 1)))
    ]
    for halo in halos:
        halo.start()

    h_target = hb.at[side, rank, group, :, my_half]
    h_own = local(4, h_in.at[group_rows, half_cols_of(rank)], h_target)
    h_moved = [
        to_mate(0, s, h_in.at[group_rows, half_cols_of(mate(s))], h_target) for s in teams
    ] + [
        across(0, s, h_in.at[group_rows, half_cols_of(mate(s))], h_target) for s in range(team)
    ]
    h_own.start()
    for copy in h_moved:
        copy.start()

    chunk = 128

    def at_cols(i):
        return pl.ds(pl.multiple_of(i * chunk, chunk), chunk)

    def extended(b, cols):
        before = jnp.where(me == 0, 0.0, pltpu.roll(tails_in[:, cols], 6 - 2 * b, 0))
        after = heads_in[:, cols]
        if b:
            after = pltpu.roll(after, 8 - 2 * b, 0)
        return before, loc[b, :, cols].astype(f32), after

    def lagged(b, cols, ahead):
        before, here, after = extended(b, cols)
        ext = jnp.concatenate((before, here, after) if ahead else (before, here), axis=0)
        return ext[8:], pltpu.roll(ext, 1, 0)[8:], pltpu.roll(ext, 2, 0)[8:]

    def short(b, lags, cols):
        tap = [taps_in[b, j : j + 1, cols] for j in range(3)]
        return tap[0] * lags[0] + tap[1] * lags[1] + tap[2] * lags[2]

    def encode(i, value, cols):
        top = jnp.max(jnp.abs(value), axis=0, keepdims=True)
        codes[i, :, cols] = coded(value, top)
        tops[i, 0:1, cols] = top * (1.0 / CODES)

    def make_gated(slot):
        @pl.loop(0, channels // chunk)
        def _(i):
            cols = at_cols(i)
            s1 = short(1, lagged(1, cols, True), cols)
            s2 = short(2, lagged(2, cols, True), cols)
            short_out[1, :, cols] = s1
            short_out[2, :, cols] = s2
            encode(slot, s1[:tok] * s2[:tok], cols)

    def make_dmix(slot):
        @pl.loop(0, channels // chunk)
        def _(i):
            cols = at_cols(i)
            _, here, after = extended(3, cols)
            ext = jnp.concatenate((here, after), axis=0)
            pos = me * tok + lax.broadcasted_iota(jnp.int32, (tok + 8, chunk), 0)
            masked = jnp.where((pos >= bound[0]) & (pos < parts * tok), ext, 0.0)
            dout[:, cols] = masked
            s0 = short(0, lagged(0, cols, True), cols)
            short_out[0, :, cols] = s0
            encode(slot, masked[:tok] * s0[:tok], cols)

    def tops_of(slot, to):
        def source(o):
            return tops.at[slot, 0:1, cols_of(o)]

        return local(5 + 2 * slot, source(rank), tops_in.at[to, rank, 0:1, :]), [
            to_mate(1 + 2 * slot, s, source(mate(s)), tops_in.at[to, rank, 0:1, :]) for s in teams
        ]

    def codes_of(slot, to):
        def source(o):
            return codes.at[slot, :, cols_of(o)]

        return local(6 + 2 * slot, source(rank), codes_in.at[to, mine, :]), [
            to_mate(2 + 2 * slot, s, source(mate(s)), codes_in.at[to, mine, :]) for s in teams
        ]

    def part_cols(k, owner):
        start = owner * width + (core if k else 1 - core) * half
        return pl.ds(pl.multiple_of(start, half), half)

    cross_tops = [
        across(1, s, tops.at[0, 0:1, cols_of(mate(s))], tops_in.at[2, rank, 0:1, :])
        for s in range(team)
    ]
    cross_codes = [
        [
            across(
                12 if k else 2, s,
                codes.at[0, :, part_cols(k, mate(s))], codes_in.at[2, mine, part_cols(k, 0)],
            )
            for s in range(team)
        ]
        for k in range(2)
    ]

    for halo in halos:
        halo.wait_recv()
    pl.when(low)(lambda: make_gated(0))
    pl.when(high)(lambda: make_dmix(0))
    first_tops, first_codes = tops_of(0, 0), codes_of(0, 0)
    for copy in (*first_tops[1], *cross_tops):
        copy.start()
    for copy in (*first_codes[1], *cross_codes[0]):
        copy.start()
    first_tops[0].start()
    first_codes[0].start()

    h_own.wait()
    for copy in h_moved:
        copy.wait_recv()
    h_quarter = hb.at[:, :, group, :, my_half]
    h_twin = to_partner(1, h_quarter, h_quarter, twin)
    h_twin.start()

    pl.when(low)(lambda: make_dmix(1))
    pl.when(high)(lambda: make_gated(1))
    second_tops, second_codes = tops_of(1, 1), codes_of(1, 1)
    second = (*second_tops[1], *second_codes[1])

    @pl.when(me > 0)
    def _():
        for copy in (*second, second_tops[0], second_codes[0]):
            copy.start()

    h_twin.wait_recv()
    h_relay = to_partner(0, hb.at[:, :, :, :, my_half], hb.at[:, :, :, :, my_half])
    h_relay.start()

    @pl.loop(0, n // rows)
    def _(i):
        at = pl.ds(pl.multiple_of(i * rows, rows), rows)
        fr, fi = fine[0, at, :], fine[1, at, :]
        cr, ci = coarse[0, at, :], coarse[1, at, :]
        for a in range(n // LANES):
            ar, ai = cr[:, a : a + 1], ci[:, a : a + 1]
            cols = slice(a * LANES, (a + 1) * LANES)
            split_to(cosines, (), at, fr * ar - fi * ai, cols)
            split_to(sines, (), at, fr * ai + fi * ar, cols)

    def at_rows(i):
        return pl.ds(pl.multiple_of(i * rows, rows), rows)

    def at_block(j):
        return pl.ds(pl.multiple_of(j * block, block), block)

    def blocks(table, at):
        return table[0, at, :], table[1, at, :]

    every = pl.ds(0, width)

    def inverse(b, at, cols=every):
        ch, cl = blocks(cosines, at)
        sh, sl = blocks(sines, at)
        return dot3(ch, cl, spec, (b, 0), cols) - dot3(sh, sl, spec, (b, 1), cols)

    def turned(at, re, im):
        end = coarse.shape[2] - 1
        tr, ti = coarse[0, at, end:], coarse[1, at, end:]
        return re * tr - im * ti, re * ti + im * tr

    def forward(i, at, cols=every):
        ch, cl = blocks(cosines, at)
        sh, sl = blocks(sines, at)
        return dot3(ch, cl, gd, (i,), cols), -dot3(sh, sl, gd, (i,), cols)

    def decode(i, cols=every):
        @pl.loop(0, n // rows)
        def _(r):
            at = at_rows(r)
            step = tops_in[i, r // (tok // rows), 0:1, cols]
            split_to(gd, (i,), at, decoded(codes_in[i, at, cols], step), cols)

    def product_to(i, at, re, im, cols=every):
        split_to(spec, (i, 0), at, re, cols)
        split_to(spec, (i, 1), at, im, cols)

    h_relay.wait_recv()

    @pl.loop(0, n // block)
    def _(j):
        at = at_block(j)
        ch, cl = blocks(cosines, at)
        sh, sl = blocks(sines, at)
        near, far = hb[0].reshape(n, width), hb[1].reshape(n, width)
        nr, ni = turned(at, dot(ch, near) + dot(cl, near), -(dot(sh, near) + dot(sl, near)))
        fr, fi = turned(at, dot(ch, far) + dot(cl, far), -(dot(sh, far) + dot(sl, far)))
        hspec[0, at, :], hspec[1, at, :] = nr, ni * sign
        kspec[0, at, :], kspec[1, at, :] = fr - ni, (fi + nr) * sign

    for own, moved in (first_tops, first_codes):
        own.wait()
        for copy in moved:
            copy.wait_recv()
    for copy in cross_codes[1]:
        copy.start()
    decode(0)

    @pl.loop(0, n // block)
    def _(j):
        at = at_block(j)
        hr, hi = hspec[0, at, :], hspec[1, at, :]
        re, im = forward(0, at)
        raw[0, 0, at, :], raw[0, 1, at, :] = re, im
        product_to(0, at, re * hr - im * hi, re * hi + im * hr)

    def src_cols(p):
        return part_cols(p - 1, 0) if p else every

    def dst_cols(p):
        return part_cols(p - 1, rank) if p else own_cols

    data_row, edge_row, own_sem = (5, 7, 13), (6, 8, 14), (9, 11, 19)

    def back_to(p, s, dest):
        i = min(p, 1)
        return to_seq(
            data_row[p], s, side * team + dest,
            back.at[i, rows_of(dest), src_cols(p)], back_in.at[i, :, dst_cols(p)],
        )

    def back_copy(p, s):
        return back_to(p, s, mate(s))

    def edge_copy(p, s):
        i = min(p, 1)
        source = edges.at[i, mate(s), 0:3, src_cols(p)]
        return to_mate(edge_row[p], s, source, edges_in.at[i, 0:3, dst_cols(p)])

    def cross_edge(p, slot, device):
        i = min(p, 1)
        source = edges.at[i, team - 1, 1:3, src_cols(p)]
        return to_seq(edge_row[p], team + slot, device, source, cross_in.at[i, 0:2, dst_cols(p)])

    def cross_copy(p):
        return cross_edge(p, lax.rem(2 * team - 1 - rank, team), team - 1)

    def back_own(p):
        i = min(p, 1)
        return (
            local(own_sem[p], back.at[i, mine, src_cols(p)], back_in.at[i, :, dst_cols(p)]),
            local(
                own_sem[p] + 1,
                edges.at[i, rank, 0:3, src_cols(p)], edges_in.at[i, 0:3, dst_cols(p)],
            ),
        )

    def send_back(p):
        i = min(p, 1)
        cols = src_cols(p)
        steps = n // block

        @pl.loop(0, steps)
        def _(r):
            j = lax.rem(rank // span + 1 + r, steps)
            value = inverse(i, at_block(j), cols) * (1.0 / n)
            for e in range(span):
                dest = j * span + e
                piece = value[e * tok : (e + 1) * tok]
                top = jnp.max(jnp.abs(piece), axis=0, keepdims=True)
                back[i, rows_of(dest), cols] = coded(piece, top)
                edges[i, dest, 0:1, cols] = top * (1.0 / CODES)
                edges[i, lax.rem(dest + team - 1, team), 1:3, cols] = piece[:2]
            for e in range(span):
                dest = j * span + e
                wanted = dest != rank
                if p == 0:
                    wanted = wanted & (side * team + dest != 0)

                @pl.when(wanted)
                def _():
                    back_to(p, lax.rem(dest + team - rank, team), dest).start()

        for s in teams:
            edge_copy(p, s).start()
        for copy in back_own(p):
            copy.start()

        @pl.when(high)
        def _():
            cross_copy(p).start()

    def back_arrived(p):
        for copy in back_own(p):
            copy.wait()
        for s in teams:
            edge_copy(p, s).wait_recv()
            if p:
                back_copy(p, s).wait_recv()
            else:
                pl.when(me > 0)(back_copy(p, s).wait_recv)

    def cross_arrived(p):
        @pl.when(seam)
        def _():
            for s in range(team):
                cross_edge(p, s, lax.rem(me + team, parts)).wait_recv()

    def back_sent(p):
        for s in teams:
            edge_copy(p, s).wait_send()
            if p:
                back_copy(p, s).wait_send()
            else:
                pl.when(side * team + mate(s) != 0)(back_copy(p, s).wait_send)

        @pl.when(high)
        def _():
            cross_copy(p).wait_send()

    send_back(0)

    @pl.when(me > 0)
    def _():
        second_tops[0].wait()
        second_codes[0].wait()

    for s in teams:
        source = side * team + lax.rem(rank + team - s, team)

        @pl.when(source != 0)
        def _(s=s):
            second_tops[1][s - 1].wait_recv()
            second_codes[1][s - 1].wait_recv()

    @pl.when(low)
    def _():
        codes_in[1, 0:tok, :] = jnp.zeros((tok, width), jnp.int16)
        tops_in[1, 0, 0:1, :] = jnp.zeros((1, width), f32)

    decode(1)

    @pl.when(low)
    def _():
        @pl.loop(0, n // block)
        def _(j):
            at = at_block(j)
            raw[1, 0, at, :], raw[1, 1, at, :] = forward(1, at)

    f_part = to_partner(2, filt.at[:, :, other_half], fother.at[0])
    f_ends = [
        to_seq(9, team + 1, rank + team * (1 - side), ftop.at[0:1, :], ftop_in.at[0:1, :]),
        to_seq(9, team, rank + team * (1 - side), fcode, fcode_in),
    ]

    @pl.when(high)
    def _():
        @pl.loop(0, n // block)
        def _(j):
            at = at_block(j)
            re, im = forward(1, at)
            raw[1, 0, at, :], raw[1, 1, at, :] = re, im
            gr, gi = turned(at, re, im)
            dr, di = raw[0, 0, at, :], raw[0, 1, at, :]
            filt[0, at, :] = gr * dr + gi * di
            filt[1, at, :] = gr * di - gi * dr

        f_part.start()

    def second_stage(at, cols):
        cr, ci = forward(2, at, cols)
        hr, hi = hspec[0, at, cols], hspec[1, at, cols]
        kr, ki = kspec[0, at, cols], kspec[1, at, cols]
        sr, si = raw[1, 0, at, cols], raw[1, 1, at, cols]
        re = hr * sr + hi * si + (kr * cr + ki * ci)
        im = hr * si - hi * sr + (kr * ci - ki * cr)
        product_to(1, at, re, im, cols)
        return cr, ci, sr, si

    f_add = to_partner(3, fsend, fother.at[1])
    def filter_to(k, at, re, im):
        if k:
            product_to(2, at, re + fother[1, 0, at, :], im + fother[1, 1, at, :], my_half)
        else:
            fsend[0, at, :], fsend[1, at, :] = re, im

    for copy in cross_tops:
        copy.wait_recv()
    for k in range(2):
        cols = part_cols(k, 0)
        for copy in cross_codes[k]:
            copy.wait_recv()
        decode(2, cols)
        if k:
            f_add.wait_recv()

        @pl.when(low)
        def _():
            @pl.loop(0, n // block)
            def _(j):
                at = at_block(j)
                cr, ci, sr, si = second_stage(at, cols)
                gr, gi = turned(at, raw[0, 0, at, cols], raw[0, 1, at, cols])
                dr, di = sr + ci, si - cr
                filter_to(k, at, gr * dr + gi * di, gr * di - gi * dr)

        @pl.when(high)
        def _():
            @pl.loop(0, n // block)
            def _(j):
                at = at_block(j)
                cr, ci, _, _ = second_stage(at, cols)
                gr, gi = turned(at, cr, ci)
                dr, di = raw[0, 0, at, cols], raw[0, 1, at, cols]
                filter_to(k, at, gr * dr + gi * di, gr * di - gi * dr)

        send_back(1 + k)

        if k:
            continue
        f_add.start()

        @pl.when(high)
        def _():
            f_part.wait_recv()

            @pl.loop(0, n // block)
            def _(j):
                at = at_block(j)
                re = filt[0, at, my_half] + fother[0, 0, at, :]
                product_to(2, at, re, filt[1, at, my_half] + fother[0, 1, at, :], my_half)

            @pl.loop(0, n // block)
            def _(j):
                at = at_block(j)
                ftotal[at, :] = inverse(2, at, my_half) * (scale / n)

            part = ftotal[...]
            top = jnp.max(jnp.abs(part), axis=0, keepdims=True)
            fcode[...] = coded(part, top)
            ftop[0:1, :] = top * (1.0 / CODES)
            for copy in f_ends:
                copy.start()

    @pl.loop(0, n // block)
    def _(j):
        at = at_block(j)
        ftotal[at, :] = inverse(2, at, my_half) * (scale / n)

    @pl.when(low)
    def _():
        for copy in f_ends:
            copy.wait_recv()
        fown[...] = (ftotal[...] + decoded(fcode_in[...], ftop_in[0:1, :])).astype(bf16)

    @pl.when(high)
    def _():
        fown[...] = ftotal[...].astype(bf16)

    f_target = f_out.at[:, half_cols_of(rank)]
    f_own = local(13, fown.at[mine, :], f_target)
    f_moved = [to_mate(9, s, fown.at[rows_of(mate(s)), :], f_target) for s in teams]
    own_relay = to_partner(4, fown.at[mine, :], f_target)
    for copy in (*f_moved, f_own, own_relay):
        copy.start()

    def finish(b, d, cols, row=0):
        tap = [taps_in[b, j : j + 1, cols] for j in range(3)]
        count = tok - row
        ahead = [pltpu.roll(d, d.shape[0] - by, 0)[:count] for by in (1, 2)]
        grad = tap[0] * d[:count] + tap[1] * ahead[0] + tap[2] * ahead[1]
        stage[b, row:, cols] = grad.astype(bf16)

    def total_of(value):
        return jnp.sum(jnp.sum(value.reshape(tok // 8, 8, chunk), axis=0), axis=0, keepdims=True)

    def add_taps(r, b, d, cols):
        lags = lagged(b, cols, False)
        for j in range(3):
            row = r + j
            sums[row // 8, row % 8 : row % 8 + 1, cols] = total_of(d[:tok] * lags[j])

    def returned(i, cols, row, crossed):
        here = decoded(back_in[i, row:, cols], edges_in[i, 0:1, cols])
        edge = pltpu.roll(edges_in[i, :, cols], 7, 0)
        if crossed:
            edge = jnp.where(seam, cross_in[1 - i, :, cols], edge)
        return jnp.concatenate((here, jnp.where(last, 0.0, edge)), axis=0)

    counts = (4, 6)

    def sum_own(r):
        return local(
            14 + r, sums.at[r, 0 : counts[r], share_of(me)], sums_in.at[me, r, 0 : counts[r], :]
        )

    def sum_copy(r, s):
        peer = lax.rem(me + s, parts)
        source = sums.at[r, 0 : counts[r], share_of(peer)]
        return to_seq(10 + r, s, peer, source, sums_in.at[me, r, 0 : counts[r], :])

    outs = [
        local(16 + b, stage.at[b], out.at[0]) for b, out in enumerate((gq_out, gk_out, gv_out))
    ]

    def over_cols(p, work):
        if p == 0:
            pl.loop(0, channels // chunk)(lambda i: work(at_cols(i)))
        else:
            per = half // chunk

            @pl.loop(0, team * per)
            def _(i):
                owner, c = i // per, lax.rem(i, per)
                start = owner * width + (core if p == 2 else 1 - core) * half + c * chunk
                work(pl.ds(pl.multiple_of(start, chunk), chunk))

    def query_signal(cols, row, crossed):
        gated = short_out[1, row:, cols] * short_out[2, row:, cols]
        dmask = dout[row:, cols]
        return gated, dmask, dmask * (returned(side, cols, row, crossed) + skip_in[:, cols] * gated)

    def finish_query(cols):
        gated, dmask, d = query_signal(cols, 0, False)
        finish(0, d, cols)
        add_taps(0, 0, d, cols)
        dmix = dmask * short_out[0, :, cols]
        sums[0, 3:4, cols] = total_of((dmix * gated)[:tok])

    def finish_rest(cols):
        dmix = dout[:, cols] * short_out[0, :, cols]
        dg = returned(1 - side, cols, 0, True) + skip_in[:, cols] * dmix
        d1 = dg * short_out[2, :, cols]
        finish(1, d1, cols)
        add_taps(8, 1, d1, cols)
        d2 = dg * short_out[1, :, cols]
        finish(2, d2, cols)
        add_taps(11, 2, d2, cols)

    def send_sums(r):
        sum_own(r).start()
        for s in peers:
            sum_copy(r, s).start()

    back_arrived(0)
    cross_arrived(0)

    @pl.when(low)
    def _():
        over_cols(0, finish_query)
        send_sums(0)

    @pl.when(high)
    def _():
        over_cols(0, finish_rest)
        send_sums(1)

    for p in (1, 2):
        back_arrived(p)
        pl.when(low)(lambda: over_cols(p, finish_rest))
        pl.when(high)(lambda: over_cols(p, finish_query))

    pl.when(low)(lambda: send_sums(1))
    pl.when(high)(lambda: send_sums(0))
    cross_arrived(1)
    cross_arrived(2)

    @pl.when(seam)
    def _():
        def mend(cols):
            finish(0, query_signal(cols, tok - 16, True)[2], cols, tok - 16)

        over_cols(0, mend)

    for out in outs:
        out.start()

    relays = [own_relay]
    for s in teams:
        f_moved[s - 1].wait_recv()
        block_cols = half_cols_of(lax.rem(rank + team - s, team))
        relay = to_partner(4 + s, f_out.at[:, block_cols], f_out.at[:, block_cols])
        relay.start()
        relays.append(relay)

    for r in range(2):
        sum_own(r).wait()
        for s in peers:
            sum_copy(r, s).wait_recv()
        value = sums_in[0, r, 0 : counts[r], :]
        for p in range(1, parts):
            value = value + sums_in[p, r, 0 : counts[r], :]
        total[r, 0 : counts[r], :] = value * scale
    s_add = to_partner(4 + team, total, other)
    s_add.start()
    s_add.wait_recv()
    taps_out[0] = total[0, 0:3, :] + other[0, 0:3, :]
    skip_out[...] = total[0, 3:4, :] + other[0, 3:4, :]
    taps_out[1] = total[1, 0:3, :] + other[1, 0:3, :]
    taps_out[2] = total[1, 3:6, :] + other[1, 3:6, :]

    f_own.wait()
    for out in outs:
        out.wait()
    for relay in relays:
        relay.wait_recv()

    for copy in (*halos, *h_moved, *first_tops[1], *first_codes[1], *f_moved):
        copy.wait_send()
    for copy in (*cross_tops, *cross_codes[0], *cross_codes[1]):
        copy.wait_send()

    @pl.when(me > 0)
    def _():
        for copy in second:
            copy.wait_send()

    @pl.when(high)
    def _():
        f_part.wait_send()
        for copy in f_ends:
            copy.wait_send()

    for p in range(3):
        back_sent(p)
    for r in range(2):
        for s in peers:
            sum_copy(r, s).wait_send()
    for copy in (h_twin, h_relay, f_add, s_add, *relays):
        copy.wait_send()


def copy_kernel(*refs):
    held, sems = refs[-2:]
    reads, writes = [], []
    for i in range(4):
        source, target = refs[i], refs[6 + i]
        if i < 3:
            source, target = source.at[0], target.at[0]
        half = source.shape[0] // 2
        for j in range(2):
            rows = pl.ds(j * half, half)
            reads.append(pltpu.make_async_copy(source.at[rows, :], held.at[i, rows, :], sems.at[0, i, j]))
            writes.append(pltpu.make_async_copy(held.at[i, rows, :], target.at[rows, :], sems.at[1, i, j]))
    for read in reads:
        read.start()
    for i in (4, 5):
        refs[6 + i][...] = refs[i][...]
    for read, write in zip(reads, writes):
        read.wait()
        write.start()
    for write in writes:
        write.wait()


def dense_body(query_proj, key_proj, value_proj, cotangent, boundary, short_taps, skip_gain, long_filter):
    tok, width = query_proj.shape[1:]
    parts = lax.axis_size("seq")
    team = parts // 2
    n = tok * team
    own, wide = width // parts, width // team
    scale = 1.0 / math.sqrt(lax.axis_size("dp") * tok * parts)
    fine, coarse = phase_tables(n)
    vmem = pl.BlockSpec(memory_space=pltpu.VMEM)
    anywhere = pl.BlockSpec(memory_space=pl.ANY)
    f32, bf16, i16 = jnp.float32, jnp.bfloat16, jnp.int16
    shape = jax.ShapeDtypeStruct
    dma = pltpu.SemaphoreType.DMA
    results = pl.pallas_call(
        functools.partial(operator_kernel, parts, scale),
        out_shape=[shape((1, tok, width), bf16)] * 3
        + [shape((tok, width), bf16), shape((3, 3, own), f32), shape((1, own), f32)],
        in_specs=[pl.BlockSpec(memory_space=pltpu.SMEM)] + [anywhere] * 5 + [vmem] * 4,
        out_specs=[anywhere] * 4 + [vmem] * 2,
        scratch_shapes=[
            pltpu.VMEM((4, tok, width), bf16),
            pltpu.VMEM((8, width), f32),
            pltpu.VMEM((8, width), f32),
            pltpu.VMEM((8, width), f32),
            pltpu.VMEM((8, width), f32),
            pltpu.VMEM((3, tok + 8, width), f32),
            pltpu.VMEM((tok + 8, width), f32),
            pltpu.VMEM((2, tok, width), i16),
            pltpu.VMEM((2, 8, width), f32),
            pltpu.VMEM((3, n, wide), i16),
            pltpu.VMEM((3, team, 8, wide), f32),
            pltpu.VMEM((2, team, 2, tok // 2, wide), bf16),
            pltpu.VMEM((2, n, n), bf16),
            pltpu.VMEM((2, n, n), bf16),
            pltpu.VMEM((3, 2, n, wide), bf16),
            pltpu.VMEM((2, 2, n, wide), f32),
            pltpu.VMEM((3, 2, 2, n, wide), bf16),
            pltpu.VMEM((2, n, wide), f32),
            pltpu.VMEM((2, n, wide), f32),
            pltpu.VMEM((2, n, wide), i16),
            pltpu.VMEM((2, team, 8, wide), f32),
            pltpu.VMEM((2, tok, width), i16),
            pltpu.VMEM((2, 8, width), f32),
            pltpu.VMEM((2, 8, width), f32),
            pltpu.VMEM((2, n, wide), f32),
            pltpu.VMEM((2, n, wide // 2), f32),
            pltpu.VMEM((2, 2, n, wide // 2), f32),
            pltpu.VMEM((n, wide // 2), f32),
            pltpu.VMEM((n, wide // 2), bf16),
            pltpu.VMEM((n, wide // 2), i16),
            pltpu.VMEM((n, wide // 2), i16),
            pltpu.VMEM((8, wide // 2), f32),
            pltpu.VMEM((8, wide // 2), f32),
            pltpu.VMEM((3, tok, width), bf16),
            pltpu.VMEM((2, 8, width), f32),
            pltpu.VMEM((parts, 2, 8, own), f32),
            pltpu.VMEM((2, 8, own), f32),
            pltpu.VMEM((2, 8, own), f32),
            dma((15, parts)),
            dma((15, parts)),
            dma((21,)),
            dma((5 + team,)),
            dma((5 + team,)),
            dma((2,)),
            dma((2,)),
        ],
        compiler_params=pltpu.CompilerParams(
            collective_id=0, has_side_effects=True, vmem_limit_bytes=56 * 2**20
        ),
    )(
        boundary, query_proj, key_proj, value_proj, cotangent, long_filter,
        short_taps, skip_gain[None], jnp.asarray(fine), jnp.asarray(coarse),
    )
    gq, gk, gv, filter_grad, taps_grad, skip_grad = pl.pallas_call(
        copy_kernel,
        out_shape=[shape(x.shape, x.dtype) for x in results],
        in_specs=[anywhere] * 4 + [vmem] * 2,
        out_specs=[anywhere] * 4 + [vmem] * 2,
        scratch_shapes=[pltpu.VMEM((4, tok, width), bf16), dma((2, 4, 2))],
    )(*results)
    return gq, gk, gv, filter_grad, taps_grad, skip_grad.reshape(own)


def body(query_proj, key_proj, value_proj, cotangent, boundary, short_taps, skip_gain, long_filter):
    pairs, tok, width = query_proj.shape
    parts = lax.axis_size("seq")
    seq_len = tok * parts
    scale = 1.0 / math.sqrt(pairs * lax.axis_size("dp") * seq_len)
    tables = build_tables(seq_len)
    filter_cols = lax.all_to_all(
        jnp.transpose(long_filter), "seq", split_axis=0, concat_axis=1, tiled=True
    ).astype(jnp.float32)
    filt_spec = forward_half(filter_cols, tables)
    taps = short_taps[:, :, None, None, :]
    raw = jnp.stack((query_proj, key_proj, value_proj))
    tails = passed_along(raw[:, :, tok - 2 :], "seq", 1)
    extended = jnp.concatenate((tails, raw), axis=2).astype(jnp.float32)
    conv = (
        taps[:, 0] * extended[:, :, 2:]
        + taps[:, 1] * extended[:, :, 1:-1]
        + taps[:, 2] * extended[:, :, :-2]
    )
    gated = conv[1] * conv[2]
    position = lax.axis_index("seq") * tok + jnp.arange(tok, dtype=jnp.int32)
    mask = (position[None, :] >= boundary[:, None]).astype(jnp.float32)
    dout = cotangent.astype(jnp.float32) * mask[:, :, None]
    dmix = dout * conv[0]
    gated_cols = lax.all_to_all(
        jnp.transpose(gated, (0, 2, 1)), "seq", split_axis=1, concat_axis=2, tiled=True
    )
    spectra = forward_half(gated_cols[0], tables)
    conv_cols = jnp.stack([convolve_cols(spectra, filt_spec, tables)])
    conv_rows = lax.all_to_all(conv_cols, "seq", split_axis=2, concat_axis=1, tiled=True)
    dmix_cols = lax.all_to_all(
        jnp.transpose(dmix, (0, 2, 1)), "seq", split_axis=1, concat_axis=2, tiled=True
    )
    back_cols, filt_part = correlate_cols(spectra, filt_spec, dmix_cols[0], tables)
    back_list = [back_cols]
    filt_list = [filt_part]
    back_rows = lax.all_to_all(jnp.stack(back_list), "seq", split_axis=2, concat_axis=1, tiled=True)
    mixed = jnp.transpose(conv_rows, (0, 2, 1)) + skip_gain * gated
    filter_part = jnp.sum(jnp.stack(filt_list), axis=0) * scale
    filter_total = lax.psum(filter_part, "dp")
    filter_rows = lax.all_to_all(
        filter_total.astype(jnp.bfloat16), "seq", split_axis=1, concat_axis=0, tiled=True
    )
    filter_grad = jnp.transpose(filter_rows)
    dgated = jnp.transpose(back_rows, (0, 2, 1)) + skip_gain * dmix
    upstream = jnp.stack((dout * mixed, dgated * conv[2], dgated * conv[1]))
    heads = passed_along(upstream[:, :, :2], "seq", -1)
    grad_ext = jnp.concatenate((upstream, heads), axis=2)
    grads = (
        taps[:, 0] * grad_ext[:, :, :tok]
        + taps[:, 1] * grad_ext[:, :, 1 : tok + 1]
        + taps[:, 2] * grad_ext[:, :, 2:]
    )
    grads = grads.astype(jnp.bfloat16)
    taps_part = (
        jnp.stack(
            [
                jnp.sum(upstream * extended[:, :, 2 - lag : 2 - lag + tok], axis=(1, 2))
                for lag in range(3)
            ],
            axis=1,
        )
        * scale
    )
    skip_part = jnp.sum(dmix * gated, axis=(0, 1)) * scale
    taps_local, skip_local = (
        lax.psum_scatter(taps_part, "seq", scatter_dimension=2, tiled=True),
        lax.psum_scatter(skip_part, "seq", scatter_dimension=0, tiled=True),
    )
    taps_grad, skip_grad = lax.psum((taps_local, skip_local), "dp")
    return (grads[0], grads[1], grads[2], filter_grad, taps_grad, skip_grad)


def solution(mesh):
    in_specs = (
        P(("groups", "dp"), "seq", None),
        P(("groups", "dp"), "seq", None),
        P(("groups", "dp"), "seq", None),
        P(("groups", "dp"), "seq", None),
        P(("groups", "dp")),
        P(),
        P(),
        P("seq", None),
    )
    out_specs = (
        P(("groups", "dp"), "seq", None),
        P(("groups", "dp"), "seq", None),
        P(("groups", "dp"), "seq", None),
        P(("groups", "seq"), None),
        P("groups", None, "seq"),
        P(("groups", "seq")),
    )
    def chosen(query_proj, *rest):
        pairs, tok, _ = query_proj.shape
        dense = pairs == 1 and mesh.shape["seq"] == 8 and mesh.shape["dp"] == mesh.shape["groups"] == 2 and tok * mesh.shape["seq"] <= DENSE_LIMIT
        return (dense_body if dense else body)(query_proj, *rest)

    return jax.shard_map(chosen, mesh=mesh, in_specs=in_specs, out_specs=out_specs, check_vma=False)
```

```python
import functools
import math

import jax
import jax.numpy as jnp
import numpy as np
from jax import lax
from jax.experimental import pallas as pl
from jax.experimental.pallas import tpu as pltpu
from jax.sharding import PartitionSpec as P

DENSE_LIMIT = 1024
LANES = 128
CODES = 32767.0
MESH = pl.DeviceIdType.MESH


def passed_along(value, axis, by):
    count = lax.axis_size(axis)
    pairs = [(i, i + by) for i in range(count) if 0 <= i + by < count]
    return lax.ppermute(value, axis, pairs)


def matmul_high(form, left, right):
    return jnp.einsum(
        form, left, right, precision=lax.Precision.HIGHEST, preferred_element_type=jnp.float32
    )


def dot_high(left, right):
    return jnp.dot(left, right, precision=lax.Precision.HIGHEST, preferred_element_type=jnp.float32)


def angle_table(left, right, period):
    phase = (left[:, None] * right[None, :] % period).astype(jnp.float32) * (2.0 * math.pi / period)
    return (jnp.cos(phase), jnp.sin(phase))


def build_tables(seq_len):
    cols = min(128, seq_len)
    rows = 2 * seq_len // cols
    half = rows // 2
    keep = half + 1
    col_index = jnp.arange(cols, dtype=jnp.int32)
    keep_index = jnp.arange(keep, dtype=jnp.int32)
    half_index = jnp.arange(half, dtype=jnp.int32)
    col_cos, col_sin = angle_table(col_index, col_index, cols)
    first_cos, first_sin = angle_table(keep_index, half_index, rows)
    first = jnp.stack((first_cos, -first_sin))
    twist_cos, twist_sin = angle_table(keep_index, col_index, 2 * seq_len)
    twist_cos = twist_cos[:, None, :]
    twist_sin = twist_sin[:, None, :]
    fwd_real = jnp.concatenate((col_cos, -col_sin), axis=1)
    fwd_imag = jnp.concatenate((col_sin, col_cos), axis=1)
    inv_real = jnp.concatenate((col_cos, col_sin), axis=1)
    inv_imag = jnp.concatenate((-col_sin, col_cos), axis=1)
    edge = (keep_index == 0) | (keep_index == half)
    weights = jnp.where(edge, 1.0, 2.0).astype(jnp.float32) / (2.0 * seq_len)
    last_cos, last_sin = angle_table(half_index, keep_index, rows)
    last_cos = last_cos * weights[None, :]
    last_sin = last_sin * weights[None, :]
    return (first, twist_cos, twist_sin, fwd_real, fwd_imag, inv_real, inv_imag, last_cos, last_sin)


def forward_half(signal, tables):
    first, twist_cos, twist_sin, fwd_real, fwd_imag = tables[:5]
    width_c, length = signal.shape
    cols = fwd_real.shape[0]
    grid = jnp.transpose(signal.reshape(width_c, length // cols, cols), (1, 0, 2))
    partial_dft = matmul_high("pkn,nca->pkca", first, grid)
    turned_re = partial_dft[0] * twist_cos + partial_dft[1] * twist_sin
    turned_im = partial_dft[1] * twist_cos - partial_dft[0] * twist_sin
    keep = partial_dft.shape[1]
    spec = dot_high(turned_re.reshape(-1, cols), fwd_real) + dot_high(
        turned_im.reshape(-1, cols), fwd_imag
    )
    spec = spec.reshape(keep, width_c, 2, cols)
    return (spec[:, :, 0], spec[:, :, 1])


def inverse_half(spec_re, spec_im, tables):
    twist_cos, twist_sin = (tables[1], tables[2])
    inv_real, inv_imag, last_cos, last_sin = tables[5:]
    keep, width_c, cols = spec_re.shape
    wide = dot_high(spec_re.reshape(-1, cols), inv_real) + dot_high(
        spec_im.reshape(-1, cols), inv_imag
    )
    wide = wide.reshape(keep, width_c, 2, cols)
    wide_re = wide[:, :, 0]
    wide_im = wide[:, :, 1]
    turned_re = wide_re * twist_cos - wide_im * twist_sin
    turned_im = wide_im * twist_cos + wide_re * twist_sin
    grid = matmul_high("nk,kca->nca", last_cos, turned_re) - matmul_high(
        "nk,kca->nca", last_sin, turned_im
    )
    return jnp.transpose(grid, (1, 0, 2)).reshape(width_c, -1)


def convolve_cols(gated_spec, filt_spec, tables):
    gated_re, gated_im = gated_spec
    filt_re, filt_im = filt_spec
    return inverse_half(
        gated_re * filt_re - gated_im * filt_im, gated_re * filt_im + gated_im * filt_re, tables
    )


def correlate_cols(gated_spec, filt_spec, dmix_cols, tables):
    gated_re, gated_im = gated_spec
    filt_re, filt_im = filt_spec
    grad_re, grad_im = forward_half(dmix_cols, tables)
    back = inverse_half(
        filt_re * grad_re + filt_im * grad_im, filt_re * grad_im - filt_im * grad_re, tables
    )
    filt_part = inverse_half(
        grad_re * gated_re + grad_im * gated_im, grad_im * gated_re - grad_re * gated_im, tables
    )
    return (back, filt_part)


def phase_tables(n):
    index = 4 * np.arange(n, dtype=np.int64) + 1
    unit = 2.0 * np.pi / (16 * n)
    fine = (index[:, None] * index[None, :LANES] % (16 * n)) * unit
    coarse = (index[:, None] * (4 * LANES * np.arange(n // LANES))[None, :] % (16 * n)) * unit
    turn = index[:, None] * unit
    pack = lambda x: np.stack((np.cos(x), np.sin(x))).astype(np.float32)
    return pack(fine), pack(np.concatenate((coarse, turn), axis=1))


def split_to(ref, lead, rows, value, cols=slice(None)):
    high = value.astype(jnp.bfloat16)
    ref[(*lead, 0, rows, cols)] = high
    ref[(*lead, 1, rows, cols)] = (value - high.astype(jnp.float32)).astype(jnp.bfloat16)


def dot(left, right):
    return jnp.dot(left, right, preferred_element_type=jnp.float32)


def dot3(high, low, ref, lead, cols=slice(None)):
    top = ref[(*lead, 0, slice(None), cols)]
    return dot(high, top) + (dot(high, ref[(*lead, 1, slice(None), cols)]) + dot(low, top))


def coded(value, top):
    return jnp.round(value * (CODES / jnp.maximum(top, 1e-30))).astype(jnp.int32).astype(jnp.int16)


def decoded(code, step):
    return code.astype(jnp.int32).astype(jnp.float32) * step


def operator_kernel(
    parts, scale, bound, q_in, k_in, v_in, c_in, h_in, taps_in, skip_in, fine, coarse,
    gq_out, gk_out, gv_out, f_out, taps_out, skip_out,
    loc, tails, heads, tails_in, heads_in, short_out, dout, codes, tops, codes_in, tops_in,
    hb, cosines, sines, gd, raw, spec, hspec, kspec, back, edges, back_in, edges_in, cross_in,
    filt, fsend, fother, ftotal, fown, fcode, fcode_in, ftop, ftop_in, stage, sums, sums_in, total, other,
    send_sem, recv_sem, local_sem, dp_send, dp_recv, halo_send, halo_recv,
):
    tok, channels = loc.shape[1:]
    team = parts // 2
    n = tok * team
    width = channels // team
    half = width // 2
    share = channels // parts
    rows = 32
    block = min(256, n)
    span = block // tok
    me = lax.axis_index("seq")
    core = lax.axis_index("dp")
    group = lax.axis_index("groups")
    side = me // team
    rank = lax.rem(me, team)
    low = side == 0
    high = side == 1
    sign = jnp.where(low, 1.0, -1.0).astype(jnp.float32)
    last = me == parts - 1
    seam = me == team - 1
    partner = {"dp": 1 - core}
    twin = {"groups": 1 - group}
    group_rows = pl.ds(pl.multiple_of(group * (tok // 2), tok // 2), tok // 2)
    f32, bf16 = jnp.float32, jnp.bfloat16
    my_half = pl.ds(pl.multiple_of(core * half, half), half)
    other_half = pl.ds(pl.multiple_of((1 - core) * half, half), half)
    teams, peers = range(1, team), range(1, parts)

    def cols_of(owner):
        return pl.ds(pl.multiple_of(owner * width, width), width)

    def half_cols_of(owner):
        return pl.ds(pl.multiple_of(owner * width + core * half, half), half)

    def share_of(owner):
        return pl.ds(pl.multiple_of(owner * share, share), share)

    def rows_of(owner):
        return pl.ds(pl.multiple_of(owner * tok, tok), tok)

    mine, own_cols = rows_of(rank), cols_of(rank)

    def mate(s):
        return lax.rem(rank + s, team)

    loads = [
        pltpu.make_async_copy(x.at[0], loc.at[i], local_sem.at[i])
        for i, x in enumerate((q_in, k_in, v_in, c_in))
    ]
    for load in loads:
        load.start()

    barrier = pltpu.get_barrier_semaphore()
    for s in peers:
        device = {"seq": lax.rem(me + s, parts)}
        pl.semaphore_signal(barrier, inc=1, device_id=device, device_id_type=MESH)
    for device in (partner, twin):
        pl.semaphore_signal(barrier, inc=1, device_id=device, device_id_type=MESH)

    for load in loads:
        load.wait()
    for i in range(4):
        tails[2 * i : 2 * i + 2, :] = loc[i, tok - 16 :, :].astype(f32)[14:]
        heads[2 * i : 2 * i + 2, :] = loc[i, :16, :].astype(f32)[:2]

    pl.semaphore_wait(barrier, parts + 1)

    def remote(source, target, sems, device):
        return pltpu.make_async_remote_copy(
            src_ref=source,
            dst_ref=target,
            send_sem=sems[0],
            recv_sem=sems[1],
            device_id=device,
            device_id_type=MESH,
        )

    def to_seq(a, slot, device, source, target):
        return remote(source, target, (send_sem.at[a, slot], recv_sem.at[a, slot]), {"seq": device})

    def to_mate(a, s, source, target):
        return to_seq(a, s, side * team + mate(s), source, target)

    def across(a, s, source, target):
        return to_seq(a, team + s, (1 - side) * team + mate(s), source, target)

    def to_partner(i, source, target, device=partner):
        return remote(source, target, (dp_send.at[i], dp_recv.at[i]), device)

    def local(a, source, target):
        return pltpu.make_async_copy(source, target, local_sem.at[a])

    @pl.when(me == 0)
    def _():
        back_in[0, :, :] = jnp.zeros((tok, channels), jnp.int16)

    halos = [
        remote(x, y, (halo_send.at[i], halo_recv.at[i]), {"seq": lax.rem(me + by, parts)})
        for i, (x, y, by) in enumerate(((tails, tails_in, 1), (heads, heads_in, parts - 1)))
    ]
    for halo in halos:
        halo.start()

    h_target = hb.at[side, rank, group, :, my_half]
    h_own = local(4, h_in.at[group_rows, half_cols_of(rank)], h_target)
    h_moved = [
        to_mate(0, s, h_in.at[group_rows, half_cols_of(mate(s))], h_target) for s in teams
    ] + [
        across(0, s, h_in.at[group_rows, half_cols_of(mate(s))], h_target) for s in range(team)
    ]
    h_own.start()
    for copy in h_moved:
        copy.start()

    chunk = 128

    def at_cols(i):
        return pl.ds(pl.multiple_of(i * chunk, chunk), chunk)

    def extended(b, cols):
        before = jnp.where(me == 0, 0.0, pltpu.roll(tails_in[:, cols], 6 - 2 * b, 0))
        after = heads_in[:, cols]
        if b:
            after = pltpu.roll(after, 8 - 2 * b, 0)
        return before, loc[b, :, cols].astype(f32), after

    def lagged(b, cols, ahead):
        before, here, after = extended(b, cols)
        ext = jnp.concatenate((before, here, after) if ahead else (before, here), axis=0)
        return ext[8:], pltpu.roll(ext, 1, 0)[8:], pltpu.roll(ext, 2, 0)[8:]

    def short(b, lags, cols):
        tap = [taps_in[b, j : j + 1, cols] for j in range(3)]
        return tap[0] * lags[0] + tap[1] * lags[1] + tap[2] * lags[2]

    def encode(i, value, cols):
        top = jnp.max(jnp.abs(value), axis=0, keepdims=True)
        codes[i, :, cols] = coded(value, top)
        tops[i, 0:1, cols] = top * (1.0 / CODES)

    def make_gated(slot):
        @pl.loop(0, channels // chunk)
        def _(i):
            cols = at_cols(i)
            s1 = short(1, lagged(1, cols, True), cols)
            s2 = short(2, lagged(2, cols, True), cols)
            short_out[1, :, cols] = s1
            short_out[2, :, cols] = s2
            encode(slot, s1[:tok] * s2[:tok], cols)

    def make_dmix(slot):
        @pl.loop(0, channels // chunk)
        def _(i):
            cols = at_cols(i)
            _, here, after = extended(3, cols)
            ext = jnp.concatenate((here, after), axis=0)
            pos = me * tok + lax.broadcasted_iota(jnp.int32, (tok + 8, chunk), 0)
            masked = jnp.where((pos >= bound[0]) & (pos < parts * tok), ext, 0.0)
            dout[:, cols] = masked
            s0 = short(0, lagged(0, cols, True), cols)
            short_out[0, :, cols] = s0
            encode(slot, masked[:tok] * s0[:tok], cols)

    def tops_of(slot, to):
        def source(o):
            return tops.at[slot, 0:1, cols_of(o)]

        return local(5 + 2 * slot, source(rank), tops_in.at[to, rank, 0:1, :]), [
            to_mate(1 + 2 * slot, s, source(mate(s)), tops_in.at[to, rank, 0:1, :]) for s in teams
        ]

    def codes_of(slot, to):
        def source(o):
            return codes.at[slot, :, cols_of(o)]

        return local(6 + 2 * slot, source(rank), codes_in.at[to, mine, :]), [
            to_mate(2 + 2 * slot, s, source(mate(s)), codes_in.at[to, mine, :]) for s in teams
        ]

    def part_cols(k, owner):
        start = owner * width + (core if k else 1 - core) * half
        return pl.ds(pl.multiple_of(start, half), half)

    cross_tops = [
        across(1, s, tops.at[0, 0:1, cols_of(mate(s))], tops_in.at[2, rank, 0:1, :])
        for s in range(team)
    ]
    cross_codes = [
        [
            across(
                12 if k else 2, s,
                codes.at[0, :, part_cols(k, mate(s))], codes_in.at[2, mine, part_cols(k, 0)],
            )
            for s in range(team)
        ]
        for k in range(2)
    ]

    for halo in halos:
        halo.wait_recv()
    pl.when(low)(lambda: make_gated(0))
    pl.when(high)(lambda: make_dmix(0))
    first_tops, first_codes = tops_of(0, 0), codes_of(0, 0)
    for copy in (*first_tops[1], *cross_tops):
        copy.start()
    for copy in (*first_codes[1], *cross_codes[0]):
        copy.start()
    first_tops[0].start()
    first_codes[0].start()

    h_own.wait()
    for copy in h_moved:
        copy.wait_recv()
    h_quarter = hb.at[:, :, group, :, my_half]
    h_twin = to_partner(1, h_quarter, h_quarter, twin)
    h_twin.start()

    pl.when(low)(lambda: make_dmix(1))
    pl.when(high)(lambda: make_gated(1))
    second_tops, second_codes = tops_of(1, 1), codes_of(1, 1)
    second = (*second_tops[1], *second_codes[1])

    @pl.when(me > 0)
    def _():
        for copy in (*second, second_tops[0], second_codes[0]):
            copy.start()

    h_twin.wait_recv()
    h_relay = to_partner(0, hb.at[:, :, :, :, my_half], hb.at[:, :, :, :, my_half])
    h_relay.start()

    @pl.loop(0, n // rows)
    def _(i):
        at = pl.ds(pl.multiple_of(i * rows, rows), rows)
        fr, fi = fine[0, at, :], fine[1, at, :]
        cr, ci = coarse[0, at, :], coarse[1, at, :]
        for a in range(n // LANES):
            ar, ai = cr[:, a : a + 1], ci[:, a : a + 1]
            cols = slice(a * LANES, (a + 1) * LANES)
            split_to(cosines, (), at, fr * ar - fi * ai, cols)
            split_to(sines, (), at, fr * ai + fi * ar, cols)

    def at_rows(i):
        return pl.ds(pl.multiple_of(i * rows, rows), rows)

    def at_block(j):
        return pl.ds(pl.multiple_of(j * block, block), block)

    def blocks(table, at):
        return table[0, at, :], table[1, at, :]

    every = pl.ds(0, width)

    def inverse(b, at, cols=every):
        ch, cl = blocks(cosines, at)
        sh, sl = blocks(sines, at)
        return dot3(ch, cl, spec, (b, 0), cols) - dot3(sh, sl, spec, (b, 1), cols)

    def turned(at, re, im):
        end = coarse.shape[2] - 1
        tr, ti = coarse[0, at, end:], coarse[1, at, end:]
        return re * tr - im * ti, re * ti + im * tr

    def forward(i, at, cols=every):
        ch, cl = blocks(cosines, at)
        sh, sl = blocks(sines, at)
        return dot3(ch, cl, gd, (i,), cols), -dot3(sh, sl, gd, (i,), cols)

    def decode(i, cols=every):
        @pl.loop(0, n // rows)
        def _(r):
            at = at_rows(r)
            step = tops_in[i, r // (tok // rows), 0:1, cols]
            split_to(gd, (i,), at, decoded(codes_in[i, at, cols], step), cols)

    def product_to(i, at, re, im, cols=every):
        split_to(spec, (i, 0), at, re, cols)
        split_to(spec, (i, 1), at, im, cols)

    h_relay.wait_recv()

    @pl.loop(0, n // block)
    def _(j):
        at = at_block(j)
        ch, cl = blocks(cosines, at)
        sh, sl = blocks(sines, at)
        near, far = hb[0].reshape(n, width), hb[1].reshape(n, width)
        nr, ni = turned(at, dot(ch, near) + dot(cl, near), -(dot(sh, near) + dot(sl, near)))
        fr, fi = turned(at, dot(ch, far) + dot(cl, far), -(dot(sh, far) + dot(sl, far)))
        hspec[0, at, :], hspec[1, at, :] = nr, ni * sign
        kspec[0, at, :], kspec[1, at, :] = fr - ni, (fi + nr) * sign

    for own, moved in (first_tops, first_codes):
        own.wait()
        for copy in moved:
            copy.wait_recv()
    for copy in cross_codes[1]:
        copy.start()
    decode(0)

    @pl.loop(0, n // block)
    def _(j):
        at = at_block(j)
        hr, hi = hspec[0, at, :], hspec[1, at, :]
        re, im = forward(0, at)
        raw[0, 0, at, :], raw[0, 1, at, :] = re, im
        product_to(0, at, re * hr - im * hi, re * hi + im * hr)

    def src_cols(p):
        return part_cols(p - 1, 0) if p else every

    def dst_cols(p):
        return part_cols(p - 1, rank) if p else own_cols

    data_row, edge_row, own_sem = (5, 7, 13), (6, 8, 14), (9, 11, 19)

    def back_to(p, s, dest):
        i = min(p, 1)
        return to_seq(
            data_row[p], s, side * team + dest,
            back.at[i, rows_of(dest), src_cols(p)], back_in.at[i, :, dst_cols(p)],
        )

    def back_copy(p, s):
        return back_to(p, s, mate(s))

    def edge_copy(p, s):
        i = min(p, 1)
        source = edges.at[i, mate(s), 0:3, src_cols(p)]
        return to_mate(edge_row[p], s, source, edges_in.at[i, 0:3, dst_cols(p)])

    def cross_edge(p, slot, device):
        i = min(p, 1)
        source = edges.at[i, team - 1, 1:3, src_cols(p)]
        return to_seq(edge_row[p], team + slot, device, source, cross_in.at[i, 0:2, dst_cols(p)])

    def cross_copy(p):
        return cross_edge(p, lax.rem(2 * team - 1 - rank, team), team - 1)

    def back_own(p):
        i = min(p, 1)
        return (
            local(own_sem[p], back.at[i, mine, src_cols(p)], back_in.at[i, :, dst_cols(p)]),
            local(
                own_sem[p] + 1,
                edges.at[i, rank, 0:3, src_cols(p)], edges_in.at[i, 0:3, dst_cols(p)],
            ),
        )

    def send_back(p):
        i = min(p, 1)
        cols = src_cols(p)
        steps = n // block

        @pl.loop(0, steps)
        def _(r):
            j = lax.rem(rank // span + 1 + r, steps)
            value = inverse(i, at_block(j), cols) * (1.0 / n)
            for e in range(span):
                dest = j * span + e
                piece = value[e * tok : (e + 1) * tok]
                top = jnp.max(jnp.abs(piece), axis=0, keepdims=True)
                back[i, rows_of(dest), cols] = coded(piece, top)
                edges[i, dest, 0:1, cols] = top * (1.0 / CODES)
                edges[i, lax.rem(dest + team - 1, team), 1:3, cols] = piece[:2]
            for e in range(span):
                dest = j * span + e
                wanted = dest != rank
                if p == 0:
                    wanted = wanted & (side * team + dest != 0)

                @pl.when(wanted)
                def _():
                    back_to(p, lax.rem(dest + team - rank, team), dest).start()

        for s in teams:
            edge_copy(p, s).start()
        for copy in back_own(p):
            copy.start()

        @pl.when(high)
        def _():
            cross_copy(p).start()

    def back_arrived(p):
        for copy in back_own(p):
            copy.wait()
        for s in teams:
            edge_copy(p, s).wait_recv()
            if p:
                back_copy(p, s).wait_recv()
            else:
                pl.when(me > 0)(back_copy(p, s).wait_recv)

    def cross_arrived(p):
        @pl.when(seam)
        def _():
            for s in range(team):
                cross_edge(p, s, lax.rem(me + team, parts)).wait_recv()

    def back_sent(p):
        for s in teams:
            edge_copy(p, s).wait_send()
            if p:
                back_copy(p, s).wait_send()
            else:
                pl.when(side * team + mate(s) != 0)(back_copy(p, s).wait_send)

        @pl.when(high)
        def _():
            cross_copy(p).wait_send()

    send_back(0)

    @pl.when(me > 0)
    def _():
        second_tops[0].wait()
        second_codes[0].wait()

    for s in teams:
        source = side * team + lax.rem(rank + team - s, team)

        @pl.when(source != 0)
        def _(s=s):
            second_tops[1][s - 1].wait_recv()
            second_codes[1][s - 1].wait_recv()

    @pl.when(low)
    def _():
        codes_in[1, 0:tok, :] = jnp.zeros((tok, width), jnp.int16)
        tops_in[1, 0, 0:1, :] = jnp.zeros((1, width), f32)

    decode(1)

    @pl.when(low)
    def _():
        @pl.loop(0, n // block)
        def _(j):
            at = at_block(j)
            raw[1, 0, at, :], raw[1, 1, at, :] = forward(1, at)

    f_part = to_partner(2, filt.at[:, :, other_half], fother.at[0])
    f_ends = [
        to_seq(9, team + 1, rank + team * (1 - side), ftop.at[0:1, :], ftop_in.at[0:1, :]),
        to_seq(9, team, rank + team * (1 - side), fcode, fcode_in),
    ]

    @pl.when(high)
    def _():
        @pl.loop(0, n // block)
        def _(j):
            at = at_block(j)
            re, im = forward(1, at)
            raw[1, 0, at, :], raw[1, 1, at, :] = re, im
            gr, gi = turned(at, re, im)
            dr, di = raw[0, 0, at, :], raw[0, 1, at, :]
            filt[0, at, :] = gr * dr + gi * di
            filt[1, at, :] = gr * di - gi * dr

        f_part.start()

    @pl.when(high)
    def _():
        f_part.wait_recv()

        @pl.loop(0, n // block)
        def _(j):
            at = at_block(j)
            re = filt[0, at, my_half] + fother[0, 0, at, :]
            product_to(2, at, re, filt[1, at, my_half] + fother[0, 1, at, :], my_half)

        @pl.loop(0, n // block)
        def _(j):
            at = at_block(j)
            ftotal[at, :] = inverse(2, at, my_half) * (scale / n)

        part = ftotal[...]
        top = jnp.max(jnp.abs(part), axis=0, keepdims=True)
        fcode[...] = coded(part, top)
        ftop[0:1, :] = top * (1.0 / CODES)
        for copy in f_ends:
            copy.start()

    def second_stage(at, cols):
        cr, ci = forward(2, at, cols)
        hr, hi = hspec[0, at, cols], hspec[1, at, cols]
        kr, ki = kspec[0, at, cols], kspec[1, at, cols]
        sr, si = raw[1, 0, at, cols], raw[1, 1, at, cols]
        re = hr * sr + hi * si + (kr * cr + ki * ci)
        im = hr * si - hi * sr + (kr * ci - ki * cr)
        product_to(1, at, re, im, cols)
        return cr, ci, sr, si

    f_add = to_partner(3, fsend, fother.at[1])
    def filter_to(k, at, re, im):
        if k:
            product_to(2, at, re + fother[1, 0, at, :], im + fother[1, 1, at, :], my_half)
        else:
            fsend[0, at, :], fsend[1, at, :] = re, im

    for copy in cross_tops:
        copy.wait_recv()
    for k in range(2):
        cols = part_cols(k, 0)
        for copy in cross_codes[k]:
            copy.wait_recv()
        decode(2, cols)
        if k:
            f_add.wait_recv()

        @pl.when(low)
        def _():
            @pl.loop(0, n // block)
            def _(j):
                at = at_block(j)
                cr, ci, sr, si = second_stage(at, cols)
                gr, gi = turned(at, raw[0, 0, at, cols], raw[0, 1, at, cols])
                dr, di = sr + ci, si - cr
                filter_to(k, at, gr * dr + gi * di, gr * di - gi * dr)

        @pl.when(high)
        def _():
            @pl.loop(0, n // block)
            def _(j):
                at = at_block(j)
                cr, ci, _, _ = second_stage(at, cols)
                gr, gi = turned(at, cr, ci)
                dr, di = raw[0, 0, at, cols], raw[0, 1, at, cols]
                filter_to(k, at, gr * dr + gi * di, gr * di - gi * dr)

        if k == 0:
            f_add.start()
        send_back(1 + k)

    @pl.loop(0, n // block)
    def _(j):
        at = at_block(j)
        ftotal[at, :] = inverse(2, at, my_half) * (scale / n)

    @pl.when(low)
    def _():
        for copy in f_ends:
            copy.wait_recv()
        fown[...] = (ftotal[...] + decoded(fcode_in[...], ftop_in[0:1, :])).astype(bf16)

    @pl.when(high)
    def _():
        fown[...] = ftotal[...].astype(bf16)

    f_target = f_out.at[:, half_cols_of(rank)]
    f_own = local(13, fown.at[mine, :], f_target)
    f_moved = [to_mate(9, s, fown.at[rows_of(mate(s)), :], f_target) for s in teams]
    own_relay = to_partner(4, fown.at[mine, :], f_target)
    for copy in (*f_moved, f_own, own_relay):
        copy.start()

    def finish(b, d, cols, row=0):
        tap = [taps_in[b, j : j + 1, cols] for j in range(3)]
        count = tok - row
        ahead = [pltpu.roll(d, d.shape[0] - by, 0)[:count] for by in (1, 2)]
        grad = tap[0] * d[:count] + tap[1] * ahead[0] + tap[2] * ahead[1]
        stage[b, row:, cols] = grad.astype(bf16)

    def total_of(value):
        return jnp.sum(jnp.sum(value.reshape(tok // 8, 8, chunk), axis=0), axis=0, keepdims=True)

    def add_taps(r, b, d, cols):
        lags = lagged(b, cols, False)
        for j in range(3):
            row = r + j
            sums[row // 8, row % 8 : row % 8 + 1, cols] = total_of(d[:tok] * lags[j])

    def returned(i, cols, row, crossed):
        here = decoded(back_in[i, row:, cols], edges_in[i, 0:1, cols])
        edge = pltpu.roll(edges_in[i, :, cols], 7, 0)
        if crossed:
            edge = jnp.where(seam, cross_in[1 - i, :, cols], edge)
        return jnp.concatenate((here, jnp.where(last, 0.0, edge)), axis=0)

    counts = (4, 6)

    def sum_own(r):
        return local(
            14 + r, sums.at[r, 0 : counts[r], share_of(me)], sums_in.at[me, r, 0 : counts[r], :]
        )

    def sum_copy(r, s):
        peer = lax.rem(me + s, parts)
        source = sums.at[r, 0 : counts[r], share_of(peer)]
        return to_seq(10 + r, s, peer, source, sums_in.at[me, r, 0 : counts[r], :])

    outs = [
        local(16 + b, stage.at[b], out.at[0]) for b, out in enumerate((gq_out, gk_out, gv_out))
    ]

    def over_cols(p, work):
        if p == 0:
            pl.loop(0, channels // chunk)(lambda i: work(at_cols(i)))
        else:
            per = half // chunk

            @pl.loop(0, team * per)
            def _(i):
                owner, c = i // per, lax.rem(i, per)
                start = owner * width + (core if p == 2 else 1 - core) * half + c * chunk
                work(pl.ds(pl.multiple_of(start, chunk), chunk))

    def query_signal(cols, row, crossed):
        gated = short_out[1, row:, cols] * short_out[2, row:, cols]
        dmask = dout[row:, cols]
        return gated, dmask, dmask * (returned(side, cols, row, crossed) + skip_in[:, cols] * gated)

    def finish_query(cols):
        gated, dmask, d = query_signal(cols, 0, False)
        finish(0, d, cols)
        add_taps(0, 0, d, cols)
        dmix = dmask * short_out[0, :, cols]
        sums[0, 3:4, cols] = total_of((dmix * gated)[:tok])

    def finish_rest(cols):
        dmix = dout[:, cols] * short_out[0, :, cols]
        dg = returned(1 - side, cols, 0, True) + skip_in[:, cols] * dmix
        d1 = dg * short_out[2, :, cols]
        finish(1, d1, cols)
        add_taps(8, 1, d1, cols)
        d2 = dg * short_out[1, :, cols]
        finish(2, d2, cols)
        add_taps(11, 2, d2, cols)

    def send_sums(r):
        sum_own(r).start()
        for s in peers:
            sum_copy(r, s).start()

    back_arrived(0)
    cross_arrived(0)

    @pl.when(low)
    def _():
        over_cols(0, finish_query)
        send_sums(0)

    @pl.when(high)
    def _():
        over_cols(0, finish_rest)
        send_sums(1)

    for p in (1, 2):
        back_arrived(p)
        pl.when(low)(lambda: over_cols(p, finish_rest))
        pl.when(high)(lambda: over_cols(p, finish_query))

    pl.when(low)(lambda: send_sums(1))
    pl.when(high)(lambda: send_sums(0))
    cross_arrived(1)
    cross_arrived(2)

    @pl.when(seam)
    def _():
        def mend(cols):
            finish(0, query_signal(cols, tok - 16, True)[2], cols, tok - 16)

        over_cols(0, mend)

    for out in outs:
        out.start()

    relays = [own_relay]
    for s in teams:
        f_moved[s - 1].wait_recv()
        block_cols = half_cols_of(lax.rem(rank + team - s, team))
        relay = to_partner(4 + s, f_out.at[:, block_cols], f_out.at[:, block_cols])
        relay.start()
        relays.append(relay)

    for r in range(2):
        sum_own(r).wait()
        for s in peers:
            sum_copy(r, s).wait_recv()
        value = sums_in[0, r, 0 : counts[r], :]
        for p in range(1, parts):
            value = value + sums_in[p, r, 0 : counts[r], :]
        total[r, 0 : counts[r], :] = value * scale
    s_add = to_partner(4 + team, total, other)
    s_add.start()
    s_add.wait_recv()
    taps_out[0] = total[0, 0:3, :] + other[0, 0:3, :]
    skip_out[...] = total[0, 3:4, :] + other[0, 3:4, :]
    taps_out[1] = total[1, 0:3, :] + other[1, 0:3, :]
    taps_out[2] = total[1, 3:6, :] + other[1, 3:6, :]

    f_own.wait()
    for out in outs:
        out.wait()
    for relay in relays:
        relay.wait_recv()

    for copy in (*halos, *h_moved, *first_tops[1], *first_codes[1], *f_moved):
        copy.wait_send()
    for copy in (*cross_tops, *cross_codes[0], *cross_codes[1]):
        copy.wait_send()

    @pl.when(me > 0)
    def _():
        for copy in second:
            copy.wait_send()

    @pl.when(high)
    def _():
        f_part.wait_send()
        for copy in f_ends:
            copy.wait_send()

    for p in range(3):
        back_sent(p)
    for r in range(2):
        for s in peers:
            sum_copy(r, s).wait_send()
    for copy in (h_twin, h_relay, f_add, s_add, *relays):
        copy.wait_send()


def copy_kernel(*refs):
    held, sems = refs[-2:]
    reads, writes = [], []
    for i in range(4):
        source, target = refs[i], refs[6 + i]
        if i < 3:
            source, target = source.at[0], target.at[0]
        half = source.shape[0] // 2
        for j in range(2):
            rows = pl.ds(j * half, half)
            reads.append(pltpu.make_async_copy(source.at[rows, :], held.at[i, rows, :], sems.at[0, i, j]))
            writes.append(pltpu.make_async_copy(held.at[i, rows, :], target.at[rows, :], sems.at[1, i, j]))
    for read in reads:
        read.start()
    for i in (4, 5):
        refs[6 + i][...] = refs[i][...]
    for read, write in zip(reads, writes):
        read.wait()
        write.start()
    for write in writes:
        write.wait()


def dense_body(query_proj, key_proj, value_proj, cotangent, boundary, short_taps, skip_gain, long_filter):
    tok, width = query_proj.shape[1:]
    parts = lax.axis_size("seq")
    team = parts // 2
    n = tok * team
    own, wide = width // parts, width // team
    scale = 1.0 / math.sqrt(lax.axis_size("dp") * tok * parts)
    fine, coarse = phase_tables(n)
    vmem = pl.BlockSpec(memory_space=pltpu.VMEM)
    anywhere = pl.BlockSpec(memory_space=pl.ANY)
    f32, bf16, i16 = jnp.float32, jnp.bfloat16, jnp.int16
    shape = jax.ShapeDtypeStruct
    dma = pltpu.SemaphoreType.DMA
    results = pl.pallas_call(
        functools.partial(operator_kernel, parts, scale),
        out_shape=[shape((1, tok, width), bf16)] * 3
        + [shape((tok, width), bf16), shape((3, 3, own), f32), shape((1, own), f32)],
        in_specs=[pl.BlockSpec(memory_space=pltpu.SMEM)] + [anywhere] * 5 + [vmem] * 4,
        out_specs=[anywhere] * 4 + [vmem] * 2,
        scratch_shapes=[
            pltpu.VMEM((4, tok, width), bf16),
            pltpu.VMEM((8, width), f32),
            pltpu.VMEM((8, width), f32),
            pltpu.VMEM((8, width), f32),
            pltpu.VMEM((8, width), f32),
            pltpu.VMEM((3, tok + 8, width), f32),
            pltpu.VMEM((tok + 8, width), f32),
            pltpu.VMEM((2, tok, width), i16),
            pltpu.VMEM((2, 8, width), f32),
            pltpu.VMEM((3, n, wide), i16),
            pltpu.VMEM((3, team, 8, wide), f32),
            pltpu.VMEM((2, team, 2, tok // 2, wide), bf16),
            pltpu.VMEM((2, n, n), bf16),
            pltpu.VMEM((2, n, n), bf16),
            pltpu.VMEM((3, 2, n, wide), bf16),
            pltpu.VMEM((2, 2, n, wide), f32),
            pltpu.VMEM((3, 2, 2, n, wide), bf16),
            pltpu.VMEM((2, n, wide), f32),
            pltpu.VMEM((2, n, wide), f32),
            pltpu.VMEM((2, n, wide), i16),
            pltpu.VMEM((2, team, 8, wide), f32),
            pltpu.VMEM((2, tok, width), i16),
            pltpu.VMEM((2, 8, width), f32),
            pltpu.VMEM((2, 8, width), f32),
            pltpu.VMEM((2, n, wide), f32),
            pltpu.VMEM((2, n, wide // 2), f32),
            pltpu.VMEM((2, 2, n, wide // 2), f32),
            pltpu.VMEM((n, wide // 2), f32),
            pltpu.VMEM((n, wide // 2), bf16),
            pltpu.VMEM((n, wide // 2), i16),
            pltpu.VMEM((n, wide // 2), i16),
            pltpu.VMEM((8, wide // 2), f32),
            pltpu.VMEM((8, wide // 2), f32),
            pltpu.VMEM((3, tok, width), bf16),
            pltpu.VMEM((2, 8, width), f32),
            pltpu.VMEM((parts, 2, 8, own), f32),
            pltpu.VMEM((2, 8, own), f32),
            pltpu.VMEM((2, 8, own), f32),
            dma((15, parts)),
            dma((15, parts)),
            dma((21,)),
            dma((5 + team,)),
            dma((5 + team,)),
            dma((2,)),
            dma((2,)),
        ],
        compiler_params=pltpu.CompilerParams(
            collective_id=0, has_side_effects=True, vmem_limit_bytes=56 * 2**20
        ),
    )(
        boundary, query_proj, key_proj, value_proj, cotangent, long_filter,
        short_taps, skip_gain[None], jnp.asarray(fine), jnp.asarray(coarse),
    )
    gq, gk, gv, filter_grad, taps_grad, skip_grad = pl.pallas_call(
        copy_kernel,
        out_shape=[shape(x.shape, x.dtype) for x in results],
        in_specs=[anywhere] * 4 + [vmem] * 2,
        out_specs=[anywhere] * 4 + [vmem] * 2,
        scratch_shapes=[pltpu.VMEM((4, tok, width), bf16), dma((2, 4, 2))],
    )(*results)
    return gq, gk, gv, filter_grad, taps_grad, skip_grad.reshape(own)


def body(query_proj, key_proj, value_proj, cotangent, boundary, short_taps, skip_gain, long_filter):
    pairs, tok, width = query_proj.shape
    parts = lax.axis_size("seq")
    seq_len = tok * parts
    scale = 1.0 / math.sqrt(pairs * lax.axis_size("dp") * seq_len)
    tables = build_tables(seq_len)
    filter_cols = lax.all_to_all(
        jnp.transpose(long_filter), "seq", split_axis=0, concat_axis=1, tiled=True
    ).astype(jnp.float32)
    filt_spec = forward_half(filter_cols, tables)
    taps = short_taps[:, :, None, None, :]
    raw = jnp.stack((query_proj, key_proj, value_proj))
    tails = passed_along(raw[:, :, tok - 2 :], "seq", 1)
    extended = jnp.concatenate((tails, raw), axis=2).astype(jnp.float32)
    conv = (
        taps[:, 0] * extended[:, :, 2:]
        + taps[:, 1] * extended[:, :, 1:-1]
        + taps[:, 2] * extended[:, :, :-2]
    )
    gated = conv[1] * conv[2]
    position = lax.axis_index("seq") * tok + jnp.arange(tok, dtype=jnp.int32)
    mask = (position[None, :] >= boundary[:, None]).astype(jnp.float32)
    dout = cotangent.astype(jnp.float32) * mask[:, :, None]
    dmix = dout * conv[0]
    gated_cols = lax.all_to_all(
        jnp.transpose(gated, (0, 2, 1)), "seq", split_axis=1, concat_axis=2, tiled=True
    )
    spectra = forward_half(gated_cols[0], tables)
    conv_cols = jnp.stack([convolve_cols(spectra, filt_spec, tables)])
    conv_rows = lax.all_to_all(conv_cols, "seq", split_axis=2, concat_axis=1, tiled=True)
    dmix_cols = lax.all_to_all(
        jnp.transpose(dmix, (0, 2, 1)), "seq", split_axis=1, concat_axis=2, tiled=True
    )
    back_cols, filt_part = correlate_cols(spectra, filt_spec, dmix_cols[0], tables)
    back_list = [back_cols]
    filt_list = [filt_part]
    back_rows = lax.all_to_all(jnp.stack(back_list), "seq", split_axis=2, concat_axis=1, tiled=True)
    mixed = jnp.transpose(conv_rows, (0, 2, 1)) + skip_gain * gated
    filter_part = jnp.sum(jnp.stack(filt_list), axis=0) * scale
    filter_total = lax.psum(filter_part, "dp")
    filter_rows = lax.all_to_all(
        filter_total.astype(jnp.bfloat16), "seq", split_axis=1, concat_axis=0, tiled=True
    )
    filter_grad = jnp.transpose(filter_rows)
    dgated = jnp.transpose(back_rows, (0, 2, 1)) + skip_gain * dmix
    upstream = jnp.stack((dout * mixed, dgated * conv[2], dgated * conv[1]))
    heads = passed_along(upstream[:, :, :2], "seq", -1)
    grad_ext = jnp.concatenate((upstream, heads), axis=2)
    grads = (
        taps[:, 0] * grad_ext[:, :, :tok]
        + taps[:, 1] * grad_ext[:, :, 1 : tok + 1]
        + taps[:, 2] * grad_ext[:, :, 2:]
    )
    grads = grads.astype(jnp.bfloat16)
    taps_part = (
        jnp.stack(
            [
                jnp.sum(upstream * extended[:, :, 2 - lag : 2 - lag + tok], axis=(1, 2))
                for lag in range(3)
            ],
            axis=1,
        )
        * scale
    )
    skip_part = jnp.sum(dmix * gated, axis=(0, 1)) * scale
    taps_local, skip_local = (
        lax.psum_scatter(taps_part, "seq", scatter_dimension=2, tiled=True),
        lax.psum_scatter(skip_part, "seq", scatter_dimension=0, tiled=True),
    )
    taps_grad, skip_grad = lax.psum((taps_local, skip_local), "dp")
    return (grads[0], grads[1], grads[2], filter_grad, taps_grad, skip_grad)


def solution(mesh):
    in_specs = (
        P(("groups", "dp"), "seq", None),
        P(("groups", "dp"), "seq", None),
        P(("groups", "dp"), "seq", None),
        P(("groups", "dp"), "seq", None),
        P(("groups", "dp")),
        P(),
        P(),
        P("seq", None),
    )
    out_specs = (
        P(("groups", "dp"), "seq", None),
        P(("groups", "dp"), "seq", None),
        P(("groups", "dp"), "seq", None),
        P(("groups", "seq"), None),
        P("groups", None, "seq"),
        P(("groups", "seq")),
    )
    def chosen(query_proj, *rest):
        pairs, tok, _ = query_proj.shape
        dense = pairs == 1 and mesh.shape["seq"] == 8 and mesh.shape["dp"] == mesh.shape["groups"] == 2 and tok * mesh.shape["seq"] <= DENSE_LIMIT
        return (dense_body if dense else body)(query_proj, *rest)

    return jax.shard_map(chosen, mesh=mesh, in_specs=in_specs, out_specs=out_specs, check_vma=False)
```

```python
import functools
import math

import jax
import jax.numpy as jnp
import numpy as np
from jax import lax
from jax.experimental import pallas as pl
from jax.experimental.pallas import tpu as pltpu
from jax.sharding import PartitionSpec as P

DENSE_LIMIT = 1024
LANES = 128
CODES = 32767.0
MESH = pl.DeviceIdType.MESH


def passed_along(value, axis, by):
    count = lax.axis_size(axis)
    pairs = [(i, i + by) for i in range(count) if 0 <= i + by < count]
    return lax.ppermute(value, axis, pairs)


def matmul_high(form, left, right):
    return jnp.einsum(
        form, left, right, precision=lax.Precision.HIGHEST, preferred_element_type=jnp.float32
    )


def dot_high(left, right):
    return jnp.dot(left, right, precision=lax.Precision.HIGHEST, preferred_element_type=jnp.float32)


def angle_table(left, right, period):
    phase = (left[:, None] * right[None, :] % period).astype(jnp.float32) * (2.0 * math.pi / period)
    return (jnp.cos(phase), jnp.sin(phase))


def build_tables(seq_len):
    cols = min(128, seq_len)
    rows = 2 * seq_len // cols
    half = rows // 2
    keep = half + 1
    col_index = jnp.arange(cols, dtype=jnp.int32)
    keep_index = jnp.arange(keep, dtype=jnp.int32)
    half_index = jnp.arange(half, dtype=jnp.int32)
    col_cos, col_sin = angle_table(col_index, col_index, cols)
    first_cos, first_sin = angle_table(keep_index, half_index, rows)
    first = jnp.stack((first_cos, -first_sin))
    twist_cos, twist_sin = angle_table(keep_index, col_index, 2 * seq_len)
    twist_cos = twist_cos[:, None, :]
    twist_sin = twist_sin[:, None, :]
    fwd_real = jnp.concatenate((col_cos, -col_sin), axis=1)
    fwd_imag = jnp.concatenate((col_sin, col_cos), axis=1)
    inv_real = jnp.concatenate((col_cos, col_sin), axis=1)
    inv_imag = jnp.concatenate((-col_sin, col_cos), axis=1)
    edge = (keep_index == 0) | (keep_index == half)
    weights = jnp.where(edge, 1.0, 2.0).astype(jnp.float32) / (2.0 * seq_len)
    last_cos, last_sin = angle_table(half_index, keep_index, rows)
    last_cos = last_cos * weights[None, :]
    last_sin = last_sin * weights[None, :]
    return (first, twist_cos, twist_sin, fwd_real, fwd_imag, inv_real, inv_imag, last_cos, last_sin)


def forward_half(signal, tables):
    first, twist_cos, twist_sin, fwd_real, fwd_imag = tables[:5]
    width_c, length = signal.shape
    cols = fwd_real.shape[0]
    grid = jnp.transpose(signal.reshape(width_c, length // cols, cols), (1, 0, 2))
    partial_dft = matmul_high("pkn,nca->pkca", first, grid)
    turned_re = partial_dft[0] * twist_cos + partial_dft[1] * twist_sin
    turned_im = partial_dft[1] * twist_cos - partial_dft[0] * twist_sin
    keep = partial_dft.shape[1]
    spec = dot_high(turned_re.reshape(-1, cols), fwd_real) + dot_high(
        turned_im.reshape(-1, cols), fwd_imag
    )
    spec = spec.reshape(keep, width_c, 2, cols)
    return (spec[:, :, 0], spec[:, :, 1])


def inverse_half(spec_re, spec_im, tables):
    twist_cos, twist_sin = (tables[1], tables[2])
    inv_real, inv_imag, last_cos, last_sin = tables[5:]
    keep, width_c, cols = spec_re.shape
    wide = dot_high(spec_re.reshape(-1, cols), inv_real) + dot_high(
        spec_im.reshape(-1, cols), inv_imag
    )
    wide = wide.reshape(keep, width_c, 2, cols)
    wide_re = wide[:, :, 0]
    wide_im = wide[:, :, 1]
    turned_re = wide_re * twist_cos - wide_im * twist_sin
    turned_im = wide_im * twist_cos + wide_re * twist_sin
    grid = matmul_high("nk,kca->nca", last_cos, turned_re) - matmul_high(
        "nk,kca->nca", last_sin, turned_im
    )
    return jnp.transpose(grid, (1, 0, 2)).reshape(width_c, -1)


def convolve_cols(gated_spec, filt_spec, tables):
    gated_re, gated_im = gated_spec
    filt_re, filt_im = filt_spec
    return inverse_half(
        gated_re * filt_re - gated_im * filt_im, gated_re * filt_im + gated_im * filt_re, tables
    )


def correlate_cols(gated_spec, filt_spec, dmix_cols, tables):
    gated_re, gated_im = gated_spec
    filt_re, filt_im = filt_spec
    grad_re, grad_im = forward_half(dmix_cols, tables)
    back = inverse_half(
        filt_re * grad_re + filt_im * grad_im, filt_re * grad_im - filt_im * grad_re, tables
    )
    filt_part = inverse_half(
        grad_re * gated_re + grad_im * gated_im, grad_im * gated_re - grad_re * gated_im, tables
    )
    return (back, filt_part)


def phase_tables(n):
    index = 4 * np.arange(n, dtype=np.int64) + 1
    unit = 2.0 * np.pi / (16 * n)
    fine = (index[:, None] * index[None, :LANES] % (16 * n)) * unit
    coarse = (index[:, None] * (4 * LANES * np.arange(n // LANES))[None, :] % (16 * n)) * unit
    turn = index[:, None] * unit
    pack = lambda x: np.stack((np.cos(x), np.sin(x))).astype(np.float32)
    return pack(fine), pack(np.concatenate((coarse, turn), axis=1))


def split_to(ref, lead, rows, value, cols=slice(None)):
    high = value.astype(jnp.bfloat16)
    ref[(*lead, 0, rows, cols)] = high
    ref[(*lead, 1, rows, cols)] = (value - high.astype(jnp.float32)).astype(jnp.bfloat16)


def dot(left, right):
    return jnp.dot(left, right, preferred_element_type=jnp.float32)


def dot3(high, low, ref, lead, cols=slice(None)):
    top = ref[(*lead, 0, slice(None), cols)]
    return dot(high, top) + (dot(high, ref[(*lead, 1, slice(None), cols)]) + dot(low, top))


def coded(value, top):
    return jnp.round(value * (CODES / jnp.maximum(top, 1e-30))).astype(jnp.int32).astype(jnp.int16)


def decoded(code, step):
    return code.astype(jnp.int32).astype(jnp.float32) * step


def operator_kernel(
    parts, scale, bound, q_in, k_in, v_in, c_in, h_in, taps_in, skip_in, fine, coarse,
    gq_out, gk_out, gv_out, f_out, taps_out, skip_out,
    loc, tails, heads, tails_in, heads_in, short_out, dout, codes, tops, codes_in, tops_in,
    hb, cosines, sines, gd, raw, spec, hspec, kspec, back, edges, back_in, edges_in, cross_in,
    filt, fsend, fother, ftotal, fown, fcode, fcode_in, ftop, ftop_in, stage, sums, sums_in, total, other,
    send_sem, recv_sem, local_sem, dp_send, dp_recv, halo_send, halo_recv,
):
    tok, channels = loc.shape[1:]
    team = parts // 2
    n = tok * team
    width = channels // team
    half = width // 2
    share = channels // parts
    rows = 32
    block = min(256, n)
    span = block // tok
    me = lax.axis_index("seq")
    core = lax.axis_index("dp")
    group = lax.axis_index("groups")
    side = me // team
    rank = lax.rem(me, team)
    low = side == 0
    high = side == 1
    sign = jnp.where(low, 1.0, -1.0).astype(jnp.float32)
    last = me == parts - 1
    seam = me == team - 1
    partner = {"dp": 1 - core}
    twin = {"groups": 1 - group}
    group_rows = pl.ds(pl.multiple_of(group * (tok // 2), tok // 2), tok // 2)
    f32, bf16 = jnp.float32, jnp.bfloat16
    my_half = pl.ds(pl.multiple_of(core * half, half), half)
    other_half = pl.ds(pl.multiple_of((1 - core) * half, half), half)
    teams, peers = range(1, team), range(1, parts)

    def cols_of(owner):
        return pl.ds(pl.multiple_of(owner * width, width), width)

    def half_cols_of(owner):
        return pl.ds(pl.multiple_of(owner * width + core * half, half), half)

    def share_of(owner):
        return pl.ds(pl.multiple_of(owner * share, share), share)

    def rows_of(owner):
        return pl.ds(pl.multiple_of(owner * tok, tok), tok)

    mine, own_cols = rows_of(rank), cols_of(rank)

    def mate(s):
        return lax.rem(rank + s, team)

    loads = [
        pltpu.make_async_copy(x.at[0], loc.at[i], local_sem.at[i])
        for i, x in enumerate((q_in, k_in, v_in, c_in))
    ]
    for load in loads:
        load.start()

    barrier = pltpu.get_barrier_semaphore()
    for s in peers:
        device = {"seq": lax.rem(me + s, parts)}
        pl.semaphore_signal(barrier, inc=1, device_id=device, device_id_type=MESH)
    for device in (partner, twin):
        pl.semaphore_signal(barrier, inc=1, device_id=device, device_id_type=MESH)

    for load in loads:
        load.wait()
    for i in range(4):
        tails[2 * i : 2 * i + 2, :] = loc[i, tok - 16 :, :].astype(f32)[14:]
        heads[2 * i : 2 * i + 2, :] = loc[i, :16, :].astype(f32)[:2]

    pl.semaphore_wait(barrier, parts + 1)

    def remote(source, target, sems, device):
        return pltpu.make_async_remote_copy(
            src_ref=source,
            dst_ref=target,
            send_sem=sems[0],
            recv_sem=sems[1],
            device_id=device,
            device_id_type=MESH,
        )

    def to_seq(a, slot, device, source, target):
        return remote(source, target, (send_sem.at[a, slot], recv_sem.at[a, slot]), {"seq": device})

    def to_mate(a, s, source, target):
        return to_seq(a, s, side * team + mate(s), source, target)

    def across(a, s, source, target):
        return to_seq(a, team + s, (1 - side) * team + mate(s), source, target)

    def to_partner(i, source, target, device=partner):
        return remote(source, target, (dp_send.at[i], dp_recv.at[i]), device)

    def local(a, source, target):
        return pltpu.make_async_copy(source, target, local_sem.at[a])

    @pl.when(me == 0)
    def _():
        back_in[0, :, :] = jnp.zeros((tok, channels), jnp.int16)

    halos = [
        remote(x, y, (halo_send.at[i], halo_recv.at[i]), {"seq": lax.rem(me + by, parts)})
        for i, (x, y, by) in enumerate(((tails, tails_in, 1), (heads, heads_in, parts - 1)))
    ]
    for halo in halos:
        halo.start()

    h_target = hb.at[side, rank, group, :, my_half]
    h_own = local(4, h_in.at[group_rows, half_cols_of(rank)], h_target)
    h_moved = [
        to_mate(0, s, h_in.at[group_rows, half_cols_of(mate(s))], h_target) for s in teams
    ] + [
        across(0, s, h_in.at[group_rows, half_cols_of(mate(s))], h_target) for s in range(team)
    ]
    h_own.start()
    for copy in h_moved:
        copy.start()

    chunk = 128

    def at_cols(i):
        return pl.ds(pl.multiple_of(i * chunk, chunk), chunk)

    def extended(b, cols):
        before = jnp.where(me == 0, 0.0, pltpu.roll(tails_in[:, cols], 6 - 2 * b, 0))
        after = heads_in[:, cols]
        if b:
            after = pltpu.roll(after, 8 - 2 * b, 0)
        return before, loc[b, :, cols].astype(f32), after

    def lagged(b, cols, ahead):
        before, here, after = extended(b, cols)
        ext = jnp.concatenate((before, here, after) if ahead else (before, here), axis=0)
        return ext[8:], pltpu.roll(ext, 1, 0)[8:], pltpu.roll(ext, 2, 0)[8:]

    def short(b, lags, cols):
        tap = [taps_in[b, j : j + 1, cols] for j in range(3)]
        return tap[0] * lags[0] + tap[1] * lags[1] + tap[2] * lags[2]

    def encode(i, value, cols):
        top = jnp.max(jnp.abs(value), axis=0, keepdims=True)
        codes[i, :, cols] = coded(value, top)
        tops[i, 0:1, cols] = top * (1.0 / CODES)

    def make_gated(slot):
        @pl.loop(0, channels // chunk)
        def _(i):
            cols = at_cols(i)
            s1 = short(1, lagged(1, cols, True), cols)
            s2 = short(2, lagged(2, cols, True), cols)
            short_out[1, :, cols] = s1
            short_out[2, :, cols] = s2
            encode(slot, s1[:tok] * s2[:tok], cols)

    def make_dmix(slot):
        @pl.loop(0, channels // chunk)
        def _(i):
            cols = at_cols(i)
            _, here, after = extended(3, cols)
            ext = jnp.concatenate((here, after), axis=0)
            pos = me * tok + lax.broadcasted_iota(jnp.int32, (tok + 8, chunk), 0)
            masked = jnp.where((pos >= bound[0]) & (pos < parts * tok), ext, 0.0)
            dout[:, cols] = masked
            s0 = short(0, lagged(0, cols, True), cols)
            short_out[0, :, cols] = s0
            encode(slot, masked[:tok] * s0[:tok], cols)

    def tops_of(slot, to):
        def source(o):
            return tops.at[slot, 0:1, cols_of(o)]

        return local(5 + 2 * slot, source(rank), tops_in.at[to, rank, 0:1, :]), [
            to_mate(1 + 2 * slot, s, source(mate(s)), tops_in.at[to, rank, 0:1, :]) for s in teams
        ]

    def codes_of(slot, to):
        def source(o):
            return codes.at[slot, :, cols_of(o)]

        return local(6 + 2 * slot, source(rank), codes_in.at[to, mine, :]), [
            to_mate(2 + 2 * slot, s, source(mate(s)), codes_in.at[to, mine, :]) for s in teams
        ]

    def part_cols(k, owner):
        start = owner * width + (core if k else 1 - core) * half
        return pl.ds(pl.multiple_of(start, half), half)

    cross_tops = [
        across(1, s, tops.at[0, 0:1, cols_of(mate(s))], tops_in.at[2, rank, 0:1, :])
        for s in range(team)
    ]
    cross_codes = [
        [
            across(
                12 if k else 2, s,
                codes.at[0, :, part_cols(k, mate(s))], codes_in.at[2, mine, part_cols(k, 0)],
            )
            for s in range(team)
        ]
        for k in range(2)
    ]

    for halo in halos:
        halo.wait_recv()
    pl.when(low)(lambda: make_gated(0))
    pl.when(high)(lambda: make_dmix(0))
    first_tops, first_codes = tops_of(0, 0), codes_of(0, 0)
    for copy in (*first_tops[1], *cross_tops):
        copy.start()
    for copy in (*first_codes[1], *cross_codes[0]):
        copy.start()
    first_tops[0].start()
    first_codes[0].start()

    h_own.wait()
    for copy in h_moved:
        copy.wait_recv()
    h_quarter = hb.at[:, :, group, :, my_half]
    h_twin = to_partner(1, h_quarter, h_quarter, twin)
    h_twin.start()

    pl.when(low)(lambda: make_dmix(1))
    pl.when(high)(lambda: make_gated(1))
    second_tops, second_codes = tops_of(1, 1), codes_of(1, 1)
    second = (*second_tops[1], *second_codes[1])

    @pl.when(me > 0)
    def _():
        for copy in (*second, second_tops[0], second_codes[0]):
            copy.start()

    h_twin.wait_recv()
    h_relay = to_partner(0, hb.at[:, :, :, :, my_half], hb.at[:, :, :, :, my_half])
    h_relay.start()

    @pl.loop(0, n // rows)
    def _(i):
        at = pl.ds(pl.multiple_of(i * rows, rows), rows)
        fr, fi = fine[0, at, :], fine[1, at, :]
        cr, ci = coarse[0, at, :], coarse[1, at, :]
        for a in range(n // LANES):
            ar, ai = cr[:, a : a + 1], ci[:, a : a + 1]
            cols = slice(a * LANES, (a + 1) * LANES)
            split_to(cosines, (), at, fr * ar - fi * ai, cols)
            split_to(sines, (), at, fr * ai + fi * ar, cols)

    def at_rows(i):
        return pl.ds(pl.multiple_of(i * rows, rows), rows)

    def at_block(j):
        return pl.ds(pl.multiple_of(j * block, block), block)

    def blocks(table, at):
        return table[0, at, :], table[1, at, :]

    every = pl.ds(0, width)

    def inverse(b, at, cols=every):
        ch, cl = blocks(cosines, at)
        sh, sl = blocks(sines, at)
        return dot3(ch, cl, spec, (b, 0), cols) - dot3(sh, sl, spec, (b, 1), cols)

    def turned(at, re, im):
        end = coarse.shape[2] - 1
        tr, ti = coarse[0, at, end:], coarse[1, at, end:]
        return re * tr - im * ti, re * ti + im * tr

    def forward(i, at, cols=every):
        ch, cl = blocks(cosines, at)
        sh, sl = blocks(sines, at)
        return dot3(ch, cl, gd, (i,), cols), -dot3(sh, sl, gd, (i,), cols)

    def decode(i, cols=every):
        @pl.loop(0, n // rows)
        def _(r):
            at = at_rows(r)
            step = tops_in[i, r // (tok // rows), 0:1, cols]
            split_to(gd, (i,), at, decoded(codes_in[i, at, cols], step), cols)

    def product_to(i, at, re, im, cols=every):
        split_to(spec, (i, 0), at, re, cols)
        split_to(spec, (i, 1), at, im, cols)

    h_relay.wait_recv()

    @pl.loop(0, n // block)
    def _(j):
        at = at_block(j)
        ch, cl = blocks(cosines, at)
        sh, sl = blocks(sines, at)
        near, far = hb[0].reshape(n, width), hb[1].reshape(n, width)
        nr, ni = turned(at, dot(ch, near) + dot(cl, near), -(dot(sh, near) + dot(sl, near)))
        fr, fi = turned(at, dot(ch, far) + dot(cl, far), -(dot(sh, far) + dot(sl, far)))
        hspec[0, at, :], hspec[1, at, :] = nr, ni * sign
        kspec[0, at, :], kspec[1, at, :] = fr - ni, (fi + nr) * sign

    for own, moved in (first_tops, first_codes):
        own.wait()
        for copy in moved:
            copy.wait_recv()
    for copy in cross_codes[1]:
        copy.start()
    decode(0)

    @pl.loop(0, n // block)
    def _(j):
        at = at_block(j)
        hr, hi = hspec[0, at, :], hspec[1, at, :]
        re, im = forward(0, at)
        raw[0, 0, at, :], raw[0, 1, at, :] = re, im
        product_to(0, at, re * hr - im * hi, re * hi + im * hr)

    def src_cols(p):
        return part_cols(p - 1, 0) if p else every

    def dst_cols(p):
        return part_cols(p - 1, rank) if p else own_cols

    data_row, edge_row, own_sem = (5, 7, 13), (6, 8, 14), (9, 11, 19)

    def back_to(p, s, dest):
        i = min(p, 1)
        return to_seq(
            data_row[p], s, side * team + dest,
            back.at[i, rows_of(dest), src_cols(p)], back_in.at[i, :, dst_cols(p)],
        )

    def back_copy(p, s):
        return back_to(p, s, mate(s))

    def edge_copy(p, s):
        i = min(p, 1)
        source = edges.at[i, mate(s), 0:3, src_cols(p)]
        return to_mate(edge_row[p], s, source, edges_in.at[i, 0:3, dst_cols(p)])

    def cross_edge(p, slot, device):
        i = min(p, 1)
        source = edges.at[i, team - 1, 1:3, src_cols(p)]
        return to_seq(edge_row[p], team + slot, device, source, cross_in.at[i, 0:2, dst_cols(p)])

    def cross_copy(p):
        return cross_edge(p, lax.rem(2 * team - 1 - rank, team), team - 1)

    def back_own(p):
        i = min(p, 1)
        return (
            local(own_sem[p], back.at[i, mine, src_cols(p)], back_in.at[i, :, dst_cols(p)]),
            local(
                own_sem[p] + 1,
                edges.at[i, rank, 0:3, src_cols(p)], edges_in.at[i, 0:3, dst_cols(p)],
            ),
        )

    def send_back(p):
        i = min(p, 1)
        cols = src_cols(p)
        steps = n // block

        @pl.loop(0, steps)
        def _(r):
            j = lax.rem(rank // span + 1 + r, steps)
            value = inverse(i, at_block(j), cols) * (1.0 / n)
            for e in range(span):
                dest = j * span + e
                piece = value[e * tok : (e + 1) * tok]
                top = jnp.max(jnp.abs(piece), axis=0, keepdims=True)
                back[i, rows_of(dest), cols] = coded(piece, top)
                edges[i, dest, 0:1, cols] = top * (1.0 / CODES)
                edges[i, lax.rem(dest + team - 1, team), 1:3, cols] = piece[:2]
            @pl.when(r == steps - 1)
            def _():
                for s in teams:
                    edge_copy(p, s).start()

                @pl.when(high)
                def _():
                    cross_copy(p).start()

            for e in range(span):
                dest = j * span + e
                wanted = dest != rank
                if p == 0:
                    wanted = wanted & (side * team + dest != 0)

                @pl.when(wanted)
                def _():
                    back_to(p, lax.rem(dest + team - rank, team), dest).start()

        for copy in back_own(p):
            copy.start()

    def back_arrived(p):
        for copy in back_own(p):
            copy.wait()
        for s in teams:
            edge_copy(p, s).wait_recv()
            if p:
                back_copy(p, s).wait_recv()
            else:
                pl.when(me > 0)(back_copy(p, s).wait_recv)

    def cross_arrived(p):
        @pl.when(seam)
        def _():
            for s in range(team):
                cross_edge(p, s, lax.rem(me + team, parts)).wait_recv()

    def back_sent(p):
        for s in teams:
            edge_copy(p, s).wait_send()
            if p:
                back_copy(p, s).wait_send()
            else:
                pl.when(side * team + mate(s) != 0)(back_copy(p, s).wait_send)

        @pl.when(high)
        def _():
            cross_copy(p).wait_send()

    send_back(0)

    @pl.when(me > 0)
    def _():
        second_tops[0].wait()
        second_codes[0].wait()

    for s in teams:
        source = side * team + lax.rem(rank + team - s, team)

        @pl.when(source != 0)
        def _(s=s):
            second_tops[1][s - 1].wait_recv()
            second_codes[1][s - 1].wait_recv()

    @pl.when(low)
    def _():
        codes_in[1, 0:tok, :] = jnp.zeros((tok, width), jnp.int16)
        tops_in[1, 0, 0:1, :] = jnp.zeros((1, width), f32)

    decode(1)

    @pl.when(low)
    def _():
        @pl.loop(0, n // block)
        def _(j):
            at = at_block(j)
            raw[1, 0, at, :], raw[1, 1, at, :] = forward(1, at)

    f_part = to_partner(2, filt.at[:, :, other_half], fother.at[0])
    f_ends = [
        to_seq(9, team + 1, rank + team * (1 - side), ftop.at[0:1, :], ftop_in.at[0:1, :]),
        to_seq(9, team, rank + team * (1 - side), fcode, fcode_in),
    ]

    @pl.when(high)
    def _():
        @pl.loop(0, n // block)
        def _(j):
            at = at_block(j)
            re, im = forward(1, at)
            raw[1, 0, at, :], raw[1, 1, at, :] = re, im
            gr, gi = turned(at, re, im)
            dr, di = raw[0, 0, at, :], raw[0, 1, at, :]
            filt[0, at, :] = gr * dr + gi * di
            filt[1, at, :] = gr * di - gi * dr

        f_part.start()

    @pl.when(high)
    def _():
        f_part.wait_recv()

        @pl.loop(0, n // block)
        def _(j):
            at = at_block(j)
            re = filt[0, at, my_half] + fother[0, 0, at, :]
            product_to(2, at, re, filt[1, at, my_half] + fother[0, 1, at, :], my_half)

        @pl.loop(0, n // block)
        def _(j):
            at = at_block(j)
            ftotal[at, :] = inverse(2, at, my_half) * (scale / n)

        part = ftotal[...]
        top = jnp.max(jnp.abs(part), axis=0, keepdims=True)
        fcode[...] = coded(part, top)
        ftop[0:1, :] = top * (1.0 / CODES)
        for copy in f_ends:
            copy.start()

    def second_stage(at, cols):
        cr, ci = forward(2, at, cols)
        hr, hi = hspec[0, at, cols], hspec[1, at, cols]
        kr, ki = kspec[0, at, cols], kspec[1, at, cols]
        sr, si = raw[1, 0, at, cols], raw[1, 1, at, cols]
        re = hr * sr + hi * si + (kr * cr + ki * ci)
        im = hr * si - hi * sr + (kr * ci - ki * cr)
        product_to(1, at, re, im, cols)
        return cr, ci, sr, si

    f_add = to_partner(3, fsend, fother.at[1])
    def filter_to(k, at, re, im):
        if k:
            product_to(2, at, re + fother[1, 0, at, :], im + fother[1, 1, at, :], my_half)
        else:
            fsend[0, at, :], fsend[1, at, :] = re, im

    for copy in cross_tops:
        copy.wait_recv()
    for k in range(2):
        cols = part_cols(k, 0)
        for copy in cross_codes[k]:
            copy.wait_recv()
        decode(2, cols)
        if k:
            f_add.wait_recv()

        @pl.when(low)
        def _():
            @pl.loop(0, n // block)
            def _(j):
                at = at_block(j)
                cr, ci, sr, si = second_stage(at, cols)
                gr, gi = turned(at, raw[0, 0, at, cols], raw[0, 1, at, cols])
                dr, di = sr + ci, si - cr
                filter_to(k, at, gr * dr + gi * di, gr * di - gi * dr)

        @pl.when(high)
        def _():
            @pl.loop(0, n // block)
            def _(j):
                at = at_block(j)
                cr, ci, _, _ = second_stage(at, cols)
                gr, gi = turned(at, cr, ci)
                dr, di = raw[0, 0, at, cols], raw[0, 1, at, cols]
                filter_to(k, at, gr * dr + gi * di, gr * di - gi * dr)

        if k == 0:
            f_add.start()
        send_back(1 + k)

    @pl.loop(0, n // block)
    def _(j):
        at = at_block(j)
        ftotal[at, :] = inverse(2, at, my_half) * (scale / n)

    @pl.when(low)
    def _():
        for copy in f_ends:
            copy.wait_recv()
        fown[...] = (ftotal[...] + decoded(fcode_in[...], ftop_in[0:1, :])).astype(bf16)

    @pl.when(high)
    def _():
        fown[...] = ftotal[...].astype(bf16)

    f_target = f_out.at[:, half_cols_of(rank)]
    f_own = local(13, fown.at[mine, :], f_target)
    f_moved = [to_mate(9, s, fown.at[rows_of(mate(s)), :], f_target) for s in teams]
    own_relay = to_partner(4, fown.at[mine, :], f_target)
    for copy in (*f_moved, f_own, own_relay):
        copy.start()

    def finish(b, d, cols, row=0):
        tap = [taps_in[b, j : j + 1, cols] for j in range(3)]
        count = tok - row
        ahead = [pltpu.roll(d, d.shape[0] - by, 0)[:count] for by in (1, 2)]
        grad = tap[0] * d[:count] + tap[1] * ahead[0] + tap[2] * ahead[1]
        stage[b, row:, cols] = grad.astype(bf16)

    def total_of(value):
        return jnp.sum(jnp.sum(value.reshape(tok // 8, 8, chunk), axis=0), axis=0, keepdims=True)

    def add_taps(r, b, d, cols):
        lags = lagged(b, cols, False)
        for j in range(3):
            row = r + j
            sums[row // 8, row % 8 : row % 8 + 1, cols] = total_of(d[:tok] * lags[j])

    def returned(i, cols, row, crossed):
        here = decoded(back_in[i, row:, cols], edges_in[i, 0:1, cols])
        edge = pltpu.roll(edges_in[i, :, cols], 7, 0)
        if crossed:
            edge = jnp.where(seam, cross_in[1 - i, :, cols], edge)
        return jnp.concatenate((here, jnp.where(last, 0.0, edge)), axis=0)

    counts = (4, 6)

    def sum_own(r):
        return local(
            14 + r, sums.at[r, 0 : counts[r], share_of(me)], sums_in.at[me, r, 0 : counts[r], :]
        )

    def sum_copy(r, s):
        peer = lax.rem(me + s, parts)
        source = sums.at[r, 0 : counts[r], share_of(peer)]
        return to_seq(10 + r, s, peer, source, sums_in.at[me, r, 0 : counts[r], :])

    outs = [
        local(16 + b, stage.at[b], out.at[0]) for b, out in enumerate((gq_out, gk_out, gv_out))
    ]

    def over_cols(p, work):
        if p == 0:
            pl.loop(0, channels // chunk)(lambda i: work(at_cols(i)))
        else:
            per = half // chunk

            @pl.loop(0, team * per)
            def _(i):
                owner, c = i // per, lax.rem(i, per)
                start = owner * width + (core if p == 2 else 1 - core) * half + c * chunk
                work(pl.ds(pl.multiple_of(start, chunk), chunk))

    def query_signal(cols, row, crossed):
        gated = short_out[1, row:, cols] * short_out[2, row:, cols]
        dmask = dout[row:, cols]
        return gated, dmask, dmask * (returned(side, cols, row, crossed) + skip_in[:, cols] * gated)

    def finish_query(cols):
        gated, dmask, d = query_signal(cols, 0, False)
        finish(0, d, cols)
        add_taps(0, 0, d, cols)
        dmix = dmask * short_out[0, :, cols]
        sums[0, 3:4, cols] = total_of((dmix * gated)[:tok])

    def finish_rest(cols):
        dmix = dout[:, cols] * short_out[0, :, cols]
        dg = returned(1 - side, cols, 0, True) + skip_in[:, cols] * dmix
        d1 = dg * short_out[2, :, cols]
        finish(1, d1, cols)
        add_taps(8, 1, d1, cols)
        d2 = dg * short_out[1, :, cols]
        finish(2, d2, cols)
        add_taps(11, 2, d2, cols)

    def send_sums(r):
        sum_own(r).start()
        for s in peers:
            sum_copy(r, s).start()

    back_arrived(0)
    cross_arrived(0)

    @pl.when(low)
    def _():
        over_cols(0, finish_query)
        send_sums(0)

    @pl.when(high)
    def _():
        over_cols(0, finish_rest)
        send_sums(1)

    for p in (1, 2):
        back_arrived(p)
        pl.when(low)(lambda: over_cols(p, finish_rest))
        pl.when(high)(lambda: over_cols(p, finish_query))

    pl.when(low)(lambda: send_sums(1))
    pl.when(high)(lambda: send_sums(0))
    cross_arrived(1)
    cross_arrived(2)

    @pl.when(seam)
    def _():
        def mend(cols):
            finish(0, query_signal(cols, tok - 16, True)[2], cols, tok - 16)

        over_cols(0, mend)

    for out in outs:
        out.start()

    relays = [own_relay]
    for s in teams:
        f_moved[s - 1].wait_recv()
        block_cols = half_cols_of(lax.rem(rank + team - s, team))
        relay = to_partner(4 + s, f_out.at[:, block_cols], f_out.at[:, block_cols])
        relay.start()
        relays.append(relay)

    for r in range(2):
        sum_own(r).wait()
        for s in peers:
            sum_copy(r, s).wait_recv()
        value = sums_in[0, r, 0 : counts[r], :]
        for p in range(1, parts):
            value = value + sums_in[p, r, 0 : counts[r], :]
        total[r, 0 : counts[r], :] = value * scale
    s_add = to_partner(4 + team, total, other)
    s_add.start()
    s_add.wait_recv()
    taps_out[0] = total[0, 0:3, :] + other[0, 0:3, :]
    skip_out[...] = total[0, 3:4, :] + other[0, 3:4, :]
    taps_out[1] = total[1, 0:3, :] + other[1, 0:3, :]
    taps_out[2] = total[1, 3:6, :] + other[1, 3:6, :]

    f_own.wait()
    for out in outs:
        out.wait()
    for relay in relays:
        relay.wait_recv()

    for copy in (*halos, *h_moved, *first_tops[1], *first_codes[1], *f_moved):
        copy.wait_send()
    for copy in (*cross_tops, *cross_codes[0], *cross_codes[1]):
        copy.wait_send()

    @pl.when(me > 0)
    def _():
        for copy in second:
            copy.wait_send()

    @pl.when(high)
    def _():
        f_part.wait_send()
        for copy in f_ends:
            copy.wait_send()

    for p in range(3):
        back_sent(p)
    for r in range(2):
        for s in peers:
            sum_copy(r, s).wait_send()
    for copy in (h_twin, h_relay, f_add, s_add, *relays):
        copy.wait_send()


def copy_kernel(*refs):
    held, sems = refs[-2:]
    reads, writes = [], []
    for i in range(4):
        source, target = refs[i], refs[6 + i]
        if i < 3:
            source, target = source.at[0], target.at[0]
        half = source.shape[0] // 2
        for j in range(2):
            rows = pl.ds(j * half, half)
            reads.append(pltpu.make_async_copy(source.at[rows, :], held.at[i, rows, :], sems.at[0, i, j]))
            writes.append(pltpu.make_async_copy(held.at[i, rows, :], target.at[rows, :], sems.at[1, i, j]))
    for read in reads:
        read.start()
    for i in (4, 5):
        refs[6 + i][...] = refs[i][...]
    for read, write in zip(reads, writes):
        read.wait()
        write.start()
    for write in writes:
        write.wait()


def dense_body(query_proj, key_proj, value_proj, cotangent, boundary, short_taps, skip_gain, long_filter):
    tok, width = query_proj.shape[1:]
    parts = lax.axis_size("seq")
    team = parts // 2
    n = tok * team
    own, wide = width // parts, width // team
    scale = 1.0 / math.sqrt(lax.axis_size("dp") * tok * parts)
    fine, coarse = phase_tables(n)
    vmem = pl.BlockSpec(memory_space=pltpu.VMEM)
    anywhere = pl.BlockSpec(memory_space=pl.ANY)
    f32, bf16, i16 = jnp.float32, jnp.bfloat16, jnp.int16
    shape = jax.ShapeDtypeStruct
    dma = pltpu.SemaphoreType.DMA
    results = pl.pallas_call(
        functools.partial(operator_kernel, parts, scale),
        out_shape=[shape((1, tok, width), bf16)] * 3
        + [shape((tok, width), bf16), shape((3, 3, own), f32), shape((1, own), f32)],
        in_specs=[pl.BlockSpec(memory_space=pltpu.SMEM)] + [anywhere] * 5 + [vmem] * 4,
        out_specs=[anywhere] * 4 + [vmem] * 2,
        scratch_shapes=[
            pltpu.VMEM((4, tok, width), bf16),
            pltpu.VMEM((8, width), f32),
            pltpu.VMEM((8, width), f32),
            pltpu.VMEM((8, width), f32),
            pltpu.VMEM((8, width), f32),
            pltpu.VMEM((3, tok + 8, width), f32),
            pltpu.VMEM((tok + 8, width), f32),
            pltpu.VMEM((2, tok, width), i16),
            pltpu.VMEM((2, 8, width), f32),
            pltpu.VMEM((3, n, wide), i16),
            pltpu.VMEM((3, team, 8, wide), f32),
            pltpu.VMEM((2, team, 2, tok // 2, wide), bf16),
            pltpu.VMEM((2, n, n), bf16),
            pltpu.VMEM((2, n, n), bf16),
            pltpu.VMEM((3, 2, n, wide), bf16),
            pltpu.VMEM((2, 2, n, wide), f32),
            pltpu.VMEM((3, 2, 2, n, wide), bf16),
            pltpu.VMEM((2, n, wide), f32),
            pltpu.VMEM((2, n, wide), f32),
            pltpu.VMEM((2, n, wide), i16),
            pltpu.VMEM((2, team, 8, wide), f32),
            pltpu.VMEM((2, tok, width), i16),
            pltpu.VMEM((2, 8, width), f32),
            pltpu.VMEM((2, 8, width), f32),
            pltpu.VMEM((2, n, wide), f32),
            pltpu.VMEM((2, n, wide // 2), f32),
            pltpu.VMEM((2, 2, n, wide // 2), f32),
            pltpu.VMEM((n, wide // 2), f32),
            pltpu.VMEM((n, wide // 2), bf16),
            pltpu.VMEM((n, wide // 2), i16),
            pltpu.VMEM((n, wide // 2), i16),
            pltpu.VMEM((8, wide // 2), f32),
            pltpu.VMEM((8, wide // 2), f32),
            pltpu.VMEM((3, tok, width), bf16),
            pltpu.VMEM((2, 8, width), f32),
            pltpu.VMEM((parts, 2, 8, own), f32),
            pltpu.VMEM((2, 8, own), f32),
            pltpu.VMEM((2, 8, own), f32),
            dma((15, parts)),
            dma((15, parts)),
            dma((21,)),
            dma((5 + team,)),
            dma((5 + team,)),
            dma((2,)),
            dma((2,)),
        ],
        compiler_params=pltpu.CompilerParams(
            collective_id=0, has_side_effects=True, vmem_limit_bytes=56 * 2**20
        ),
    )(
        boundary, query_proj, key_proj, value_proj, cotangent, long_filter,
        short_taps, skip_gain[None], jnp.asarray(fine), jnp.asarray(coarse),
    )
    gq, gk, gv, filter_grad, taps_grad, skip_grad = pl.pallas_call(
        copy_kernel,
        out_shape=[shape(x.shape, x.dtype) for x in results],
        in_specs=[anywhere] * 4 + [vmem] * 2,
        out_specs=[anywhere] * 4 + [vmem] * 2,
        scratch_shapes=[pltpu.VMEM((4, tok, width), bf16), dma((2, 4, 2))],
    )(*results)
    return gq, gk, gv, filter_grad, taps_grad, skip_grad.reshape(own)


def body(query_proj, key_proj, value_proj, cotangent, boundary, short_taps, skip_gain, long_filter):
    pairs, tok, width = query_proj.shape
    parts = lax.axis_size("seq")
    seq_len = tok * parts
    scale = 1.0 / math.sqrt(pairs * lax.axis_size("dp") * seq_len)
    tables = build_tables(seq_len)
    filter_cols = lax.all_to_all(
        jnp.transpose(long_filter), "seq", split_axis=0, concat_axis=1, tiled=True
    ).astype(jnp.float32)
    filt_spec = forward_half(filter_cols, tables)
    taps = short_taps[:, :, None, None, :]
    raw = jnp.stack((query_proj, key_proj, value_proj))
    tails = passed_along(raw[:, :, tok - 2 :], "seq", 1)
    extended = jnp.concatenate((tails, raw), axis=2).astype(jnp.float32)
    conv = (
        taps[:, 0] * extended[:, :, 2:]
        + taps[:, 1] * extended[:, :, 1:-1]
        + taps[:, 2] * extended[:, :, :-2]
    )
    gated = conv[1] * conv[2]
    position = lax.axis_index("seq") * tok + jnp.arange(tok, dtype=jnp.int32)
    mask = (position[None, :] >= boundary[:, None]).astype(jnp.float32)
    dout = cotangent.astype(jnp.float32) * mask[:, :, None]
    dmix = dout * conv[0]
    gated_cols = lax.all_to_all(
        jnp.transpose(gated, (0, 2, 1)), "seq", split_axis=1, concat_axis=2, tiled=True
    )
    spectra = forward_half(gated_cols[0], tables)
    conv_cols = jnp.stack([convolve_cols(spectra, filt_spec, tables)])
    conv_rows = lax.all_to_all(conv_cols, "seq", split_axis=2, concat_axis=1, tiled=True)
    dmix_cols = lax.all_to_all(
        jnp.transpose(dmix, (0, 2, 1)), "seq", split_axis=1, concat_axis=2, tiled=True
    )
    back_cols, filt_part = correlate_cols(spectra, filt_spec, dmix_cols[0], tables)
    back_list = [back_cols]
    filt_list = [filt_part]
    back_rows = lax.all_to_all(jnp.stack(back_list), "seq", split_axis=2, concat_axis=1, tiled=True)
    mixed = jnp.transpose(conv_rows, (0, 2, 1)) + skip_gain * gated
    filter_part = jnp.sum(jnp.stack(filt_list), axis=0) * scale
    filter_total = lax.psum(filter_part, "dp")
    filter_rows = lax.all_to_all(
        filter_total.astype(jnp.bfloat16), "seq", split_axis=1, concat_axis=0, tiled=True
    )
    filter_grad = jnp.transpose(filter_rows)
    dgated = jnp.transpose(back_rows, (0, 2, 1)) + skip_gain * dmix
    upstream = jnp.stack((dout * mixed, dgated * conv[2], dgated * conv[1]))
    heads = passed_along(upstream[:, :, :2], "seq", -1)
    grad_ext = jnp.concatenate((upstream, heads), axis=2)
    grads = (
        taps[:, 0] * grad_ext[:, :, :tok]
        + taps[:, 1] * grad_ext[:, :, 1 : tok + 1]
        + taps[:, 2] * grad_ext[:, :, 2:]
    )
    grads = grads.astype(jnp.bfloat16)
    taps_part = (
        jnp.stack(
            [
                jnp.sum(upstream * extended[:, :, 2 - lag : 2 - lag + tok], axis=(1, 2))
                for lag in range(3)
            ],
            axis=1,
        )
        * scale
    )
    skip_part = jnp.sum(dmix * gated, axis=(0, 1)) * scale
    taps_local, skip_local = (
        lax.psum_scatter(taps_part, "seq", scatter_dimension=2, tiled=True),
        lax.psum_scatter(skip_part, "seq", scatter_dimension=0, tiled=True),
    )
    taps_grad, skip_grad = lax.psum((taps_local, skip_local), "dp")
    return (grads[0], grads[1], grads[2], filter_grad, taps_grad, skip_grad)


def solution(mesh):
    in_specs = (
        P(("groups", "dp"), "seq", None),
        P(("groups", "dp"), "seq", None),
        P(("groups", "dp"), "seq", None),
        P(("groups", "dp"), "seq", None),
        P(("groups", "dp")),
        P(),
        P(),
        P("seq", None),
    )
    out_specs = (
        P(("groups", "dp"), "seq", None),
        P(("groups", "dp"), "seq", None),
        P(("groups", "dp"), "seq", None),
        P(("groups", "seq"), None),
        P("groups", None, "seq"),
        P(("groups", "seq")),
    )
    def chosen(query_proj, *rest):
        pairs, tok, _ = query_proj.shape
        dense = pairs == 1 and mesh.shape["seq"] == 8 and mesh.shape["dp"] == mesh.shape["groups"] == 2 and tok * mesh.shape["seq"] <= DENSE_LIMIT
        return (dense_body if dense else body)(query_proj, *rest)

    return jax.shard_map(chosen, mesh=mesh, in_specs=in_specs, out_specs=out_specs, check_vma=False)
```
